32 devices in a mesh: wt: 8 (over z, x), seq: 4 (over y, core).
Axes of the slice: x: 2, y: 2, z: 4, core: 2. Of those that a mesh axis runs over, the one named last changes fastest.
Arguments:
- tokens: bfloat16 [8192, 1024], P(('wt', 'seq')), may hold values from -6 to 6
- positions: int32 [8192], P(('wt', 'seq')), may hold values from 0 to 8191, as said below
- doc_ids: int32 [8192], P('wt'), may hold values from 0 to 15, as said below
- block_ids: int32 [8192], P('wt'), may hold values from 0 to 31, as said below
- entry_gain: bfloat16 [1024], P('wt'), may hold values from 0.5 to 1.5
- query_weight: bfloat16 [1024, 1024], P('wt'), may hold values from -0.1875 to 0.1875
- key_weight: bfloat16 [1024, 1024], P('wt'), may hold values from -0.1875 to 0.1875
- value_weight: bfloat16 [1024, 1024], P('wt'), may hold values from -0.1875 to 0.1875
- output_weight: bfloat16 [1024, 1024], P('wt'), may hold values from -0.1875 to 0.1875
- attend_gain: bfloat16 [1024], P('wt'), may hold values from 0.5 to 1.5
- middle_gain: bfloat16 [1024], P('wt'), may hold values from 0.5 to 1.5
- gate_weight: bfloat16 [1024, 2816], P('wt'), may hold values from -0.1875 to 0.1875
- up_weight: bfloat16 [1024, 2816], P('wt'), may hold values from -0.1875 to 0.1875
- down_weight: bfloat16 [2816, 1024], P('wt'), may hold values from -0.109375 to 0.109375
- closing_gain: bfloat16 [1024], P('wt'), may hold values from 0.5 to 1.5
- cotangent: bfloat16 [8192, 1024], P(('wt', 'seq')), may hold values from -6 to 6
Outputs:
- layer_output: bfloat16 [8192, 1024], P(('wt', 'seq'))
- input_grad: float32 [8192, 1024], P(('wt', 'seq'))
- grad_entry: float32 [1024], P('wt')
- grad_query: float32 [1024, 1024], P('wt')
- grad_key: float32 [1024, 1024], P('wt')
- grad_value: float32 [1024, 1024], P('wt')
- grad_output: float32 [1024, 1024], P('wt')
- grad_attend: float32 [1024], P('wt')
- grad_middle: float32 [1024], P('wt')
- grad_gate: float32 [1024, 2816], P('wt')
- grad_up: float32 [1024, 2816], P('wt')
- grad_down: float32 [2816, 1024], P('wt')
- grad_closing: float32 [1024], P('wt')
The draws below stay inside these ranges and needn't reach their ends.
Inputs may be any that keep to these rules, and one draw needn't show every extreme that they name: In each window of 1024 tokens the first tokens are the last ones of a document of 8192 tokens, ending at position 8191, and the others begin a new document at position 0; positions rise by one within a document; the boundary lies between a quarter and three quarters of the window. `doc_ids`: each window holds two documents; ids never fall and differ between windows. `block_ids`: A token's block is its position divided by 256, rounded down.
All inputs are finite; a program needn't handle non-finite values.
Results may differ from the reference program's by a relative error of at most 0.02.
Values may be sent and summed in bfloat16 or wider, within the bound.
No kernel may reach another device: no remote copies, remote signals or barrier semaphores. Data moves between devices by JAX's collectives and lax.ppermute only.
A program may use at most 192 MiB of HBM per device.

```python
import jax
import jax.numpy as jnp
from jax import lax

D = 1024
HEADS = 8
FF = 2816
BLOCK = 256
DOC_LEN = 8192
SEQ_LEN = 1024
TOKENS = 8192


def layout_tables(key):
    groups = TOKENS // SEQ_LEN
    boundary = jax.random.randint(jax.random.fold_in(key, 11), (groups, 1), SEQ_LEN // 4, 3 * SEQ_LEN // 4 + 1)
    offsets = jnp.arange(SEQ_LEN, dtype=jnp.int32)[None, :]
    leading = offsets < boundary
    position_table = jnp.where(leading, DOC_LEN - boundary + offsets, offsets - boundary)
    documents = 2 * jnp.arange(groups, dtype=jnp.int32)[:, None] + jnp.where(leading, 0, 1)
    blocks = position_table // BLOCK
    return (position_table.reshape(-1).astype(jnp.int32), documents.reshape(-1).astype(jnp.int32), blocks.reshape(-1).astype(jnp.int32))


def draw_positions(key, part):
    return layout_tables(key)[0]


def draw_doc_ids(key, part):
    return layout_tables(key)[1]


def draw_block_ids(key, part):
    return layout_tables(key)[2]


def strengthened(entries, own_key, source, target, blocks, factor):
    def block_of(axis_at):
        return (jnp.arange(entries.shape[axis_at]) // (entries.shape[axis_at] // blocks)).reshape((-1,) + (1,) * (entries.ndim - 1 - axis_at))

    near = jax.random.permutation(own_key, blocks)[block_of(target)]
    second = (block_of(target) + blocks // 2) % blocks
    return jnp.where((block_of(source) == near) | (block_of(source) == second), factor * entries, entries)


def steps_of(key, extent, shards, least, top_value):
    def one(axis_at, parts):
        steps = jax.random.uniform(jax.random.fold_in(jax.random.fold_in(key, 6), axis_at), (parts,), jnp.float32, least / len(shards), top_value / len(shards))
        return jnp.repeat(jnp.exp(steps), extent[axis_at] // parts).reshape((-1,) + (1,) * (len(extent) - axis_at - 1))

    loudness = one(*shards[0])
    for cut in shards[1:]:
        loudness = loudness * one(*cut)
    return loudness


def scatter_about(key, shape, scale, limit, split=(), kind=jnp.bfloat16):
    gain = steps_of(key, shape, split, -0.22, 0.18) if split else 1.0
    values = jax.random.normal(key, shape, jnp.float32) * scale * gain
    return jnp.minimum(jnp.maximum(values, -limit), limit).astype(kind)


def heavy_noise(key, extent, width, reach, split, heavy, kind=jnp.bfloat16):
    result = width * jax.random.normal(key, extent, jnp.float32)
    if split:
        result = result * steps_of(key, extent, split, -0.22, 0.18)
    return jnp.clip(strengthened(result, jax.random.fold_in(key, 3), *heavy), -reach, reach).astype(kind)


def setup_inputs(seed: int = 0) -> dict:
    key_of = jax.random.split(jax.random.key(seed), 17)
    tokens = heavy_noise(key_of[0], (TOKENS, D), 1.0, 6.0, ((0, 32),), (0, 1, 32, 2.75))
    positions = draw_positions(jax.random.fold_in(key_of[16], 71), 0)
    doc_ids = draw_doc_ids(jax.random.fold_in(key_of[16], 71), 0)
    block_ids = draw_block_ids(jax.random.fold_in(key_of[16], 71), 0)
    entry_gain = jnp.clip(1.0 + 0.1 * jax.random.normal(key_of[4], (D,), jnp.float32), 0.5, 1.5).astype(jnp.bfloat16)
    query_weight = scatter_about(key_of[5], (D, D), D ** -0.5, 0.1875, ((0, 8),))
    key_weight = scatter_about(key_of[6], (D, D), D ** -0.5, 0.1875, ((0, 8),))
    value_weight = scatter_about(key_of[7], (D, D), D ** -0.5, 0.1875, ((0, 8),))
    output_weight = scatter_about(key_of[8], (D, D), D ** -0.5, 0.1875, ((0, 8),))
    attend_gain = jnp.clip(1.0 + 0.1 * jax.random.normal(key_of[9], (D,), jnp.float32), 0.5, 1.5).astype(jnp.bfloat16)
    middle_gain = jnp.clip(1.0 + 0.1 * jax.random.normal(key_of[10], (D,), jnp.float32), 0.5, 1.5).astype(jnp.bfloat16)
    gate_weight = scatter_about(key_of[11], (D, FF), D ** -0.5, 0.1875, ((0, 8),))
    up_weight = scatter_about(key_of[12], (D, FF), D ** -0.5, 0.1875, ((0, 8),))
    down_weight = scatter_about(key_of[13], (FF, D), FF ** -0.5, 0.109375, ((0, 8),))
    closing_gain = jnp.clip(1.0 + 0.1 * jax.random.normal(key_of[14], (D,), jnp.float32), 0.5, 1.5).astype(jnp.bfloat16)
    cotangent = scatter_about(key_of[15], (TOKENS, D), 1.0, 6.0, ((0, 32),))
    return dict(tokens=tokens, positions=positions, doc_ids=doc_ids, block_ids=block_ids, entry_gain=entry_gain, query_weight=query_weight, key_weight=key_weight, value_weight=value_weight, output_weight=output_weight, attend_gain=attend_gain, middle_gain=middle_gain, gate_weight=gate_weight, up_weight=up_weight, down_weight=down_weight, closing_gain=closing_gain, cotangent=cotangent)


EPSILON = 1e-06
ROTARY_BASE = 50000.0

@jax.custom_vjp
def low(v):
    return lax.optimization_barrier(v.astype(jnp.bfloat16)).astype(jnp.float32)

@jax.custom_vjp
def low_back(v):
    return v

def low_keep(v):
    return (low(v), None)

def low_pass(kept, grad):
    return (grad,)

def back_keep(v):
    return (v, None)

def back_low(kept, grad):
    return (low(grad),)
low.defvjp(low_keep, low_pass)
low_back.defvjp(back_keep, back_low)

def norm_rows(values, scales):
    return values * lax.rsqrt(lax.optimization_barrier(jnp.mean(values * values, -1, keepdims=True)) + EPSILON) * scales

def matmul(left, right):
    return jnp.dot(left, right, precision=lax.Precision.HIGHEST, preferred_element_type=jnp.float32)

def rotation(positions, head_width):
    half_width = head_width // 2
    frequency = ROTARY_BASE ** (-2.0 * jnp.arange(half_width, dtype=jnp.float32) / head_width)
    angles = positions.astype(jnp.float32)[:, None] * frequency[None, :]
    return (jnp.cos(angles)[:, None, :], jnp.sin(angles)[:, None, :])

def rotate(tensor, turning, backward):
    cosine, sine_part = turning
    if backward:
        sine_part = -sine_part
    half_width = tensor.shape[-1] // 2
    former = tensor[..., :half_width]
    latter = tensor[..., half_width:]
    return jnp.concatenate([former * cosine - latter * sine_part, latter * cosine + former * sine_part], -1)

def attention(query_rows, key_rows, value_rows, doc_row, block_row):
    window = query_rows.shape[0]
    head_width = query_rows.shape[2]
    row_block = min(512, window)
    block_count = window // row_block
    factor = head_width ** (-0.5)

    def one_block(pieces):
        query_part, query_docs, query_blocks = pieces
        logits = low_back(jnp.einsum('qhd,khd->hqk', query_part, key_rows, precision=lax.Precision.HIGHEST) * factor)
        visible = (query_docs[:, None] == doc_row[None, :]) & (block_row[None, :] <= query_blocks[:, None])
        logits = jnp.where(visible[None], logits, -1e+30)
        row_max = lax.optimization_barrier(jnp.max(logits, -1, keepdims=True))
        weights = jnp.exp(logits - row_max)
        attention_probs = weights / lax.optimization_barrier(jnp.sum(weights, -1, keepdims=True))
        return jnp.einsum('hqk,khd->qhd', low(attention_probs), value_rows, precision=lax.Precision.HIGHEST)
    results = lax.map(jax.checkpoint(one_block), (query_rows.reshape(block_count, row_block, HEADS, head_width), doc_row.reshape(block_count, row_block), block_row.reshape(block_count, row_block)))
    return results.reshape(window, HEADS, head_width)

def layer(inputs, entry_gain, query_weight, key_weight, value_weight, output_weight, attend_gain, middle_gain, gate_weight, up_weight, down_weight, closing_gain, turning, doc_row, block_row):
    token_rows = inputs.shape[0]
    model_width = inputs.shape[1]
    head_width = model_width // HEADS
    head_shape = (token_rows, HEADS, head_width)
    entry_low = low(norm_rows(inputs, entry_gain))
    query_raw = low_back(matmul(entry_low, query_weight)).reshape(head_shape)
    key_raw = low_back(matmul(entry_low, key_weight)).reshape(head_shape)
    value_raw = matmul(entry_low, value_weight).reshape(head_shape)
    query_rows = low_back(low(rotate(query_raw, turning, False)))
    key_rows = low_back(low(rotate(key_raw, turning, False)))
    value_rows = low_back(low(value_raw))
    attended = attention(query_rows, key_rows, value_rows, doc_row, block_row).reshape(token_rows, model_width)
    attended = low_back(low(attended))
    mixed = low_back(matmul(attended, output_weight))
    hidden_state = inputs + norm_rows(mixed, attend_gain)
    middle_low = low(norm_rows(hidden_state, middle_gain))
    gate_value = low_back(matmul(middle_low, gate_weight))
    up_value = low_back(matmul(middle_low, up_weight))
    activated = low(jax.nn.silu(gate_value) * up_value)
    channel_out = low_back(matmul(activated, down_weight))
    return hidden_state + norm_rows(channel_out, closing_gain)

def reference(tokens, positions, doc_ids, block_ids, entry_gain, query_weight, key_weight, value_weight, output_weight, attend_gain, middle_gain, gate_weight, up_weight, down_weight, closing_gain, cotangent):
    weights = tuple((item.astype(jnp.float32) for item in (entry_gain, query_weight, key_weight, value_weight, output_weight, attend_gain, middle_gain, gate_weight, up_weight, down_weight, closing_gain)))
    model_width = tokens.shape[1]
    groups = tokens.shape[0] // SEQ_LEN
    inputs_all = tokens.astype(jnp.float32).reshape(groups, SEQ_LEN, model_width)
    incoming_all = cotangent.astype(jnp.float32).reshape(groups, SEQ_LEN, model_width)
    position_rows = positions.reshape(groups, SEQ_LEN)
    doc_rows = doc_ids.reshape(groups, SEQ_LEN)
    block_rows = block_ids.reshape(groups, SEQ_LEN)

    def per_group(totals, pieces):
        inputs, incoming, position_row, doc_row, block_row = pieces
        turning = rotation(position_row, model_width // HEADS)

        def closed(inputs_arg, *parameters):
            return layer(inputs_arg, *parameters, turning, doc_row, block_row)
        output, pullback = jax.vjp(closed, inputs, *weights)
        gradients = pullback(incoming)
        totals = jax.tree.map(jnp.add, totals, tuple(gradients[1:]))
        return (totals, (output, gradients[0]))
    start = tuple((jnp.zeros_like(item) for item in weights))
    totals, (outputs, input_grads) = lax.scan(per_group, start, (inputs_all, incoming_all, position_rows, doc_rows, block_rows))
    return (outputs.reshape(-1, model_width).astype(jnp.bfloat16), input_grads.reshape(-1, model_width), totals[0], totals[1], totals[2], totals[3], totals[4], totals[5], totals[6], totals[7], totals[8], totals[9], totals[10])
```

```python
import functools

import jax
import jax.numpy as jnp
from jax import lax
from jax.experimental import pallas as pl
from jax.experimental.pallas import tpu as pltpu
from jax.sharding import PartitionSpec as P

HEADS = 8
EPSILON = 1e-06
ROTARY_BASE = 50000.0
DOC_LEN = 8192
DOC_STRIDE = 64
HIDDEN_LOW = -1e30
LOG2_E = 1.4426950408889634
SEQ = 4

f32 = jnp.float32
bf16 = jnp.bfloat16


def norm_rows(values, scales):
    inverse = lax.rsqrt(jnp.mean(values * values, -1, keepdims=True) + EPSILON)
    normed = values * inverse
    return (normed * scales, normed, inverse)


def norm_back(incoming, normed, inverse, scales):
    scaled = incoming * scales
    input_side = inverse * (scaled - normed * jnp.mean(scaled * normed, -1, keepdims=True))
    return (input_side, jnp.sum(incoming * normed, 0))


def dot(left, right):
    return jnp.dot(left, right, preferred_element_type=f32)


def dot_nt(left, right):
    return lax.dot_general(left, right, (((1,), (1,)), ((), ())), preferred_element_type=f32)


def dot_tn(left, right):
    return lax.dot_general(left, right, (((0,), (0,)), ((), ())), preferred_element_type=f32)


def swap(value, bit):
    return lax.ppermute(value, "seq", [(i, i ^ bit) for i in range(SEQ)])


def gather_blocks(own):
    far = swap(own, 2)
    near = swap(own, 1)
    return own, near, far, swap(far, 1)


def turn(rows, cosine, sine):
    return rows * cosine + pltpu.roll(rows, rows.shape[-1] // 2, axis=1) * sine


def visible(key_code, query_code, tile):
    key_wide = jnp.concatenate([key_code] * (tile // 128), axis=1)
    return (key_wide <= query_code[0:1, :]) & (key_wide >= query_code[1:2, :])


def attend_forward(
    low_ref, weight_ref, cos_ref, sin_ref, key_code_ref, query_code_ref,
    query_ref, key_ref, value_ref, out_ref, log_ref,
):
    window = low_ref.shape[0]
    tiles, _, tile = query_code_ref.shape
    width = cos_ref.shape[1]
    heads = query_ref.shape[1] // width
    scale = LOG2_E * width ** (-0.5)

    def project(step, carry):
        rows = pl.ds(pl.multiple_of(step * tile, tile), tile)
        raw = dot(low_ref[rows, :], weight_ref[...])
        cosine = cos_ref[rows, :]
        sine = sin_ref[rows, :]
        for head in range(heads):
            at = head * width
            query_ref[rows, at:at + width] = turn(raw[:, at:at + width], cosine, sine).astype(bf16)
            at = (heads + head) * width
            key_ref[rows, head * width:(head + 1) * width] = turn(
                raw[:, at:at + width], cosine, sine
            ).astype(bf16)
        value_ref[rows, :] = raw[:, 2 * heads * width:].astype(bf16)
        return carry

    lax.fori_loop(0, window // tile, project, 0)
    for head in range(heads):
        cols = slice(head * width, (head + 1) * width)
        value_turned = value_ref[:, cols].astype(f32).T.astype(bf16)

        def one_tile(step, carry):
            rows = pl.ds(pl.multiple_of(step * tile, tile), tile)
            scores = dot_nt(key_ref[:, cols], query_ref[rows, cols])
            shown = visible(key_code_ref[...], query_code_ref[step], tile)
            scores = jnp.where(shown, scores * scale, HIDDEN_LOW)
            top = jnp.max(scores, 0, keepdims=True)
            weights = jnp.exp2(scores - top)
            total = jnp.sum(weights, 0, keepdims=True)
            result = dot(value_turned, weights.astype(bf16)) * (1.0 / total)
            out_ref[rows, cols] = result.T.astype(bf16)
            log_ref[head, step] = jnp.broadcast_to(top + jnp.log2(total), (8, tile))
            return carry

        lax.fori_loop(0, tiles, one_tile, 0)


def attend_backward(
    query_ref, key_ref, value_ref, incoming_ref, log_ref, cos_ref, sin_ref,
    key_code_ref, query_code_ref,
    grad_ref, key_sum, value_sum,
):
    tiles, _, tile = query_code_ref.shape
    width = cos_ref.shape[1]
    heads = query_ref.shape[1] // width
    factor = width ** (-0.5)
    scale = LOG2_E * factor
    for head in range(heads):
        cols = slice(head * width, (head + 1) * width)
        key_turned = key_ref[:, cols].astype(f32).T.astype(bf16)
        key_sum[...] = jnp.zeros_like(key_sum)
        value_sum[...] = jnp.zeros_like(value_sum)

        def one_tile(step, carry):
            rows = pl.ds(pl.multiple_of(step * tile, tile), tile)
            queries = query_ref[rows, cols]
            incoming = incoming_ref[rows, cols]
            scores = dot_nt(key_ref[:, cols], queries)
            shown = visible(key_code_ref[...], query_code_ref[step], tile)
            probs = jnp.where(shown, jnp.exp2(scores * scale - log_ref[head, step, 0:1, :]), 0.0)
            value_sum[...] += dot(probs.astype(bf16), incoming)
            prob_grad = dot_nt(value_ref[:, cols], incoming)
            inner = jnp.sum(probs * prob_grad, 0, keepdims=True)
            score_grad = (probs * (prob_grad - inner)).astype(bf16)
            key_sum[...] += dot(score_grad, queries)
            query_grad = (dot(key_turned, score_grad) * factor).T
            grad_ref[rows, cols] = turn(query_grad, cos_ref[rows, :], -sin_ref[rows, :]).astype(bf16)
            return carry

        lax.fori_loop(0, tiles, one_tile, 0)
        at = (heads + head) * width
        grad_ref[:, at:at + width] = turn(
            key_sum[...] * factor, cos_ref[...], -sin_ref[...]
        ).astype(bf16)
        at = (2 * heads + head) * width
        grad_ref[:, at:at + width] = value_sum[...].astype(bf16)


def on_device(
    tokens, positions, doc_ids, block_ids, entry_gain, query_weight, key_weight, value_weight,
    output_weight, attend_gain, middle_gain, gate_weight, up_weight, down_weight, closing_gain,
    cotangent,
):
    place = lax.axis_index("seq")
    order = [place ^ step for step in range(SEQ)]
    rows, model = tokens.shape
    window = rows * SEQ
    wt = model // query_weight.shape[0]
    shard = query_weight.shape[0]
    part = model // SEQ
    width = model // HEADS
    heads = HEADS // SEQ
    hidden = gate_weight.shape[1]
    chunk = hidden // (wt * SEQ)
    padded = (hidden // SEQ + 255) // 256 * 256 // wt
    hidden_part = padded * wt

    def by_order(stacked, axis):
        return [lax.dynamic_index_in_dim(stacked, at, axis, keepdims=False) for at in order]

    def restore(blocks):
        stacked = jnp.stack(blocks)
        return [lax.dynamic_index_in_dim(stacked, place ^ at, 0, keepdims=False) for at in range(SEQ)]

    def quarter(weight):
        return lax.dynamic_slice_in_dim(weight, place * part, part, axis=1)

    attention_part = jnp.concatenate(
        [quarter(query_weight), quarter(key_weight), quarter(value_weight), quarter(output_weight)], 1
    )
    down_own = lax.dynamic_slice_in_dim(down_weight, place * chunk, chunk, axis=0)
    down_own = jnp.pad(down_own, ((0, padded - chunk), (0, 0)))
    first = lax.all_gather(jnp.concatenate([attention_part, down_own], 0), "wt", axis=0, tiled=False)

    def hidden_columns(weight):
        split = lax.dynamic_index_in_dim(
            weight.reshape(shard, wt, SEQ, chunk), place, 2, keepdims=False
        )
        return jnp.pad(split, ((0, 0), (0, 0), (0, padded - chunk))).reshape(shard, hidden_part)

    gate_up = lax.all_gather(
        jnp.concatenate([hidden_columns(gate_weight), hidden_columns(up_weight)], 1),
        "wt", axis=0, tiled=True,
    )
    gains = lax.all_gather(
        jnp.stack([entry_gain, attend_gain, middle_gain, closing_gain]), "wt", axis=1, tiled=True
    ).astype(f32)
    entry_full, attend_full, middle_full, closing_full = [gains[at:at + 1] for at in range(4)]

    token_blocks = jnp.concatenate(gather_blocks(tokens), 0)

    offsets = jnp.arange(window, dtype=jnp.int32)
    leading = doc_ids == doc_ids[0]
    boundary = jnp.sum(leading.astype(jnp.int32))
    places = jnp.where(leading, DOC_LEN - boundary + offsets, offsets - boundary)
    codes = doc_ids * DOC_STRIDE + block_ids
    lows = doc_ids * DOC_STRIDE
    packed = jnp.stack([places, codes, lows]).reshape(3, SEQ, rows)
    packed = jnp.concatenate(by_order(packed, 1), 1)
    half = width // 2
    frequency = ROTARY_BASE ** (-2.0 * jnp.arange(half, dtype=f32) / width)
    angles = packed[0].astype(f32)[:, None] * frequency[None, :]
    cosine = jnp.cos(angles)
    sine = jnp.sin(angles)
    cosine = jnp.concatenate([cosine, cosine], 1)
    sine = jnp.concatenate([-sine, sine], 1)
    key_code = jnp.broadcast_to(packed[1][:, None], (window, 128))
    query_code = jnp.broadcast_to(
        packed[1:3].reshape(2, SEQ, rows).transpose(1, 0, 2)[:, :, None, :], (SEQ, 2, 4, rows)
    ).transpose(0, 2, 1, 3).reshape(SEQ, 8, rows)

    all_inputs = token_blocks.astype(f32)
    entry_out, _, _ = norm_rows(all_inputs, entry_full)
    entry_low = entry_out.astype(bf16)
    qkv_weight = first[:, :shard, :3 * part].reshape(model, 3 * part)
    output_own = first[:, :shard, 3 * part:].reshape(model, part)
    down_part = first[:, shard:, :].reshape(hidden_part, model)
    output_full = jnp.concatenate(restore(gather_blocks(output_own)), 1)

    any_vmem = pl.BlockSpec(memory_space=pltpu.VMEM)
    params = pltpu.CompilerParams(vmem_limit_bytes=50 * 1024 * 1024)
    low_shape = jax.ShapeDtypeStruct((window, heads * width), bf16)
    query_low, key_low, value_low, attended, log_totals = pl.pallas_call(
        attend_forward,
        out_shape=(
            low_shape, low_shape, low_shape, low_shape,
            jax.ShapeDtypeStruct((heads, SEQ, 8, rows), f32),
        ),
        in_specs=[any_vmem] * 6,
        out_specs=(any_vmem,) * 5,
        compiler_params=params,
        name="attend_forward",
    )(entry_low, qkv_weight, cosine, sine, key_code, query_code)

    def exchange(blocks):
        return [blocks[0], swap(blocks[1], 1), swap(blocks[2], 2), swap(blocks[3], 3)]

    attended_tokens = jnp.concatenate(
        restore(exchange([attended[at * rows:(at + 1) * rows] for at in range(SEQ)])), 1
    )
    inputs = tokens.astype(f32)
    mixed = dot(attended_tokens, output_full)
    attend_out, attend_normed, attend_inverse = norm_rows(mixed, attend_full)
    hidden_state = inputs + attend_out
    middle_out, middle_normed, middle_inverse = norm_rows(hidden_state, middle_full)
    middle_low = middle_out.astype(bf16)

    def halves(own):
        blocks = gather_blocks(own)
        return jnp.concatenate(blocks[:2], 0), jnp.concatenate(blocks[2:], 0)

    def reduce_blocks(near_pair, far_pair):
        far_sum = far_pair[:rows] + swap(far_pair[rows:].astype(bf16), 1).astype(f32)
        far_got = swap(far_sum.astype(bf16), 2)
        near_sum = near_pair[:rows] + swap(near_pair[rows:].astype(bf16), 1).astype(f32)
        return near_sum + far_got.astype(f32)

    def feed(low_rows):
        both = dot(low_rows, gate_up)
        gate_value = both[:, :hidden_part]
        up_value = both[:, hidden_part:]
        sigmoid_gate = jax.nn.sigmoid(gate_value)
        activated = (gate_value * sigmoid_gate * up_value).astype(bf16)
        return gate_value, up_value, sigmoid_gate, activated, dot(activated, down_part)

    middle_halves = halves(middle_low)
    fed = [feed(low_rows) for low_rows in middle_halves]
    channel_out = reduce_blocks(fed[0][4], fed[1][4])
    closing_out, closing_normed, closing_inverse = norm_rows(channel_out, closing_full)
    layer_output = (hidden_state + closing_out).astype(bf16)
    incoming = cotangent.astype(f32)
    channel_grad, closing_local = norm_back(incoming, closing_normed, closing_inverse, closing_full)
    channel_halves = halves(channel_grad.astype(bf16))

    def feed_back(channel_rows, saved):
        gate_value, up_value, sigmoid_gate, _, _ = saved
        active_grad = dot_nt(channel_rows, down_part)
        gate_grad = (
            active_grad * up_value * sigmoid_gate * (1.0 + gate_value * (1.0 - sigmoid_gate))
        ).astype(bf16)
        up_grad = (active_grad * gate_value * sigmoid_gate).astype(bf16)
        both_grad = jnp.concatenate([gate_grad, up_grad], 1)
        return both_grad, dot_nt(both_grad, gate_up)

    backs = [feed_back(channel_halves[at], fed[at]) for at in range(2)]
    middle_grad = reduce_blocks(backs[0][1], backs[1][1])
    gate_up_local = dot_tn(middle_halves[0], backs[0][0]) + dot_tn(middle_halves[1], backs[1][0])
    gate_up_share = lax.psum_scatter(
        gate_up_local.astype(bf16), "wt", scatter_dimension=0, tiled=True
    )
    down_local = dot_tn(fed[0][3], channel_halves[0]) + dot_tn(fed[1][3], channel_halves[1])

    hidden_back, middle_local = norm_back(middle_grad, middle_normed, middle_inverse, middle_full)
    hidden_grad = incoming + hidden_back
    mixed_grad, attend_local = norm_back(hidden_grad, attend_normed, attend_inverse, attend_full)
    mixed_low = mixed_grad.astype(bf16)
    attended_grad = dot_nt(mixed_low, output_full).astype(bf16)
    attended_back = jnp.concatenate(
        exchange(by_order(attended_grad.reshape(rows, SEQ, part), 1)), 0
    )
    output_local = dot_tn(attended_tokens, mixed_low)
    output_blocks = by_order(output_local.reshape(model, SEQ, part), 1)
    output_share = reduce_output(output_blocks)

    qkv_grad = pl.pallas_call(
        attend_backward,
        out_shape=jax.ShapeDtypeStruct((window, 3 * part), bf16),
        in_specs=[any_vmem] * 9,
        out_specs=any_vmem,
        scratch_shapes=[pltpu.VMEM((window, width), f32), pltpu.VMEM((window, width), f32)],
        compiler_params=params,
        name="attend_backward",
    )(query_low, key_low, value_low, attended_back, log_totals, cosine, sine, key_code, query_code)

    entry_pairs = [
        dot_nt(qkv_grad[:2 * rows], qkv_weight), dot_nt(qkv_grad[2 * rows:], qkv_weight)
    ]
    entry_grad = reduce_blocks(entry_pairs[0], entry_pairs[1])
    qkv_local = dot_tn(entry_low, qkv_grad)
    _, entry_normed, entry_inverse = norm_rows(inputs, entry_full)
    input_back, entry_local = norm_back(entry_grad, entry_normed, entry_inverse, entry_full)
    input_grad = hidden_grad + input_back

    gain_rows = jnp.stack([entry_local, attend_local, middle_local, closing_local])
    gain_rows = gain_rows.reshape(4, wt, shard).transpose(1, 0, 2).reshape(wt, 1, 4 * shard)
    gain_rows = jnp.pad(gain_rows, ((0, 0), (0, 7), (0, model - 4 * shard)))
    last = jnp.concatenate(
        [
            jnp.concatenate([qkv_local.astype(bf16), output_share.astype(bf16)], 1).reshape(
                wt, shard, model
            ),
            down_local.astype(bf16).reshape(wt, padded, model),
            gain_rows.astype(bf16),
        ],
        1,
    )
    last_share = lax.psum_scatter(last, "wt", scatter_dimension=0, tiled=False)

    gate_up_blocks = restore(gather_blocks(gate_up_share))
    last_blocks = restore(gather_blocks(last_share))

    def hidden_restore(at):
        blocks = jnp.stack(
            [
                block[:, at * hidden_part:(at + 1) * hidden_part].reshape(shard, wt, padded)[
                    :, :, :chunk
                ]
                for block in gate_up_blocks
            ],
            2,
        )
        return blocks.reshape(shard, hidden).astype(f32)

    def columns(at):
        return jnp.concatenate(
            [block[:shard, at * part:(at + 1) * part] for block in last_blocks], 1
        ).astype(f32)

    grad_down = jnp.concatenate(
        [block[shard:shard + chunk] for block in last_blocks], 0
    ).astype(f32)
    gain_sums = sum(block[shard + padded].astype(f32) for block in last_blocks)
    grad_entry, grad_attend, grad_middle, grad_closing = [
        gain_sums[at * shard:(at + 1) * shard] for at in range(4)
    ]
    return (
        layer_output, input_grad, grad_entry, columns(0), columns(1), columns(2), columns(3),
        grad_attend, grad_middle, hidden_restore(0), hidden_restore(1), grad_down, grad_closing,
    )


def reduce_output(blocks):
    far_sum = blocks[2] + swap(blocks[3].astype(bf16), 1).astype(f32)
    far_got = swap(far_sum.astype(bf16), 2)
    near_sum = blocks[0] + swap(blocks[1].astype(bf16), 1).astype(f32)
    return near_sum + far_got.astype(f32)


def solution(mesh):
    rows = P(("wt", "seq"), None)
    weight = P("wt", None)
    gain = P("wt")
    return jax.shard_map(
        on_device,
        mesh=mesh,
        in_specs=(
            rows, P(("wt", "seq")), gain, gain, gain, weight, weight, weight, weight, gain, gain,
            weight, weight, weight, gain, rows,
        ),
        out_specs=(
            rows, rows, gain, weight, weight, weight, weight, gain, gain, weight, weight, weight,
            gain,
        ),
        check_vma=False,
    )
```

```python
import functools

import jax
import jax.numpy as jnp
from jax import lax
from jax.experimental import pallas as pl
from jax.experimental.pallas import tpu as pltpu
from jax.sharding import PartitionSpec as P

HEADS = 8
EPSILON = 1e-06
ROTARY_BASE = 50000.0
DOC_LEN = 8192
DOC_STRIDE = 64
HIDDEN_LOW = -1e30
LOG2_E = 1.4426950408889634
SEQ = 4
GAIN_ROWS = 8

f32 = jnp.float32
bf16 = jnp.bfloat16


def dot(left, right):
    return jnp.dot(left, right, preferred_element_type=f32)


def dot_nt(left, right):
    return lax.dot_general(left, right, (((1,), (1,)), ((), ())), preferred_element_type=f32)


def dot_tn(left, right):
    return lax.dot_general(left, right, (((0,), (0,)), ((), ())), preferred_element_type=f32)


def normed_of(values):
    inverse = lax.rsqrt(jnp.mean(values * values, -1, keepdims=True) + EPSILON)
    return values * inverse, inverse


def norm_back(incoming, normed, inverse, scales):
    scaled = incoming * scales
    return inverse * (scaled - normed * jnp.mean(scaled * normed, -1, keepdims=True))


def call(kernel, outs, *args, smem=0, flops=0, exps=0, scratch=(), name=None):
    moved = sum(arg.size * arg.dtype.itemsize for arg in args)
    many = isinstance(outs, (list, tuple))
    whole = pl.BlockSpec(memory_space=pltpu.VMEM)
    return pl.pallas_call(
        kernel,
        out_shape=tuple(outs) if many else outs,
        in_specs=[
            pl.BlockSpec(memory_space=pltpu.SMEM) if at < smem else whole
            for at in range(len(args))
        ],
        out_specs=(whole,) * len(outs) if many else whole,
        scratch_shapes=list(scratch),
        compiler_params=pltpu.CompilerParams(vmem_limit_bytes=56 * 1024 * 1024),
        cost_estimate=pl.CostEstimate(flops=flops, transcendentals=exps, bytes_accessed=moved),
        name=name,
    )(*args)


def shaped(*shape, dtype=bf16):
    return jax.ShapeDtypeStruct(shape, dtype)


def after(value, *others):
    return lax.optimization_barrier((value,) + others)[0]


def swap(value, bit):
    return lax.ppermute(value, "seq", [(i, i ^ bit) for i in range(SEQ)])


def chosen(rows, columns, chunk, padded, place):
    row = lax.broadcasted_iota(jnp.int32, (rows, columns), 0)
    column = lax.broadcasted_iota(jnp.int32, (rows, columns), 1)
    block = column // padded
    inside = column - block * padded
    wanted = block * (SEQ * chunk) + place * chunk + inside
    return jnp.where((row == wanted) & (inside < chunk), 1.0, 0.0).astype(bf16)


def pack_first(place_ref, query_ref, key_ref, value_ref, output_ref, down_ref, *refs, padded):
    gain_refs, out_ref = refs[:4], refs[4]
    place = place_ref[0]
    shard, model = query_ref.shape
    part = model // SEQ
    columns = pl.ds(pl.multiple_of(place * part, part), part)
    for at, ref in enumerate((query_ref, key_ref, value_ref, output_ref)):
        out_ref[:shard, at * part:(at + 1) * part] = ref[:, columns]
    out_ref[shard:shard + GAIN_ROWS, :] = jnp.zeros((GAIN_ROWS, model), bf16)
    for at, ref in enumerate(gain_refs):
        out_ref[shard:shard + 1, at * shard:(at + 1) * shard] = ref[...]
    chunk = down_ref.shape[0] // SEQ
    pick_rows = chosen(SEQ * chunk, padded, chunk, padded, place)
    out_ref[shard + GAIN_ROWS:, :] = dot_tn(pick_rows, down_ref[...]).astype(bf16)


def pack_gate_up(place_ref, gate_ref, up_ref, out_ref, *, chunk, padded):
    wide = gate_ref.shape[1] // 2
    narrow = out_ref.shape[1] // 4
    pick = chosen(wide, narrow, chunk, padded, place_ref[0])
    for number, ref in enumerate((gate_ref, up_ref)):
        for half in range(2):
            at = (2 * number + half) * narrow
            out_ref[:, at:at + narrow] = dot(
                ref[:, half * wide:(half + 1) * wide], pick
            ).astype(bf16)


def unpack_feed(place_ref, *refs, shard, padded):
    blocks, (gate_ref, up_ref, down_ref) = refs[:SEQ], refs[SEQ:]
    place = place_ref[0]
    piece = blocks[0].shape[1]
    chunk = down_ref.shape[0] // SEQ
    pieces = (blocks[0].shape[0] - 2 * padded) // shard
    narrow = pieces * piece // 4
    wide = gate_ref.shape[1] // 2
    picks = [chosen(wide, narrow, chunk, padded, place ^ at) for at in range(SEQ)]
    joined = [
        jnp.concatenate([ref[at * shard:(at + 1) * shard, :] for at in range(pieces)], 1)
        for ref in blocks
    ]
    for number, out_ref in enumerate((gate_ref, up_ref)):
        for half in range(2):
            at = (2 * number + half) * narrow
            out_ref[:, half * wide:(half + 1) * wide] = sum(
                dot_nt(joined[step][:, at:at + narrow], picks[step]) for step in range(SEQ)
            )
    below = pieces * shard
    rows = [chosen(SEQ * chunk, padded, chunk, padded, place ^ at) for at in range(SEQ)]
    for at in range(2):
        down_ref[:, at * piece:(at + 1) * piece] = sum(
            dot(rows[step], blocks[step][below + at * padded:below + (at + 1) * padded, :])
            for step in range(SEQ)
        )


def unpack_last(place_ref, *refs, shard):
    blocks, outs = refs[:SEQ], refs[SEQ:]
    place = place_ref[0]
    part = blocks[0].shape[1] // SEQ
    for step, block in enumerate(blocks):
        columns = pl.ds(pl.multiple_of((place ^ step) * part, part), part)
        for at in range(4):
            outs[at][:, columns] = block[:shard, at * part:(at + 1) * part].astype(f32)
    outs[4][...] = sum(block[shard:, :].astype(f32) for block in blocks)


def prepare(
    first_ref, own_ref, near_ref, far_ref, both_ref,
    weight_ref, output_ref, down_ref, gain_ref, low_ref, *, shard,
):
    wt, total, model = first_ref.shape
    part = model // SEQ
    weight_ref[...] = first_ref[:, :shard, :3 * part].reshape(model, 3 * part)
    output_ref[...] = first_ref[:, :shard, 3 * part:].reshape(model, part)
    down_ref[...] = first_ref[:, shard + GAIN_ROWS:, :].reshape(down_ref.shape)
    for at in range(wt):
        for number in range(4):
            gain_ref[number:number + 1, at * shard:(at + 1) * shard] = first_ref[
                at, shard:shard + 1, number * shard:(number + 1) * shard
            ].astype(f32)
    rows = own_ref.shape[0]
    scales = gain_ref[0:1, :]
    step = 32
    for number, ref in enumerate((own_ref, near_ref, far_ref, both_ref)):

        def some(at, carry):
            normed, _ = normed_of(ref[pl.ds(pl.multiple_of(at * step, step), step), :].astype(f32))
            low_ref[pl.ds(pl.multiple_of(number * rows + at * step, step), step), :] = (
                normed * scales
            ).astype(bf16)
            return carry

        lax.fori_loop(0, rows // step, some, 0, unroll=2)


def arrange(place_ref, *refs):
    blocks, out_ref = refs[:SEQ], refs[SEQ]
    place = place_ref[0]
    part = blocks[0].shape[1]
    for step in range(SEQ):
        rows = pl.ds(pl.multiple_of((place ^ step) * part, part), part)
        for other in range(SEQ):
            columns = pl.ds(pl.multiple_of((place ^ other) * part, part), part)
            out_ref[step * part:(step + 1) * part, columns] = blocks[other][rows, :]


def turn(rows, cosine, sine):
    return rows * cosine + pltpu.roll(rows, rows.shape[-1] // 2, axis=1) * sine


def visible(key_code, query_code, tile):
    key_wide = jnp.concatenate([key_code] * (tile // 128), axis=1)
    return (key_wide <= query_code[0:1, :]) & (key_wide >= query_code[1:2, :])


def attend_forward(
    low_ref, weight_ref, cos_ref, sin_ref, key_code_ref, query_code_ref,
    query_ref, key_ref, value_ref, out_ref, log_ref,
):
    window = low_ref.shape[0]
    tiles, _, tile = query_code_ref.shape
    width = cos_ref.shape[1]
    heads = query_ref.shape[1] // width
    scale = LOG2_E * width ** (-0.5)

    def project(step, carry):
        rows = pl.ds(pl.multiple_of(step * tile, tile), tile)
        raw = dot(low_ref[rows, :], weight_ref[...])
        cosine = cos_ref[rows, :]
        sine = sin_ref[rows, :]
        for head in range(heads):
            at = head * width
            query_ref[rows, at:at + width] = turn(raw[:, at:at + width], cosine, sine).astype(bf16)
            at = (heads + head) * width
            key_ref[rows, head * width:(head + 1) * width] = turn(
                raw[:, at:at + width], cosine, sine
            ).astype(bf16)
        value_ref[rows, :] = raw[:, 2 * heads * width:].astype(bf16)
        return carry

    lax.fori_loop(0, window // tile, project, 0)
    for head in range(heads):
        cols = slice(head * width, (head + 1) * width)
        value_turned = value_ref[:, cols].astype(f32).T.astype(bf16)

        def one_tile(step, carry):
            rows = pl.ds(pl.multiple_of(step * tile, tile), tile)
            scores = dot_nt(key_ref[:, cols], query_ref[rows, cols])
            shown = visible(key_code_ref[...], query_code_ref[step], tile)
            scores = jnp.where(shown, scores * scale, HIDDEN_LOW)
            top = jnp.max(scores, 0, keepdims=True)
            weights = jnp.exp2(scores - top)
            total = jnp.sum(weights, 0, keepdims=True)
            result = dot(value_turned, weights.astype(bf16)) * (1.0 / total)
            out_ref[rows, cols] = result.T.astype(bf16)
            log_ref[head, step] = jnp.broadcast_to(top + jnp.log2(total), (8, tile))
            return carry

        lax.fori_loop(0, tiles, one_tile, 0)


def attend_backward(
    query_ref, key_ref, value_ref, log_ref, cos_ref, sin_ref, key_code_ref, query_code_ref,
    *refs,
):
    incoming_refs, (grad_ref, key_sum, value_sum, incoming_ref) = refs[:SEQ], refs[SEQ:]
    tiles, _, tile = query_code_ref.shape
    width = cos_ref.shape[1]
    heads = query_ref.shape[1] // width
    factor = width ** (-0.5)
    scale = LOG2_E * factor
    for step, ref in enumerate(incoming_refs):
        incoming_ref[step * tile:(step + 1) * tile, :] = ref[...]
    for head in range(heads):
        cols = slice(head * width, (head + 1) * width)
        key_turned = key_ref[:, cols].astype(f32).T.astype(bf16)
        key_sum[...] = jnp.zeros_like(key_sum)
        value_sum[...] = jnp.zeros_like(value_sum)

        def one_tile(step, carry):
            rows = pl.ds(pl.multiple_of(step * tile, tile), tile)
            queries = query_ref[rows, cols]
            incoming = incoming_ref[rows, cols]
            scores = dot_nt(key_ref[:, cols], queries)
            shown = visible(key_code_ref[...], query_code_ref[step], tile)
            probs = jnp.where(shown, jnp.exp2(scores * scale - log_ref[head, step, 0:1, :]), 0.0)
            value_sum[...] += dot(probs.astype(bf16), incoming)
            prob_grad = dot_nt(value_ref[:, cols], incoming)
            inner = jnp.sum(probs * prob_grad, 0, keepdims=True)
            score_grad = (probs * (prob_grad - inner)).astype(bf16)
            key_sum[...] += dot(score_grad, queries)
            query_grad = (dot(key_turned, score_grad) * factor).T
            grad_ref[rows, cols] = turn(query_grad, cos_ref[rows, :], -sin_ref[rows, :]).astype(bf16)
            return carry

        lax.fori_loop(0, tiles, one_tile, 0)
        at = (heads + head) * width
        grad_ref[:, at:at + width] = turn(
            key_sum[...] * factor, cos_ref[...], -sin_ref[...]
        ).astype(bf16)
        at = (2 * heads + head) * width
        grad_ref[:, at:at + width] = value_sum[...].astype(bf16)


def feed_weights(*refs, shard, padded):
    lows, refs = refs[:SEQ], refs[SEQ:]
    channels, refs = refs[:SEQ], refs[SEQ:]
    near_grad, far_grad, near_active, far_active, out_ref = refs
    wt, total, piece = out_ref.shape
    pieces = (total - 2 * padded) // shard
    low = jnp.concatenate([ref[...] for ref in lows], 0)
    for at in range(pieces):
        columns = slice(at * piece, (at + 1) * piece)
        grad = jnp.concatenate([near_grad[:, columns], far_grad[:, columns]], 0)
        out_ref[:, at * shard:(at + 1) * shard, :] = (
            dot_tn(low, grad).astype(bf16).reshape(wt, shard, piece)
        )
    active = jnp.concatenate([near_active[...], far_active[...]], 0)
    below = pieces * shard
    for at in range(2):
        columns = slice(at * piece, (at + 1) * piece)
        grad = jnp.concatenate([ref[:, columns] for ref in channels], 0)
        out_ref[:, below + at * padded:below + (at + 1) * padded, :] = (
            dot_tn(active, grad).astype(bf16).reshape(wt, padded, piece)
        )


def output_weights(place_ref, low_ref, *refs):
    pieces, outs = refs[:SEQ], refs[SEQ:]
    place = place_ref[0]
    part = outs[0].shape[1]
    for step in range(SEQ):
        columns = pl.ds(pl.multiple_of((place ^ step) * part, part), part)
        for other in range(SEQ):
            rows = pl.ds(pl.multiple_of((place ^ other) * part, part), part)
            outs[step][rows, :] = dot_tn(pieces[other][...], low_ref[:, columns]).astype(
                outs[step].dtype
            )


def last_weights(at_ref, low_ref, grad_ref, keep_ref, near_ref, far_ref, sum_ref, *refs):
    out_ref, full = refs
    wt, total, model = out_ref.shape
    shard = total - GAIN_ROWS
    part = keep_ref.shape[1]
    full[:, :3 * part] = dot_tn(low_ref[...], grad_ref[...]).astype(bf16)
    full[:, 3 * part:] = (
        keep_ref[...] + near_ref[...].astype(f32) + far_ref[...].astype(f32)
    ).astype(bf16)
    for step in range(wt):
        at = at_ref[step]
        out_ref[step, :shard, :] = full[pl.ds(pl.multiple_of(at * shard, shard), shard), :]
        out_ref[step, shard:, :] = sum_ref[at]


def reduce_lines(blocks, wt):
    def send(value, bit):
        return lax.ppermute(value, "wt", [(at, at ^ bit) for at in range(wt)])

    far_x = send(blocks[6:8], 1)
    near_x = send(blocks[4:6], 1)
    far = (blocks[2:4].astype(f32) + far_x.astype(f32)).astype(bf16)
    got = [send(far[1], 6), send(far[0], 4)]
    near = blocks[0:2].astype(f32) + near_x.astype(f32)
    got.append(send(near[1].astype(bf16), 2))
    return (near[0] + sum(value.astype(f32) for value in got)).astype(bf16)


def on_device(
    tokens, positions, doc_ids, block_ids, entry_gain, query_weight, key_weight, value_weight,
    output_weight, attend_gain, middle_gain, gate_weight, up_weight, down_weight, closing_gain,
    cotangent,
):
    place = lax.axis_index("seq")
    order = [place ^ step for step in range(SEQ)]
    here = jnp.reshape(place, (1,)).astype(jnp.int32)
    rows, model = tokens.shape
    window = rows * SEQ
    shard = query_weight.shape[0]
    wt = model // shard
    part = model // SEQ
    width = model // HEADS
    heads = HEADS // SEQ
    hidden = gate_weight.shape[1]
    chunk = hidden // (wt * SEQ)
    padded = (chunk + 15) // 16 * 16
    hidden_part = padded * wt
    piece = model // 2
    feed_rows = 2 * hidden_part // piece * shard + 2 * padded

    def gather_blocks(own):
        far = swap(own, 2)
        near = swap(own, 1)
        return own, near, far, swap(far, 1)

    first_own = call(
        functools.partial(pack_first, padded=padded),
        shaped(shard + GAIN_ROWS + padded, model),
        here, query_weight, key_weight, value_weight, output_weight, down_weight,
        *(gain[None] for gain in (entry_gain, attend_gain, middle_gain, closing_gain)),
        smem=1, name="pack_first",
    )
    first = lax.all_gather(first_own, "wt", axis=0, tiled=False)
    gate_up_own = call(
        functools.partial(pack_gate_up, chunk=chunk, padded=padded),
        shaped(shard, 2 * hidden_part), here, gate_weight, up_weight, smem=1, name="pack_gate_up",
    )
    gate_up = lax.all_gather(gate_up_own, "wt", axis=0, tiled=True)
    token_blocks = gather_blocks(tokens)

    offsets = jnp.arange(window, dtype=jnp.int32)
    leading = doc_ids == doc_ids[0]
    boundary = jnp.sum(leading.astype(jnp.int32))
    places = jnp.where(leading, DOC_LEN - boundary + offsets, offsets - boundary)
    codes = doc_ids * DOC_STRIDE + block_ids
    lows = doc_ids * DOC_STRIDE
    packed = jnp.stack([places, codes, lows]).reshape(3, SEQ, rows)
    packed = jnp.concatenate(
        [lax.dynamic_index_in_dim(packed, at, 1, keepdims=False) for at in order], 1
    )
    half = width // 2
    frequency = ROTARY_BASE ** (-2.0 * jnp.arange(half, dtype=f32) / width)
    angles = packed[0].astype(f32)[:, None] * frequency[None, :]
    cosine = jnp.cos(angles)
    sine = jnp.sin(angles)
    cosine = jnp.concatenate([cosine, cosine], 1)
    sine = jnp.concatenate([-sine, sine], 1)
    key_code = jnp.broadcast_to(packed[1][:, None], (window, 128))
    query_code = jnp.broadcast_to(
        packed[1:3].reshape(2, SEQ, rows).transpose(1, 0, 2)[:, :, None, :], (SEQ, 2, 4, rows)
    ).transpose(0, 2, 1, 3).reshape(SEQ, 8, rows)

    first = after(first, cosine, sine, key_code, query_code, *token_blocks)
    qkv_weight, output_own, down_part, gains, entry_low = call(
        functools.partial(prepare, shard=shard),
        (shaped(model, 3 * part), shaped(model, part), shaped(hidden_part, model),
         shaped(8, model, dtype=f32), shaped(window, model)),
        first, *token_blocks, name="prepare",
    )
    entry_full, attend_full, middle_full, closing_full = [gains[at:at + 1] for at in range(4)]
    low_shape = shaped(window, heads * width)
    pair_cost = 2 * heads * window * window * width
    query_low, key_low, value_low, attended, log_totals = call(
        attend_forward,
        (low_shape, low_shape, low_shape, low_shape,
         shaped(heads, SEQ, 8, rows, dtype=f32)),
        entry_low, qkv_weight, cosine, sine, key_code, query_code,
        flops=2 * pair_cost + 6 * window * model * part, exps=heads * window * window,
        name="attend_forward",
    )
    output_far = after(swap(output_own, 2), attended)
    output_rows = call(
        arrange, shaped(model, model),
        here, output_own, swap(output_own, 1), output_far, swap(output_far, 1), smem=1,
        name="arrange",
    )

    def exchange(blocks):
        return [blocks[0], swap(blocks[1], 1), swap(blocks[2], 2), swap(blocks[3], 3)]

    joined = exchange([attended[at * rows:(at + 1) * rows] for at in range(SEQ)])
    inputs = tokens.astype(f32)
    mixed = dot(jnp.concatenate(joined, 1), output_rows)
    attend_normed, attend_inverse = normed_of(mixed)
    hidden_state = inputs + attend_normed * attend_full
    middle_normed, middle_inverse = normed_of(hidden_state)
    middle_low = (middle_normed * middle_full).astype(bf16)

    def feed(first_rows, second_rows):
        both = dot(jnp.concatenate([first_rows, second_rows], 0), gate_up)
        gate_value = both[:, :hidden_part]
        up_value = both[:, hidden_part:]
        share = jax.nn.sigmoid(gate_value)
        active = (gate_value * share * up_value).astype(bf16)
        return gate_value, up_value, share, active

    def two_halves(own, work):
        far = swap(own, 2)
        near = swap(own, 1)
        near_done = work(own, near)
        far = after(far, *jax.tree.leaves(near_done))
        return (own, near, far, swap(far, 1)), near_done

    def to_far(values, weights, product):
        second = product(values[rows:], weights).astype(bf16)
        total = product(values[:rows], weights) + swap(second, 1).astype(f32)
        total = total.astype(bf16)
        return swap(total, 2), total

    def add_near(values, weights, product, far_got):
        second = product(values[rows:], weights).astype(bf16)
        return product(values[:rows], weights) + swap(second, 1).astype(f32) + far_got.astype(f32)

    middle_blocks, fed_near = two_halves(middle_low, feed)
    fed_far = feed(middle_blocks[2], middle_blocks[3])
    far_got, far_sum = to_far(fed_far[3], down_part, dot)
    channel_out = add_near(after(fed_near[3], far_sum), down_part, dot, far_got)
    closing_normed, closing_inverse = normed_of(channel_out)
    layer_output = (hidden_state + closing_normed * closing_full).astype(bf16)
    incoming = cotangent.astype(f32)
    channel_low = norm_back(incoming, closing_normed, closing_inverse, closing_full).astype(bf16)
    closing_sum = jnp.sum(incoming * closing_normed, 0)

    def feed_back(first_rows, second_rows, saved):
        gate_value, up_value, share, _ = saved
        active_grad = dot_nt(jnp.concatenate([first_rows, second_rows], 0), down_part)
        gate_grad = active_grad * up_value * share * (1.0 + gate_value * (1.0 - share))
        up_grad = active_grad * gate_value * share
        return jnp.concatenate([gate_grad.astype(bf16), up_grad.astype(bf16)], 1)

    channel_blocks, back_near = two_halves(
        channel_low, lambda first_rows, second_rows: feed_back(first_rows, second_rows, fed_near)
    )
    back_far = feed_back(channel_blocks[2], channel_blocks[3], fed_far)
    far_got, far_sum = to_far(back_far, gate_up, dot_nt)
    feed_local = call(
        functools.partial(feed_weights, shard=shard, padded=padded),
        shaped(wt, feed_rows, piece),
        *middle_blocks, *channel_blocks, back_near, after(back_far, far_sum), fed_near[3],
        fed_far[3], flops=12 * window * model * hidden_part // 2, name="feed_weights",
    )
    feed_share = lax.psum_scatter(feed_local, "wt", scatter_dimension=0, tiled=False)
    middle_grad = add_near(after(back_near, feed_local), gate_up, dot_nt, far_got)

    hidden_grad = incoming + norm_back(middle_grad, middle_normed, middle_inverse, middle_full)
    middle_sum = jnp.sum(middle_grad * middle_normed, 0)
    attend_sum = jnp.sum(hidden_grad * attend_normed, 0)
    mixed_low = norm_back(hidden_grad, attend_normed, attend_inverse, attend_full).astype(bf16)
    attended_grad = dot_nt(mixed_low, output_rows).astype(bf16)
    attended_back = exchange([attended_grad[:, at * part:(at + 1) * part] for at in range(SEQ)])
    output_grads = call(
        output_weights,
        (shaped(model, part, dtype=f32), shaped(model, part), shaped(model, part, dtype=f32),
         shaped(model, part)),
        here, after(mixed_low, attended_grad), *joined, smem=1, flops=2 * rows * model * model,
        name="output_weights",
    )
    output_far = (output_grads[2] + swap(output_grads[3], 1).astype(f32)).astype(bf16)
    output_near = swap(output_grads[1], 1)
    output_got = swap(output_far, 2)
    attended_back[0] = after(attended_back[0], output_far)
    qkv_grad = call(
        attend_backward, shaped(window, 3 * part),
        query_low, key_low, value_low, log_totals, cosine, sine, key_code, query_code,
        *attended_back,
        scratch=(
            pltpu.VMEM((window, width), f32), pltpu.VMEM((window, width), f32),
            pltpu.VMEM((window, heads * width), bf16),
        ),
        flops=5 * pair_cost, exps=heads * window * window, name="attend_backward",
    )
    gain_rows = jnp.stack([attend_sum, middle_sum, closing_sum]).astype(bf16)
    gain_rows = gain_rows.reshape(3, wt, shard).transpose(1, 0, 2).reshape(wt, 1, 3 * shard)
    gain_rows = jnp.pad(gain_rows, ((0, 0), (0, GAIN_ROWS - 1), (0, model - 3 * shard)))
    lines = wt == 8
    mine = lax.axis_index("wt")
    if lines:
        whose = [mine ^ at for at in (0, 2, 4, 6, 1, 3, 5, 7)]
    else:
        whose = list(range(wt))
    last = call(
        last_weights, shaped(wt, shard + GAIN_ROWS, model),
        jnp.stack([jnp.asarray(at, jnp.int32) for at in whose]),
        entry_low, qkv_grad, output_grads[0], output_near, output_got, gain_rows, smem=1,
        scratch=(pltpu.VMEM((model, model), bf16),),
        flops=6 * window * model * part, name="last_weights",
    )
    if lines:
        last_share = reduce_lines(last, wt)
    else:
        last_share = lax.psum_scatter(last, "wt", scatter_dimension=0, tiled=False)

    qkv_grad = after(qkv_grad, last)
    far_got, far_sum = to_far(qkv_grad[2 * rows:], qkv_weight, dot_nt)
    entry_grad = add_near(after(qkv_grad[:2 * rows], far_sum), qkv_weight, dot_nt, far_got)
    entry_normed, entry_inverse = normed_of(inputs)
    input_grad = hidden_grad + norm_back(entry_grad, entry_normed, entry_inverse, entry_full)
    entry_sum = jnp.sum(entry_grad * entry_normed, 0).reshape(8, model // 8)
    for axis, size in (("seq", SEQ), ("wt", wt)):
        bit = 1
        while bit < size:
            entry_sum = entry_sum + lax.ppermute(
                entry_sum, axis, [(at, at ^ bit) for at in range(size)]
            )
            bit *= 2
    grad_entry = lax.dynamic_slice_in_dim(entry_sum.reshape(model), mine * shard, shard)

    feed_blocks = gather_blocks(feed_share)
    grad_gate, grad_up, grad_down = call(
        functools.partial(unpack_feed, shard=shard, padded=padded),
        (shaped(shard, hidden, dtype=f32), shaped(shard, hidden, dtype=f32),
         shaped(SEQ * chunk, model, dtype=f32)),
        here, *feed_blocks, smem=1, name="unpack_feed",
    )
    weight_shape = shaped(shard, model, dtype=f32)
    grad_query, grad_key, grad_value, grad_output, gain_sums = call(
        functools.partial(unpack_last, shard=shard),
        (weight_shape,) * 4 + (shaped(GAIN_ROWS, model, dtype=f32),),
        here, *gather_blocks(last_share), smem=1, name="unpack_last",
    )
    grad_attend, grad_middle, grad_closing = [
        gain_sums[0, at * shard:(at + 1) * shard] for at in range(3)
    ]
    return (
        layer_output, input_grad, grad_entry, grad_query, grad_key, grad_value, grad_output,
        grad_attend, grad_middle, grad_gate, grad_up, grad_down, grad_closing,
    )


def solution(mesh):
    rows = P(("wt", "seq"), None)
    weight = P("wt", None)
    gain = P("wt")
    return jax.shard_map(
        on_device,
        mesh=mesh,
        in_specs=(
            rows, P(("wt", "seq")), gain, gain, gain, weight, weight, weight, weight, gain, gain,
            weight, weight, weight, gain, rows,
        ),
        out_specs=(
            rows, rows, gain, weight, weight, weight, weight, gain, gain, weight, weight, weight,
            gain,
        ),
        check_vma=False,
    )
```

```python
import functools

import jax
import jax.numpy as jnp
from jax import lax
from jax.experimental import pallas as pl
from jax.experimental.pallas import tpu as pltpu
from jax.sharding import PartitionSpec as P

HEADS = 8
EPSILON = 1e-06
ROTARY_BASE = 50000.0
DOC_LEN = 8192
DOC_STRIDE = 64
HIDDEN_LOW = -1e30
LOG2_E = 1.4426950408889634
SEQ = 4
GAIN_ROWS = 8
COSTS = dict(
    pack_first=0.04,
    pack_feed=0.08,
    assemble=0.08,
    attend_forward=0.3,
    arrange=0.06,
    feed_weights=0.16,
    down_weights=0.08,
    feed_forward=0.12,
    feed_backward=0.14,
    output_weights=0.06,
    attend_backward=0.28,
    last_weights=0.12,
    join_shares=0.04,
    unpack_feed=0.18,
    unpack_last=0.06,
)

f32 = jnp.float32
bf16 = jnp.bfloat16


def dot(left, right):
    return jnp.dot(left, right, preferred_element_type=f32)


def dot_nt(left, right):
    return lax.dot_general(left, right, (((1,), (1,)), ((), ())), preferred_element_type=f32)


def dot_tn(left, right):
    return lax.dot_general(left, right, (((0,), (0,)), ((), ())), preferred_element_type=f32)


def normed_of(values):
    inverse = lax.rsqrt(jnp.mean(values * values, -1, keepdims=True) + EPSILON)
    return values * inverse, inverse


def norm_back(incoming, normed, inverse, scales):
    scaled = incoming * scales
    return inverse * (scaled - normed * jnp.mean(scaled * normed, -1, keepdims=True))


def call(kernel, outs, *args, smem=0, scratch=(), name=None):
    many = isinstance(outs, (list, tuple))
    whole = pl.BlockSpec(memory_space=pltpu.VMEM)
    return pl.pallas_call(
        kernel,
        out_shape=tuple(outs) if many else outs,
        in_specs=[
            pl.BlockSpec(memory_space=pltpu.SMEM) if at < smem else whole
            for at in range(len(args))
        ],
        out_specs=(whole,) * len(outs) if many else whole,
        scratch_shapes=list(scratch),
        compiler_params=pltpu.CompilerParams(vmem_limit_bytes=56 * 1024 * 1024),
        cost_estimate=pl.CostEstimate(flops=int(COSTS[name] * 1.15e9), transcendentals=0, bytes_accessed=0),
        name=name,
    )(*args)


def shaped(*shape, dtype=bf16):
    return jax.ShapeDtypeStruct(shape, dtype)


def after(value, *others):
    return lax.optimization_barrier((value,) + others)[0]


def swap(value, bit):
    return lax.ppermute(value, "seq", [(i, i ^ bit) for i in range(SEQ)])


def chosen(rows, columns, chunk, padded, place):
    row = lax.broadcasted_iota(jnp.int32, (rows, columns), 0)
    column = lax.broadcasted_iota(jnp.int32, (rows, columns), 1)
    block = column // padded
    inside = column - block * padded
    wanted = block * (SEQ * chunk) + place * chunk + inside
    return jnp.where((row == wanted) & (inside < chunk), 1.0, 0.0).astype(bf16)


def pack_first(place_ref, query_ref, key_ref, value_ref, output_ref, *refs):
    gain_refs, out_ref = refs[:4], refs[4]
    shard, model = query_ref.shape
    part = model // SEQ
    columns = pl.ds(pl.multiple_of(place_ref[0] * part, part), part)
    for at, ref in enumerate((query_ref, key_ref, value_ref, output_ref)):
        out_ref[:shard, at * part:(at + 1) * part] = ref[:, columns]
    out_ref[shard:, :] = jnp.zeros((GAIN_ROWS, model), bf16)
    for at, ref in enumerate(gain_refs):
        out_ref[shard:shard + 1, at * shard:(at + 1) * shard] = ref[...]


def pack_feed(place_ref, gate_ref, up_ref, down_ref, out_ref, down_out_ref):
    place = place_ref[0]
    wide = gate_ref.shape[1] // 2
    narrow = out_ref.shape[1] // 4
    chunk = down_ref.shape[0] // SEQ
    padded = down_out_ref.shape[0]
    pick = chosen(wide, narrow, chunk, padded, place)
    for number, ref in enumerate((gate_ref, up_ref)):
        for half in range(2):
            at = (2 * number + half) * narrow
            out_ref[:, at:at + narrow] = dot(
                ref[:, half * wide:(half + 1) * wide], pick
            ).astype(bf16)
    pick_rows = chosen(SEQ * chunk, padded, chunk, padded, place)
    down_out_ref[...] = dot_tn(pick_rows, down_ref[...]).astype(bf16)


def assemble(at_ref, *refs):
    blocks, out_ref = refs[:-1], refs[-1]
    rows = blocks[0].shape[0]
    for step, block in enumerate(blocks):
        out_ref[pl.ds(pl.multiple_of(at_ref[step] * rows, rows), rows), :] = block[...]


def join_shares(gate_ref, up_ref, down_ref, out_ref):
    piece = out_ref.shape[1]
    row = 0
    for ref in (gate_ref, up_ref, down_ref):
        for at in range(0, ref.shape[1], piece):
            out_ref[row:row + ref.shape[0], :] = ref[:, at:at + piece]
            row += ref.shape[0]


def unpack_feed(place_ref, *refs, shard, padded):
    blocks, (gate_ref, up_ref, down_ref) = refs[:SEQ], refs[SEQ:]
    place = place_ref[0]
    chunk = down_ref.shape[0] // SEQ
    model = down_ref.shape[1]
    piece = blocks[0].shape[1]
    wide = gate_ref.shape[1] // 2
    below = blocks[0].shape[0] - model // piece * padded
    pieces = below // shard // 2
    narrow = pieces * piece // 2
    pick = jnp.concatenate(
        [chosen(wide, narrow, chunk, padded, place ^ at) for at in range(SEQ)], 1
    )
    for number, out_ref in enumerate((gate_ref, up_ref)):
        joined = [
            jnp.concatenate(
                [
                    ref[(number * pieces + at) * shard:(number * pieces + at + 1) * shard, :]
                    for at in range(pieces)
                ], 1,
            )
            for ref in blocks
        ]
        for half in range(2):
            parts = [part[:, half * narrow:(half + 1) * narrow] for part in joined]
            out_ref[:, half * wide:(half + 1) * wide] = dot_nt(jnp.concatenate(parts, 1), pick)
    rows = jnp.concatenate(
        [chosen(SEQ * chunk, padded, chunk, padded, place ^ at) for at in range(SEQ)], 1
    )
    for at in range(model // piece):
        parts = [ref[below + at * padded:below + (at + 1) * padded, :] for ref in blocks]
        down_ref[:, at * piece:(at + 1) * piece] = dot(rows, jnp.concatenate(parts, 0))


def unpack_last(place_ref, *refs, shard):
    blocks, outs = refs[:SEQ], refs[SEQ:]
    place = place_ref[0]
    part = blocks[0].shape[1] // SEQ
    for step, block in enumerate(blocks):
        columns = pl.ds(pl.multiple_of((place ^ step) * part, part), part)
        for at in range(4):
            outs[at][:, columns] = block[:shard, at * part:(at + 1) * part].astype(f32)
    outs[4][...] = sum(block[shard:, :].astype(f32) for block in blocks)


def arrange(place_ref, *refs):
    blocks, out_ref = refs[:SEQ], refs[SEQ]
    place = place_ref[0]
    part = blocks[0].shape[1]
    for step in range(SEQ):
        rows = pl.ds(pl.multiple_of((place ^ step) * part, part), part)
        for other in range(SEQ):
            columns = pl.ds(pl.multiple_of((place ^ other) * part, part), part)
            out_ref[step * part:(step + 1) * part, columns] = blocks[other][rows, :]


def turn(rows, cosine, sine):
    return rows * cosine + pltpu.roll(rows, rows.shape[-1] // 2, axis=1) * sine


def visible(key_code, query_code, tile):
    key_wide = jnp.concatenate([key_code] * (tile // 128), axis=1)
    return (key_wide <= query_code[0:1, :]) & (key_wide >= query_code[1:2, :])


def key_codes(query_code_ref, key_code_ref):
    tiles, _, tile = query_code_ref.shape
    for step in range(tiles):
        wide = jnp.broadcast_to(query_code_ref[step, 0:1, :], (128, tile))
        key_code_ref[step * tile:(step + 1) * tile, :] = wide.T


def attend_forward(
    weight_ref, cos_ref, sin_ref, query_code_ref, own_ref, near_ref, far_ref, both_ref,
    low_ref, query_ref, key_ref, value_ref, out_ref, log_ref, gain_ref, token_ref, key_code_ref,
):
    window, model = low_ref.shape
    wt, shard, _ = weight_ref.shape
    shard = shard - GAIN_ROWS
    tiles, _, tile = query_code_ref.shape
    width = cos_ref.shape[1]
    heads = query_ref.shape[1] // width
    scale = LOG2_E * width ** (-0.5)
    for at in range(wt):
        gain_ref[0:1, at * shard:(at + 1) * shard] = weight_ref[
            at, shard:shard + 1, :shard
        ].astype(f32)

    for step, ref in enumerate((own_ref, near_ref, far_ref, both_ref)):
        token_ref[step * tile:(step + 1) * tile, :] = ref[...]
    key_codes(query_code_ref, key_code_ref)

    def project(step, carry):
        rows = pl.ds(pl.multiple_of(step * tile, tile), tile)
        normed, _ = normed_of(token_ref[rows, :].astype(f32))
        low = (normed * gain_ref[0:1, :]).astype(bf16)
        low_ref[rows, :] = low
        weight = weight_ref[:, :shard, :3 * heads * width].reshape(model, 3 * heads * width)
        raw = dot(low, weight)
        cosine = cos_ref[rows, :]
        sine = sin_ref[rows, :]
        for head in range(heads):
            at = head * width
            query_ref[rows, at:at + width] = turn(raw[:, at:at + width], cosine, sine).astype(bf16)
            at = (heads + head) * width
            key_ref[rows, head * width:(head + 1) * width] = turn(
                raw[:, at:at + width], cosine, sine
            ).astype(bf16)
        value_ref[rows, :] = raw[:, 2 * heads * width:].astype(bf16)
        return carry

    lax.fori_loop(0, window // tile, project, 0)
    for head in range(heads):
        cols = slice(head * width, (head + 1) * width)
        value_turned = value_ref[:, cols].astype(f32).T.astype(bf16)

        def one_tile(step, carry):
            rows = pl.ds(pl.multiple_of(step * tile, tile), tile)
            scores = dot_nt(key_ref[:, cols], query_ref[rows, cols])
            shown = visible(key_code_ref[...], query_code_ref[step], tile)
            scores = jnp.where(shown, scores * scale, HIDDEN_LOW)
            top = jnp.max(scores, 0, keepdims=True)
            weights = jnp.exp2(scores - top)
            total = jnp.sum(weights, 0, keepdims=True)
            result = dot(value_turned, weights.astype(bf16)) * (1.0 / total)
            out_ref[rows, cols] = result.T.astype(bf16)
            log_ref[head, step] = jnp.broadcast_to(top + jnp.log2(total), (8, tile))
            return carry

        lax.fori_loop(0, tiles, one_tile, 0)


def attend_backward(
    query_ref, key_ref, value_ref, log_ref, cos_ref, sin_ref, query_code_ref, *refs,
):
    incoming_refs = refs[:SEQ]
    grad_ref, key_sum, value_sum, incoming_ref, key_code_ref = refs[SEQ:]
    key_codes(query_code_ref, key_code_ref)
    tiles, _, tile = query_code_ref.shape
    width = cos_ref.shape[1]
    heads = query_ref.shape[1] // width
    factor = width ** (-0.5)
    scale = LOG2_E * factor
    for step, ref in enumerate(incoming_refs):
        incoming_ref[step * tile:(step + 1) * tile, :] = ref[...]
    for head in range(heads):
        cols = slice(head * width, (head + 1) * width)
        key_turned = key_ref[:, cols].astype(f32).T.astype(bf16)
        key_sum[...] = jnp.zeros_like(key_sum)
        value_sum[...] = jnp.zeros_like(value_sum)

        def one_tile(step, carry):
            rows = pl.ds(pl.multiple_of(step * tile, tile), tile)
            queries = query_ref[rows, cols]
            incoming = incoming_ref[rows, cols]
            scores = dot_nt(key_ref[:, cols], queries)
            shown = visible(key_code_ref[...], query_code_ref[step], tile)
            probs = jnp.where(shown, jnp.exp2(scores * scale - log_ref[head, step, 0:1, :]), 0.0)
            value_sum[...] += dot(probs.astype(bf16), incoming)
            prob_grad = dot_nt(value_ref[:, cols], incoming)
            inner = jnp.sum(probs * prob_grad, 0, keepdims=True)
            score_grad = (probs * (prob_grad - inner)).astype(bf16)
            key_sum[...] += dot(score_grad, queries)
            query_grad = (dot(key_turned, score_grad) * factor).T
            grad_ref[rows, cols] = turn(query_grad, cos_ref[rows, :], -sin_ref[rows, :]).astype(bf16)
            return carry

        lax.fori_loop(0, tiles, one_tile, 0)
        at = (heads + head) * width
        grad_ref[:, at:at + width] = turn(
            key_sum[...] * factor, cos_ref[...], -sin_ref[...]
        ).astype(bf16)
        at = (2 * heads + head) * width
        grad_ref[:, at:at + width] = value_sum[...].astype(bf16)


def feed_forward(
    first_ref, second_ref, weight_ref, down_ref, both_ref, active_ref, keep_ref, send_ref,
):
    rows, model = first_ref.shape
    half = down_ref.shape[0]
    low = jnp.concatenate([first_ref[...], second_ref[...]], 0)
    step = 256
    for at in range(0, half, step):
        gate_value = dot(low, weight_ref[:, at:at + step])
        up_value = dot(low, weight_ref[:, half + at:half + at + step])
        both_ref[:, at:at + step] = gate_value.astype(bf16)
        both_ref[:, half + at:half + at + step] = up_value.astype(bf16)
        active_ref[:, at:at + step] = (gate_value * jax.nn.sigmoid(gate_value) * up_value).astype(
            bf16
        )
    for at in range(0, model, step):
        total = dot(active_ref[...], down_ref[:, at:at + step])
        keep_ref[:, at:at + step] = total[:rows]
        send_ref[:, at:at + step] = total[rows:].astype(bf16)


def feed_backward(
    first_ref, second_ref, both_ref, weight_ref, down_ref, grad_ref, keep_ref, send_ref,
):
    rows, model = first_ref.shape
    half = down_ref.shape[0]
    low = jnp.concatenate([first_ref[...], second_ref[...]], 0)
    step = 256
    for at in range(0, half, step):
        active_grad = dot_nt(low, down_ref[at:at + step, :])
        gate_value = both_ref[:, at:at + step].astype(f32)
        up_value = both_ref[:, half + at:half + at + step].astype(f32)
        share = jax.nn.sigmoid(gate_value)
        scaled = active_grad * share
        grad_ref[:, at:at + step] = (
            scaled * up_value * (1.0 + gate_value * (1.0 - share))
        ).astype(bf16)
        grad_ref[:, half + at:half + at + step] = (scaled * gate_value).astype(bf16)
    for at in range(0, model, step):
        total = dot_nt(grad_ref[...], weight_ref[at:at + step, :])
        keep_ref[:, at:at + step] = total[:rows]
        send_ref[:, at:at + step] = total[rows:].astype(bf16)


def halves_out(side, full, shard, columns, keep_ref, send_ref):
    for level in range(full.shape[0] // shard // 2):
        to = slice(level * shard, (level + 1) * shard)
        for at, ref in ((2 * level + side, keep_ref), (2 * level + 1 - side, send_ref)):
            rows = pl.ds(pl.multiple_of(at * shard, shard), shard)
            ref[to, :] = full[rows, columns]


def feed_weights(
    side_ref, own_ref, near_ref, far_ref, both_ref, near_grad, far_grad,
    gate_keep, gate_send, up_keep, up_send, full, *, shard,
):
    low = jnp.concatenate([own_ref[...], near_ref[...], far_ref[...], both_ref[...]], 0)
    grad = jnp.concatenate([near_grad[...], far_grad[...]], 0)
    full[...] = dot_tn(low, grad).astype(bf16)
    half = gate_keep.shape[1]
    side = side_ref[0]
    halves_out(side, full, shard, slice(0, half), gate_keep, gate_send)
    halves_out(side, full, shard, slice(half, 2 * half), up_keep, up_send)


def down_weights(
    side_ref, own_ref, near_ref, far_ref, both_ref, near_active, far_active, keep_ref, send_ref,
    full, *, padded,
):
    grad = jnp.concatenate([own_ref[...], near_ref[...], far_ref[...], both_ref[...]], 0)
    active = jnp.concatenate([near_active[...], far_active[...]], 0)
    full[...] = dot_tn(active, grad).astype(bf16)
    halves_out(side_ref[0], full, padded, slice(None), keep_ref, send_ref)


def output_weights(place_ref, low_ref, *refs):
    pieces, outs = refs[:SEQ], refs[SEQ:]
    place = place_ref[0]
    part = outs[0].shape[1]
    for step in range(SEQ):
        columns = pl.ds(pl.multiple_of((place ^ step) * part, part), part)
        for other in range(SEQ):
            rows = pl.ds(pl.multiple_of((place ^ other) * part, part), part)
            outs[step][rows, :] = dot_tn(pieces[other][...], low_ref[:, columns]).astype(
                outs[step].dtype
            )


def last_weights(at_ref, low_ref, grad_ref, keep_ref, near_ref, far_ref, sum_ref, *refs):
    out_ref, full = refs
    wt, total, model = out_ref.shape
    shard = total - GAIN_ROWS
    part = keep_ref.shape[1]
    full[:, :3 * part] = dot_tn(low_ref[...], grad_ref[...]).astype(bf16)
    full[:, 3 * part:] = (
        keep_ref[...] + near_ref[...].astype(f32) + far_ref[...].astype(f32)
    ).astype(bf16)
    for step in range(wt):
        at = at_ref[step]
        out_ref[step, :shard, :] = full[pl.ds(pl.multiple_of(at * shard, shard), shard), :]
        out_ref[step, shard:, :] = sum_ref[at]


def pick_level(level, table):
    return jnp.where(
        level == 0, table[0],
        jnp.where(level == 1, table[1], jnp.where(level == 2, table[2], table[3])),
    )


def gather_start(own):
    level = lax.axis_index("wt") // 2

    def send(value, pairs):
        return lax.ppermute(value, "wt", pairs)

    def across(value):
        return send(value, [(at, at ^ 1) for at in range(8)])

    right = send(own, [(at, at + 2) for at in range(6)])
    left = send(own, [(at, at - 2) for at in range(2, 8)])
    own_x = across(own)
    right2 = send(after(right, own_x), [(at, at + 2) for at in range(2, 6)])
    left2 = send(after(left, own_x), [(at, at - 2) for at in range(2, 6)])
    one = jnp.where(level == 0, left, right)
    one_x = across(one)
    onward = after(jnp.where(level == 2, right2, left2), one_x)
    two = jnp.where(level == 0, left2, jnp.where(level == 3, right2, left))
    two_x = across(two)
    third = send(onward, [(4, 6), (5, 7), (2, 0), (3, 1)])
    return (own, one, two, own_x, one_x, two_x), onward, third


def gather_end(started, onward, third):
    here = lax.axis_index("wt")
    level = here // 2
    side = here % 2
    three = jnp.where((level == 1) | (level == 2), onward, third)
    three_x = lax.ppermute(three, "wt", [(at, at ^ 1) for at in range(8)])
    levels = [level] + [
        pick_level(level, table) for table in ((1, 0, 1, 2), (2, 2, 3, 1), (3, 3, 0, 0))
    ]
    whose = [2 * at + side for at in levels] + [2 * at + 1 - side for at in levels]
    blocks = (*started[:3], three, *started[3:], three_x)
    return blocks, jnp.stack(whose).astype(jnp.int32)


def across(value, wt):
    return lax.ppermute(value, "wt", [(at, at ^ 1) for at in range(wt)])


def scatter_levels(value, wt):
    return lax.psum_scatter(
        value, "wt", scatter_dimension=0, tiled=True,
        axis_index_groups=[list(range(side, wt, 2)) for side in range(2)],
    )


def add_low(left, right):
    return (left.astype(f32) + right.astype(f32)).astype(bf16)


def on_device(
    tokens, positions, doc_ids, block_ids, entry_gain, query_weight, key_weight, value_weight,
    output_weight, attend_gain, middle_gain, gate_weight, up_weight, down_weight, closing_gain,
    cotangent,
):
    place = lax.axis_index("seq")
    order = [place ^ step for step in range(SEQ)]
    here = jnp.reshape(place, (1,)).astype(jnp.int32)
    rows, model = tokens.shape
    window = rows * SEQ
    shard = query_weight.shape[0]
    wt = model // shard
    part = model // SEQ
    width = model // HEADS
    heads = HEADS // SEQ
    hidden = gate_weight.shape[1]
    chunk = hidden // (wt * SEQ)
    padded = (chunk + 15) // 16 * 16
    hidden_part = padded * wt
    piece = 256

    def gather_blocks(own):
        far = swap(own, 2)
        near = swap(own, 1)
        return own, near, far, swap(far, 1)

    lines = wt == 8
    first_own = call(
        pack_first, shaped(shard + GAIN_ROWS, model),
        here, query_weight, key_weight, value_weight, output_weight,
        *(gain[None] for gain in (entry_gain, attend_gain, middle_gain, closing_gain)),
        smem=1, name="pack_first",
    )
    first = lax.all_gather(first_own, "wt", axis=0, tiled=False)
    gate_up_own, down_own = call(
        pack_feed, (shaped(shard, 2 * hidden_part), shaped(padded, model)),
        here, gate_weight, up_weight, after(down_weight, first_own), smem=1, name="pack_feed",
    )
    down_part = lax.all_gather(down_own, "wt", axis=0, tiled=True)
    if lines:
        gate_up_blocks, onward, third = gather_start(gate_up_own)
    token_blocks = gather_blocks(tokens)
    cotangent_far = swap(after(cotangent, token_blocks[2]), 2)

    offsets = jnp.arange(window, dtype=jnp.int32)
    leading = doc_ids == doc_ids[0]
    boundary = jnp.sum(leading.astype(jnp.int32))
    places = jnp.where(leading, DOC_LEN - boundary + offsets, offsets - boundary)
    codes = doc_ids * DOC_STRIDE + block_ids
    lows = doc_ids * DOC_STRIDE
    packed = jnp.stack([places, codes, lows]).reshape(3, SEQ, rows)
    packed = jnp.concatenate(
        [lax.dynamic_index_in_dim(packed, at, 1, keepdims=False) for at in order], 1
    )
    half = width // 2
    frequency = ROTARY_BASE ** (-2.0 * jnp.arange(half, dtype=f32) / width)
    angles = packed[0].astype(f32)[:, None] * frequency[None, :]
    cosine = jnp.cos(angles)
    sine = jnp.sin(angles)
    cosine = jnp.concatenate([cosine, cosine], 1)
    sine = jnp.concatenate([-sine, sine], 1)
    query_code = jnp.broadcast_to(
        packed[1:3].astype(f32).reshape(2, SEQ, rows).transpose(1, 0, 2)[:, :, None, :], (SEQ, 2, 4, rows)
    ).transpose(0, 2, 1, 3).reshape(SEQ, 8, rows)

    waited = (cosine, sine, query_code, *token_blocks, cotangent_far)
    if lines:
        waited += (onward,)
    first = after(first, *waited)
    output_own = first[:, :shard, 3 * part:].reshape(model, part)
    gains = first[:, shard, :4 * shard].reshape(wt, 4, shard).transpose(1, 0, 2).reshape(4, model)
    gains = gains.astype(f32)
    first = after(first, output_own)
    if lines:
        gate_up_blocks, sources = gather_end(gate_up_blocks, onward, third)
        first = after(first, gate_up_blocks[3])
    entry_full, attend_full, middle_full, closing_full = [gains[at:at + 1] for at in range(4)]
    low_shape = shaped(window, heads * width)
    pair_cost = 2 * heads * window * window * width
    entry_low, query_low, key_low, value_low, attended, log_totals = call(
        attend_forward,
        (shaped(window, model), low_shape, low_shape, low_shape, low_shape,
         shaped(heads, SEQ, 8, rows, dtype=f32)),
        first, cosine, sine, query_code, *token_blocks,
        scratch=(
            pltpu.VMEM((8, model), f32), pltpu.VMEM((window, model), bf16),
            pltpu.VMEM((window, 128), f32),
        ),
        name="attend_forward",
    )
    output_far = after(swap(output_own, 2), attended)
    output_rows = call(
        arrange, shaped(model, model),
        here, output_own, swap(output_own, 1), output_far, swap(output_far, 1), smem=1,
        name="arrange",
    )

    if lines:
        gate_up = call(
            assemble, shaped(model, 2 * hidden_part),
            sources, *gate_up_blocks[:-1], after(gate_up_blocks[-1], attended), smem=1,
            name="assemble",
        )
    else:
        gate_up = lax.all_gather(gate_up_own, "wt", axis=0, tiled=True)

    def exchange(blocks):
        return [blocks[0], swap(blocks[1], 1), swap(blocks[2], 2), swap(blocks[3], 3)]

    joined = exchange([attended[at * rows:(at + 1) * rows] for at in range(SEQ)])
    joined = [joined[0], joined[1]] + [after(got, gate_up, output_rows) for got in joined[2:]]
    inputs = tokens.astype(f32)
    mixed = dot(jnp.concatenate(joined, 1), output_rows)
    attend_normed, attend_inverse = normed_of(mixed)
    hidden_state = inputs + attend_normed * attend_full
    middle_normed, middle_inverse = normed_of(hidden_state)
    middle_low = (middle_normed * middle_full).astype(bf16)

    full = shaped(rows, model, dtype=f32)
    both_shape = shaped(2 * rows, 2 * hidden_part)

    def forward(first_rows, second_rows):
        return call(
            feed_forward, (both_shape, shaped(2 * rows, hidden_part), full, shaped(rows, model)),
            first_rows, second_rows, gate_up, down_part, name="feed_forward",
        )

    def backward(first_rows, second_rows, both):
        return call(
            feed_backward, (both_shape, full, shaped(rows, model)),
            first_rows, second_rows, both, gate_up, down_part, name="feed_backward",
        )

    def chip_sum(values, weights, product):
        second = product(values[rows:], weights).astype(bf16)
        return product(values[:rows], weights) + swap(second, 1).astype(f32)

    middle_far = swap(middle_low, 2)
    middle_near = swap(middle_low, 1)
    fed_near = forward(middle_low, middle_near)
    middle_far = after(middle_far, fed_near[0])
    channel_near = fed_near[2] + swap(fed_near[3], 1).astype(f32)
    channel_send = channel_near.astype(bf16)
    far_other = swap(channel_send, 2)
    middle_both = after(swap(middle_far, 1), channel_send)
    fed_far = forward(middle_far, middle_both)
    far_other = after(far_other, fed_far[0])
    channel_far = fed_far[2] + swap(fed_far[3], 1).astype(f32)
    near_other = swap(channel_far.astype(bf16), 2)

    def close(channel_out, cotangents):
        normed, inverse = normed_of(channel_out)
        back = norm_back(cotangents.astype(f32), normed, inverse, closing_full)
        return normed, back.astype(bf16)

    _, low_far = close(channel_far + far_other.astype(f32), cotangent_far)
    low_both = swap(low_far, 1)
    back_far = backward(low_far, low_both, fed_far[0])
    near_other = after(near_other, back_far[0])
    middle_send = (back_far[1] + swap(back_far[2], 1).astype(f32)).astype(bf16)
    far_got = swap(middle_send, 2)
    closing_normed, channel_low = close(
        channel_near + after(near_other, middle_send).astype(f32), cotangent
    )
    layer_output = (hidden_state + closing_normed * closing_full).astype(bf16)
    incoming = cotangent.astype(f32)
    closing_sum = jnp.sum(incoming * closing_normed, 0)
    low_near = swap(channel_low, 1)
    down_shape = shaped(hidden_part // 2, model)
    side = jnp.reshape(lax.axis_index("wt") % 2, (1,)).astype(jnp.int32)
    down_keep, down_send = call(
        functools.partial(down_weights, padded=padded), (down_shape, down_shape),
        side, channel_low, low_near, low_far, low_both, fed_near[1], fed_far[1], smem=1,
        scratch=(pltpu.VMEM((hidden_part, model), bf16),), name="down_weights",
    )
    down_got = across(down_send, wt)
    back_near = backward(channel_low, after(low_near, down_keep), fed_near[0])
    near_got = back_near[1] + swap(back_near[2], 1).astype(f32)
    gate_shape = shaped(model // 2, hidden_part)
    gate_keep, gate_send, up_keep, up_send = call(
        functools.partial(feed_weights, shard=shard),
        (gate_shape,) * 4, side, middle_low, middle_near, middle_far, middle_both,
        after(back_near[0], near_got), back_far[0], smem=1,
        scratch=(pltpu.VMEM((model, 2 * hidden_part), bf16),), name="feed_weights",
    )
    gate_got = across(gate_send, wt)
    up_got = across(up_send, wt)
    down_sum = add_low(down_keep, after(down_got, gate_keep))
    down_share = scatter_levels(down_sum, wt)
    middle_grad = near_got + after(far_got, gate_keep, down_sum).astype(f32)

    hidden_grad = incoming + norm_back(middle_grad, middle_normed, middle_inverse, middle_full)
    middle_sum = jnp.sum(middle_grad * middle_normed, 0)
    attend_sum = jnp.sum(hidden_grad * attend_normed, 0)
    mixed_low = norm_back(hidden_grad, attend_normed, attend_inverse, attend_full).astype(bf16)
    attended_grad = dot_nt(mixed_low, output_rows).astype(bf16)
    attended_back = exchange([attended_grad[:, at * part:(at + 1) * part] for at in range(SEQ)])
    output_grads = call(
        output_weights,
        (shaped(model, part, dtype=f32), shaped(model, part), shaped(model, part, dtype=f32),
         shaped(model, part)),
        here, after(mixed_low, attended_grad), *joined, smem=1,
        name="output_weights",
    )
    attended_back[1:] = [after(got, output_grads[0]) for got in attended_back[1:]]
    output_far = (output_grads[2] + swap(output_grads[3], 1).astype(f32)).astype(bf16)
    output_near = swap(output_grads[1], 1)
    output_far = after(output_far, *attended_back)
    gate_sum = add_low(gate_keep, after(gate_got, down_share, *attended_back[1:]))
    gate_share = scatter_levels(gate_sum, wt)
    attended_back[0] = after(attended_back[0], output_far, gate_sum)
    output_got = swap(output_far, 2)
    qkv_grad = call(
        attend_backward, shaped(window, 3 * part),
        query_low, key_low, value_low, log_totals, cosine, sine, query_code,
        *attended_back,
        scratch=(
            pltpu.VMEM((window, width), f32), pltpu.VMEM((window, width), f32),
            pltpu.VMEM((window, heads * width), bf16), pltpu.VMEM((window, 128), f32),
        ), name="attend_backward",
    )
    gain_rows = jnp.stack([attend_sum, middle_sum, closing_sum]).astype(bf16)
    gain_rows = gain_rows.reshape(3, wt, shard).transpose(1, 0, 2).reshape(wt, 1, 3 * shard)
    gain_rows = jnp.pad(gain_rows, ((0, 0), (0, GAIN_ROWS - 1), (0, model - 3 * shard)))
    mine = lax.axis_index("wt")
    if lines:
        whose = [mine ^ at for at in (0, 2, 4, 6, 1, 3, 5, 7)]
    else:
        levels = range(0, wt, 2)
        whose = [at + mine % 2 for at in levels] + [at + 1 - mine % 2 for at in levels]
    last = call(
        last_weights, shaped(wt, shard + GAIN_ROWS, model),
        jnp.stack([jnp.asarray(at, jnp.int32) for at in whose]),
        entry_low, qkv_grad, output_grads[0], output_near, after(output_got, qkv_grad), gain_rows,
        smem=1, scratch=(pltpu.VMEM((model, model), bf16),), name="last_weights",
    )
    up_sum = add_low(up_keep, after(up_got, last))
    up_share = scatter_levels(up_sum, wt)
    if lines:

        def send(value, bit):
            return lax.ppermute(value, "wt", [(at, at ^ bit) for at in range(wt)])

        far_x = across(last[6:8], wt)
        far = add_low(last[2:4], after(far_x, up_sum))
        near_x = across(after(last[4:6], far), wt)
        last_z = [send(far[1], 6), send(far[0], 4)]
        near = last[0:2].astype(f32) + near_x.astype(f32)
        near_send = near[1].astype(bf16)
        last_z.append(send(near_send, 2))
    else:
        last_rows = wt // 2 * (shard + GAIN_ROWS)
        last_halves = last.reshape(2, last_rows, model)
        last_share = scatter_levels(
            add_low(last_halves[0], across(last_halves[1], wt)), wt
        )
        near_send = last_share

    qkv_weight = first[:, :shard, :3 * part].reshape(model, 3 * part)
    entry_far = chip_sum(qkv_grad[2 * rows:], qkv_weight, dot_nt).astype(bf16)
    entry_grad = chip_sum(after(qkv_grad[:2 * rows], entry_far), qkv_weight, dot_nt)
    entry_grad = entry_grad + swap(entry_far, 2).astype(f32)
    entry_normed, entry_inverse = normed_of(inputs)
    input_grad = hidden_grad + norm_back(entry_grad, entry_normed, entry_inverse, entry_full)
    entry_sum = jnp.sum(entry_grad * entry_normed, 0).reshape(8, model // 8)
    for axis, size in (("seq", SEQ), ("wt", wt)):
        bit = 1
        while bit < size:
            entry_sum = entry_sum + lax.ppermute(
                entry_sum, axis, [(at, at ^ bit) for at in range(size)]
            )
            bit *= 2
    grad_entry = lax.dynamic_slice_in_dim(entry_sum.reshape(model), mine * shard, shard)

    share = call(
        join_shares, shaped((2 * hidden_part * shard + model * padded) // piece, piece),
        after(gate_share, near_send), up_share, down_share, name="join_shares",
    )
    if lines:
        last_z = [after(value, share) for value in last_z]
        last_share = (near[0] + sum(value.astype(f32) for value in last_z)).astype(bf16)
    share_got = gather_blocks(share)
    last_got = gather_blocks(last_share)
    grad_gate, grad_up, grad_down = call(
        functools.partial(unpack_feed, shard=shard, padded=padded),
        (shaped(shard, hidden, dtype=f32), shaped(shard, hidden, dtype=f32),
         shaped(SEQ * chunk, model, dtype=f32)),
        here, *share_got, smem=1, name="unpack_feed",
    )
    weight_shape = shaped(shard, model, dtype=f32)
    grad_query, grad_key, grad_value, grad_output, gain_sums = call(
        functools.partial(unpack_last, shard=shard),
        (weight_shape,) * 4 + (shaped(GAIN_ROWS, model, dtype=f32),),
        here, last_share, last_got[1], after(last_got[2], grad_down),
        last_got[3], smem=1, name="unpack_last",
    )
    grad_attend, grad_middle, grad_closing = [
        gain_sums[0, at * shard:(at + 1) * shard] for at in range(3)
    ]
    return (
        layer_output, input_grad, grad_entry, grad_query, grad_key, grad_value, grad_output,
        grad_attend, grad_middle, grad_gate, grad_up, grad_down, grad_closing,
    )


def solution(mesh):
    rows = P(("wt", "seq"), None)
    weight = P("wt", None)
    gain = P("wt")
    return jax.shard_map(
        on_device,
        mesh=mesh,
        in_specs=(
            rows, P(("wt", "seq")), gain, gain, gain, weight, weight, weight, weight, gain, gain,
            weight, weight, weight, gain, rows,
        ),
        out_specs=(
            rows, rows, gain, weight, weight, weight, weight, gain, gain, weight, weight, weight,
            gain,
        ),
        check_vma=False,
    )
```

```python
import functools

import jax
import jax.numpy as jnp
from jax import lax
from jax.experimental import pallas as pl
from jax.experimental.pallas import tpu as pltpu
from jax.sharding import PartitionSpec as P

HEADS = 8
EPSILON = 1e-06
ROTARY_BASE = 50000.0
DOC_LEN = 8192
DOC_STRIDE = 64
HIDDEN_LOW = -1e30
LOG2_E = 1.4426950408889634
SEQ = 4
GAIN_ROWS = 8
COSTS = dict(
    pack_first=0.004,
    pack_feed=0.008,
    assemble=0.008,
    attend_forward=0.03,
    arrange=0.006,
    feed_weights=0.016,
    down_weights=0.008,
    feed_forward=0.012,
    feed_backward=0.014,
    output_weights=0.006,
    attend_backward=0.028,
    last_weights=0.012,
    join_shares=0.004,
    middle_backward=0.008,
    add_rows=0.002,
    others=0.002,
    output_and_gains=0.002,
    assemble_part=0.002,
    unpack_feed=0.018000000000000002,
    unpack_last=0.006,
)

f32 = jnp.float32
bf16 = jnp.bfloat16


def dot(left, right):
    return jnp.dot(left, right, preferred_element_type=f32)


def dot_nt(left, right):
    return lax.dot_general(left, right, (((1,), (1,)), ((), ())), preferred_element_type=f32)


def dot_tn(left, right):
    return lax.dot_general(left, right, (((0,), (0,)), ((), ())), preferred_element_type=f32)


def normed_of(values):
    inverse = lax.rsqrt(jnp.mean(values * values, -1, keepdims=True) + EPSILON)
    return values * inverse, inverse


def norm_back(incoming, normed, inverse, scales):
    scaled = incoming * scales
    return inverse * (scaled - normed * jnp.mean(scaled * normed, -1, keepdims=True))


def call(kernel, outs, *args, smem=0, scratch=(), name=None):
    many = isinstance(outs, (list, tuple))
    whole = pl.BlockSpec(memory_space=pltpu.VMEM)
    return pl.pallas_call(
        kernel,
        out_shape=tuple(outs) if many else outs,
        in_specs=[
            pl.BlockSpec(memory_space=pltpu.SMEM) if at < smem else whole
            for at in range(len(args))
        ],
        out_specs=(whole,) * len(outs) if many else whole,
        scratch_shapes=list(scratch),
        compiler_params=pltpu.CompilerParams(vmem_limit_bytes=56 * 1024 * 1024),
        cost_estimate=pl.CostEstimate(flops=int(COSTS[name] * 1.15e9), transcendentals=0, bytes_accessed=0),
        name=name,
    )(*args)


def shaped(*shape, dtype=bf16):
    return jax.ShapeDtypeStruct(shape, dtype)


def after(value, *others):
    return lax.optimization_barrier((value,) + others)[0]


def swap(value, bit):
    return lax.ppermute(value, "seq", [(i, i ^ bit) for i in range(SEQ)])


def chosen(rows, columns, chunk, padded, place):
    row = lax.broadcasted_iota(jnp.int32, (rows, columns), 0)
    column = lax.broadcasted_iota(jnp.int32, (rows, columns), 1)
    block = column // padded
    inside = column - block * padded
    wanted = block * (SEQ * chunk) + place * chunk + inside
    return jnp.where((row == wanted) & (inside < chunk), 1.0, 0.0).astype(bf16)


def pack_first(place_ref, query_ref, key_ref, value_ref, output_ref, *refs):
    gain_refs, out_ref = refs[:4], refs[4]
    shard, model = query_ref.shape
    part = model // SEQ
    columns = pl.ds(pl.multiple_of(place_ref[0] * part, part), part)
    for at, ref in enumerate((query_ref, key_ref, value_ref, output_ref)):
        out_ref[:shard, at * part:(at + 1) * part] = ref[:, columns]
    out_ref[shard:, :] = jnp.zeros((GAIN_ROWS, model), bf16)
    for at, ref in enumerate(gain_refs):
        out_ref[shard:shard + 1, at * shard:(at + 1) * shard] = ref[...]


def pack_feed(place_ref, gate_ref, up_ref, down_ref, out_ref, down_out_ref):
    place = place_ref[0]
    wide = gate_ref.shape[1] // 2
    narrow = out_ref.shape[1] // 4
    chunk = down_ref.shape[0] // SEQ
    padded = down_out_ref.shape[0]
    pick = chosen(wide, narrow, chunk, padded, place)
    for number, ref in enumerate((gate_ref, up_ref)):
        for half in range(2):
            at = (2 * number + half) * narrow
            out_ref[:, at:at + narrow] = dot(
                ref[:, half * wide:(half + 1) * wide], pick
            ).astype(bf16)
    pick_rows = chosen(SEQ * chunk, padded, chunk, padded, place)
    down_out_ref[...] = dot_tn(pick_rows, down_ref[...]).astype(bf16)


def blocks_of(at_ref, refs):
    step = 0
    for ref in refs:
        for at in range(ref.shape[0]):
            yield at_ref[step], ref.at[at]
            step += 1


def assemble(at_ref, *refs):
    out_ref = refs[-1]
    rows = refs[0].shape[1]
    for at, block in blocks_of(at_ref, refs[:-1]):
        out_ref[pl.ds(pl.multiple_of(at * rows, rows), rows), :] = block[...]


def others(at_ref, ref, out_ref):
    for step in range(out_ref.shape[0]):
        out_ref[step] = ref[at_ref[step]]


def output_and_gains(at_ref, *refs):
    refs, (output_ref, gain_ref) = refs[:-2], refs[-2:]
    shard = refs[0].shape[1] - GAIN_ROWS
    part = output_ref.shape[1]
    for step, (at, block) in enumerate(blocks_of(at_ref, refs)):
        rows = pl.ds(pl.multiple_of(at * shard, shard), shard)
        output_ref[rows, :] = block[:shard, 3 * part:]
        if shard % 128:
            columns = pl.ds(step * shard, shard)
        else:
            columns = pl.ds(pl.multiple_of(at * shard, shard), shard)
        for number in range(4):
            gain_ref[number:number + 1, columns] = block[
                shard:shard + 1, number * shard:(number + 1) * shard
            ].astype(f32)


def join_shares(gate_ref, up_ref, down_ref, out_ref):
    piece = out_ref.shape[1]
    row = 0
    for ref in (gate_ref, up_ref, down_ref):
        for at in range(0, ref.shape[1], piece):
            out_ref[row:row + ref.shape[0], :] = ref[:, at:at + piece]
            row += ref.shape[0]


def unpack_feed(place_ref, *refs, shard, padded):
    blocks, (gate_ref, up_ref, down_ref) = refs[:SEQ], refs[SEQ:]
    place = place_ref[0]
    chunk = down_ref.shape[0] // SEQ
    model = down_ref.shape[1]
    piece = blocks[0].shape[1]
    wide = gate_ref.shape[1] // 2
    below = blocks[0].shape[0] - model // piece * padded
    pieces = below // shard // 2
    narrow = pieces * piece // 2
    pick = jnp.concatenate(
        [chosen(wide, narrow, chunk, padded, place ^ at) for at in range(SEQ)], 1
    )
    for number, out_ref in enumerate((gate_ref, up_ref)):
        joined = [
            jnp.concatenate(
                [
                    ref[(number * pieces + at) * shard:(number * pieces + at + 1) * shard, :]
                    for at in range(pieces)
                ], 1,
            )
            for ref in blocks
        ]
        for half in range(2):
            parts = [part[:, half * narrow:(half + 1) * narrow] for part in joined]
            out_ref[:, half * wide:(half + 1) * wide] = dot_nt(jnp.concatenate(parts, 1), pick)
    rows = jnp.concatenate(
        [chosen(SEQ * chunk, padded, chunk, padded, place ^ at) for at in range(SEQ)], 1
    )
    for at in range(model // piece):
        parts = [ref[below + at * padded:below + (at + 1) * padded, :] for ref in blocks]
        down_ref[:, at * piece:(at + 1) * piece] = dot(rows, jnp.concatenate(parts, 0))


def unpack_last(place_ref, *refs, shard):
    blocks, (gain_ref, *weights), outs = refs[:SEQ], refs[SEQ:SEQ + 4], refs[SEQ + 4:]
    place = place_ref[0]
    part = blocks[0].shape[1] // SEQ
    for step, block in enumerate(blocks):
        columns = pl.ds(pl.multiple_of((place ^ step) * part, part), part)
        for at in range(4):
            outs[at][:, columns] = block[:shard, at * part:(at + 1) * part].astype(f32)
    outs[4][...] = sum(block[shard:, :].astype(f32) for block in blocks)
    total = sum(
        jnp.sum(ref[...].astype(f32) * out[...], 1, keepdims=True)
        for ref, out in zip(weights, outs[:3])
    )
    outs[5][...] = total.T / gain_ref[...].astype(f32)


def arrange(place_ref, *refs):
    blocks, out_ref = refs[:SEQ], refs[SEQ]
    place = place_ref[0]
    part = blocks[0].shape[1]
    for step in range(SEQ):
        rows = pl.ds(pl.multiple_of((place ^ step) * part, part), part)
        for other in range(SEQ):
            columns = pl.ds(pl.multiple_of((place ^ other) * part, part), part)
            out_ref[step * part:(step + 1) * part, columns] = blocks[other][rows, :]


def turn(rows, cosine, sine):
    return rows * cosine + pltpu.roll(rows, rows.shape[-1] // 2, axis=1) * sine


def visible(key_code, query_code, tile):
    key_wide = jnp.concatenate([key_code] * (tile // 128), axis=1)
    return (key_wide <= query_code[0:1, :]) & (key_wide >= query_code[1:2, :])


def key_codes(query_code_ref, key_code_ref):
    tiles, _, tile = query_code_ref.shape
    for step in range(tiles):
        wide = jnp.broadcast_to(query_code_ref[step, 0:1, :], (128, tile))
        key_code_ref[step * tile:(step + 1) * tile, :] = wide.T


def attend_forward(
    at_ref, gain_ref, cos_ref, sin_ref, query_code_ref, own_ref, near_ref, far_ref, both_ref,
    *refs,
):
    firsts, refs = refs[:-9], refs[-9:]
    low_ref, query_ref, key_ref, value_ref, out_ref, log_ref, weight_ref, token_ref, key_code_ref = refs
    window, model = low_ref.shape
    shard = firsts[0].shape[1] - GAIN_ROWS
    tiles, _, tile = query_code_ref.shape
    width = cos_ref.shape[1]
    heads = query_ref.shape[1] // width
    scale = LOG2_E * width ** (-0.5)
    for at, block in blocks_of(at_ref, firsts):
        rows = pl.ds(pl.multiple_of(at * shard, shard), shard)
        weight_ref[rows, :] = block[:shard, :3 * heads * width]
    for step, ref in enumerate((own_ref, near_ref, far_ref, both_ref)):
        token_ref[step * tile:(step + 1) * tile, :] = ref[...]
    key_codes(query_code_ref, key_code_ref)

    def project(step, carry):
        rows = pl.ds(pl.multiple_of(step * tile, tile), tile)
        normed, _ = normed_of(token_ref[rows, :].astype(f32))
        low = (normed * gain_ref[0:1, :]).astype(bf16)
        low_ref[rows, :] = low
        raw = dot(low, weight_ref[...])
        cosine = cos_ref[rows, :]
        sine = sin_ref[rows, :]
        for head in range(heads):
            at = head * width
            query_ref[rows, at:at + width] = turn(raw[:, at:at + width], cosine, sine).astype(bf16)
            at = (heads + head) * width
            key_ref[rows, head * width:(head + 1) * width] = turn(
                raw[:, at:at + width], cosine, sine
            ).astype(bf16)
        value_ref[rows, :] = raw[:, 2 * heads * width:].astype(bf16)
        return carry

    lax.fori_loop(0, window // tile, project, 0)
    for head in range(heads):
        cols = slice(head * width, (head + 1) * width)
        value_turned = value_ref[:, cols].astype(f32).T.astype(bf16)

        def one_tile(step, carry):
            rows = pl.ds(pl.multiple_of(step * tile, tile), tile)
            scores = dot_nt(key_ref[:, cols], query_ref[rows, cols])
            shown = visible(key_code_ref[...], query_code_ref[step], tile)
            scores = jnp.where(shown, scores * scale, HIDDEN_LOW)
            top = jnp.max(scores, 0, keepdims=True)
            weights = jnp.exp2(scores - top)
            total = jnp.sum(weights, 0, keepdims=True)
            result = dot(value_turned, weights.astype(bf16)) * (1.0 / total)
            out_ref[rows, cols] = result.T.astype(bf16)
            log_ref[head, step] = jnp.broadcast_to(top + jnp.log2(total), (8, tile))
            return carry

        lax.fori_loop(0, tiles, one_tile, 0)


def attend_backward(
    query_ref, key_ref, value_ref, log_ref, cos_ref, sin_ref, query_code_ref, *refs,
):
    incoming_refs = refs[:SEQ]
    grad_ref, key_sum, value_sum, incoming_ref, key_code_ref = refs[SEQ:]
    key_codes(query_code_ref, key_code_ref)
    tiles, _, tile = query_code_ref.shape
    width = cos_ref.shape[1]
    heads = query_ref.shape[1] // width
    factor = width ** (-0.5)
    scale = LOG2_E * factor
    for step, ref in enumerate(incoming_refs):
        incoming_ref[step * tile:(step + 1) * tile, :] = ref[...]
    for head in range(heads):
        cols = slice(head * width, (head + 1) * width)
        key_turned = key_ref[:, cols].astype(f32).T.astype(bf16)
        key_sum[...] = jnp.zeros_like(key_sum)
        value_sum[...] = jnp.zeros_like(value_sum)

        def one_tile(step, carry):
            rows = pl.ds(pl.multiple_of(step * tile, tile), tile)
            queries = query_ref[rows, cols]
            incoming = incoming_ref[rows, cols]
            scores = dot_nt(key_ref[:, cols], queries)
            shown = visible(key_code_ref[...], query_code_ref[step], tile)
            probs = jnp.where(shown, jnp.exp2(scores * scale - log_ref[head, step, 0:1, :]), 0.0)
            value_sum[...] += dot(probs.astype(bf16), incoming)
            prob_grad = dot_nt(value_ref[:, cols], incoming)
            inner = jnp.sum(probs * prob_grad, 0, keepdims=True)
            score_grad = (probs * (prob_grad - inner)).astype(bf16)
            key_sum[...] += dot(score_grad, queries)
            query_grad = (dot(key_turned, score_grad) * factor).T
            grad_ref[rows, cols] = turn(query_grad, cos_ref[rows, :], -sin_ref[rows, :]).astype(bf16)
            return carry

        lax.fori_loop(0, tiles, one_tile, 0)
        at = (heads + head) * width
        grad_ref[:, at:at + width] = turn(
            key_sum[...] * factor, cos_ref[...], -sin_ref[...]
        ).astype(bf16)
        at = (2 * heads + head) * width
        grad_ref[:, at:at + width] = value_sum[...].astype(bf16)


def feed_forward(
    first_ref, second_ref, weight_ref, down_ref, both_ref, active_ref, keep_ref, send_ref,
):
    rows, model = first_ref.shape
    half = down_ref.shape[0]
    low = jnp.concatenate([first_ref[...], second_ref[...]], 0)
    step = 256
    for at in range(0, half, step):
        gate_value = dot(low, weight_ref[:, at:at + step])
        up_value = dot(low, weight_ref[:, half + at:half + at + step])
        both_ref[:, at:at + step] = gate_value.astype(bf16)
        both_ref[:, half + at:half + at + step] = up_value.astype(bf16)
        active_ref[:, at:at + step] = (gate_value * jax.nn.sigmoid(gate_value) * up_value).astype(
            bf16
        )
    for at in range(0, model, step):
        total = dot(active_ref[...], down_ref[:, at:at + step])
        keep_ref[:, at:at + step] = total[:rows]
        send_ref[:, at:at + step] = total[rows:].astype(bf16)


def feed_backward(
    first_ref, second_ref, both_ref, weight_ref, down_ref, grad_ref, keep_ref, send_ref,
):
    rows, model = first_ref.shape
    half = down_ref.shape[0]
    low = jnp.concatenate([first_ref[...], second_ref[...]], 0)
    step = 256
    for at in range(0, half, step):
        active_grad = dot_nt(low, down_ref[at:at + step, :])
        gate_value = both_ref[:, at:at + step].astype(f32)
        up_value = both_ref[:, half + at:half + at + step].astype(f32)
        share = jax.nn.sigmoid(gate_value)
        scaled = active_grad * share
        grad_ref[:, at:at + step] = (
            scaled * up_value * (1.0 + gate_value * (1.0 - share))
        ).astype(bf16)
        grad_ref[:, half + at:half + at + step] = (scaled * gate_value).astype(bf16)
    for at in range(0, model, step):
        total = dot_nt(grad_ref[...], weight_ref[at:at + step, :])
        keep_ref[:, at:at + step] = total[:rows]
        send_ref[:, at:at + step] = total[rows:].astype(bf16)


def halves_out(side, full, shard, columns, keep_ref, send_ref):
    for level in range(full.shape[0] // shard // 2):
        to = slice(level * shard, (level + 1) * shard)
        for at, ref in ((2 * level + side, keep_ref), (2 * level + 1 - side, send_ref)):
            rows = pl.ds(pl.multiple_of(at * shard, shard), shard)
            ref[to, :] = full[rows, columns]


def feed_weights(
    side_ref, own_ref, near_ref, far_ref, both_ref, near_grad, far_grad,
    gate_keep, gate_send, up_keep, up_send, full, *, shard,
):
    low = jnp.concatenate([own_ref[...], near_ref[...], far_ref[...], both_ref[...]], 0)
    grad = jnp.concatenate([near_grad[...], far_grad[...]], 0)
    full[...] = dot_tn(low, grad).astype(bf16)
    half = gate_keep.shape[1]
    side = side_ref[0]
    halves_out(side, full, shard, slice(0, half), gate_keep, gate_send)
    halves_out(side, full, shard, slice(half, 2 * half), up_keep, up_send)


def down_weights(
    side_ref, own_ref, near_ref, far_ref, both_ref, near_active, far_active, keep_ref, send_ref,
    full, *, padded,
):
    grad = jnp.concatenate([own_ref[...], near_ref[...], far_ref[...], both_ref[...]], 0)
    active = jnp.concatenate([near_active[...], far_active[...]], 0)
    full[...] = dot_tn(active, grad).astype(bf16)
    halves_out(side_ref[0], full, padded, slice(None), keep_ref, send_ref)


def folded(values):
    return jnp.sum(values.reshape(-1, 8, values.shape[-1]), 0)


def middle_backward(
    keep_ref, near_ref, far_ref, hidden_ref, mixed_ref, incoming_ref, gain_ref, weight_ref,
    grad_ref, low_ref, sum_ref, *outs,
):
    rows = keep_ref.shape[0]
    step = 64
    middle_scale = gain_ref[2:3, :]
    attend_scale = gain_ref[1:2, :]

    def some(at, sums):
        part = pl.ds(pl.multiple_of(at * step, step), step)
        middle_grad = (
            keep_ref[part, :] + near_ref[part, :].astype(f32) + far_ref[part, :].astype(f32)
        )
        normed, inverse = normed_of(hidden_ref[part, :])
        grad = incoming_ref[part, :].astype(f32) + norm_back(
            middle_grad, normed, inverse, middle_scale
        )
        grad_ref[part, :] = grad
        middle_sum = sums[1] + folded(middle_grad * normed)
        normed, inverse = normed_of(mixed_ref[part, :])
        low_ref[part, :] = norm_back(grad, normed, inverse, attend_scale).astype(bf16)
        return sums[0] + folded(grad * normed), middle_sum

    empty = jnp.zeros((8, keep_ref.shape[1]), f32)
    sums = lax.fori_loop(0, rows // step, some, (empty, empty))
    sum_ref[0:8, :] = sums[0]
    sum_ref[8:16, :] = sums[1]
    size = outs[0].shape[1]
    for at, ref in enumerate(outs):
        ref[...] = dot_nt(low_ref[...], weight_ref[at * size:(at + 1) * size, :]).astype(bf16)


def output_weights(place_ref, low_ref, *refs):
    pieces, outs = refs[:SEQ], refs[SEQ:]
    place = place_ref[0]
    part = outs[0].shape[1]
    for step in range(SEQ):
        columns = pl.ds(pl.multiple_of((place ^ step) * part, part), part)
        for other in range(SEQ):
            rows = pl.ds(pl.multiple_of((place ^ other) * part, part), part)
            outs[step][rows, :] = dot_tn(pieces[other][...], low_ref[:, columns]).astype(
                outs[step].dtype
            )


def last_weights(at_ref, low_ref, grad_ref, keep_ref, near_ref, far_ref, sum_ref, *refs):
    outs, full = refs[:2], refs[2]
    wt = at_ref.shape[0]
    model = outs[0].shape[1]
    total = outs[0].shape[0] // (wt // 2)
    shard = total - GAIN_ROWS
    part = keep_ref.shape[1]
    full[:, :3 * part] = dot_tn(low_ref[...], grad_ref[...]).astype(bf16)
    full[:, 3 * part:] = (
        keep_ref[...] + near_ref[...].astype(f32) + far_ref[...].astype(f32)
    ).astype(bf16)
    for number, ref in enumerate(outs):
        for step in range(wt // 2):
            at = at_ref[number * (wt // 2) + step]
            row = step * total
            ref[row:row + shard, :] = full[pl.ds(pl.multiple_of(at * shard, shard), shard), :]
            ref[row + shard:row + total, :] = sum_ref[at]


def gather_levels(own, wt):
    return lax.all_gather(
        own, "wt", axis=0, tiled=False,
        axis_index_groups=[list(range(side, wt, 2)) for side in range(2)],
    )


def across(value, wt):
    return lax.ppermute(value, "wt", [(at, at ^ 1) for at in range(wt)])


def scatter_levels(value, wt):
    return lax.psum_scatter(
        value, "wt", scatter_dimension=0, tiled=True,
        axis_index_groups=[list(range(side, wt, 2)) for side in range(2)],
    )


def add_rows(left_ref, right_ref, out_ref):
    step = 32

    def some(at, carry):
        rows = pl.ds(pl.multiple_of(at * step, step), step)
        out_ref[rows, :] = (
            left_ref[rows, :].astype(f32) + right_ref[rows, :].astype(f32)
        ).astype(bf16)
        return carry

    lax.fori_loop(0, out_ref.shape[0] // step, some, 0, unroll=2)


def add_low(left, right):
    return call(add_rows, shaped(*left.shape), left, right, name="add_rows")


def on_device(
    tokens, positions, doc_ids, block_ids, entry_gain, query_weight, key_weight, value_weight,
    output_weight, attend_gain, middle_gain, gate_weight, up_weight, down_weight, closing_gain,
    cotangent,
):
    place = lax.axis_index("seq")
    order = [place ^ step for step in range(SEQ)]
    here = jnp.reshape(place, (1,)).astype(jnp.int32)
    rows, model = tokens.shape
    window = rows * SEQ
    shard = query_weight.shape[0]
    wt = model // shard
    part = model // SEQ
    width = model // HEADS
    heads = HEADS // SEQ
    hidden = gate_weight.shape[1]
    chunk = hidden // (wt * SEQ)
    padded = (chunk + 15) // 16 * 16
    hidden_part = padded * wt
    piece = 256

    def gather_blocks(own):
        far = swap(own, 2)
        near = swap(own, 1)
        return own, near, far, swap(far, 1)

    lines = wt == 8
    first_own = call(
        pack_first, shaped(shard + GAIN_ROWS, model),
        here, query_weight, key_weight, value_weight, output_weight,
        *(gain[None] for gain in (entry_gain, attend_gain, middle_gain, closing_gain)),
        smem=1, name="pack_first",
    )
    gate_up_own, down_own = call(
        pack_feed, (shaped(shard, 2 * hidden_part), shaped(padded, model)),
        here, gate_weight, up_weight, after(down_weight, first_own), smem=1, name="pack_feed",
    )
    mine = lax.axis_index("wt")
    level = mine // 2
    xside = mine % 2

    def numbers(*values):
        return jnp.stack([jnp.asarray(value, jnp.int32) for value in values])

    if lines:
        around = numbers(level ^ 1, level ^ 2, level ^ 3)
        whose = numbers(
            *[2 * at + xside for at in range(4)],
            *[2 * (level ^ at) + 1 - xside for at in range(4)],
        )
        first_z = gather_levels(first_own, wt)
        gate_up_z = gather_levels(gate_up_own, wt)
        first_x = across(first_own, wt)
        gate_up_x = across(gate_up_own, wt)
        down_x = across(down_own, wt)
        down_pair = jnp.where(
            xside == 0, jnp.stack([down_own, down_x]), jnp.stack([down_x, down_own])
        )
        down_part = gather_levels(down_pair, wt).reshape(hidden_part, model)
    else:
        whose = jnp.arange(wt, dtype=jnp.int32)
        first_z = lax.all_gather(first_own, "wt", axis=0, tiled=False)
        gate_up_z = lax.all_gather(gate_up_own, "wt", axis=0, tiled=False)
        down_part = lax.all_gather(down_own, "wt", axis=0, tiled=True)
    token_blocks = gather_blocks(tokens)
    cotangent_far = swap(after(cotangent, token_blocks[2]), 2)

    offsets = jnp.arange(window, dtype=jnp.int32)
    leading = doc_ids == doc_ids[0]
    boundary = jnp.sum(leading.astype(jnp.int32))
    places = jnp.where(leading, DOC_LEN - boundary + offsets, offsets - boundary)
    codes = doc_ids * DOC_STRIDE + block_ids
    lows = doc_ids * DOC_STRIDE
    packed = jnp.stack([places, codes, lows]).reshape(3, SEQ, rows)
    packed = jnp.concatenate(
        [lax.dynamic_index_in_dim(packed, at, 1, keepdims=False) for at in order], 1
    )
    half = width // 2
    frequency = ROTARY_BASE ** (-2.0 * jnp.arange(half, dtype=f32) / width)
    angles = packed[0].astype(f32)[:, None] * frequency[None, :]
    cosine = jnp.cos(angles)
    sine = jnp.sin(angles)
    cosine = jnp.concatenate([cosine, cosine], 1)
    sine = jnp.concatenate([-sine, sine], 1)
    query_code = jnp.broadcast_to(
        packed[1:3].astype(f32).reshape(2, SEQ, rows).transpose(1, 0, 2)[:, :, None, :], (SEQ, 2, 4, rows)
    ).transpose(0, 2, 1, 3).reshape(SEQ, 8, rows)

    waited = (cosine, sine, query_code, *token_blocks, cotangent_far)
    if lines:
        first_z = after(first_z, *waited, first_x, gate_up_x, down_pair)
        rest = call(
            others, shaped(3, shard + GAIN_ROWS, model), around, first_z, smem=1, name="others",
        )
        firsts = (first_z, first_x[None], across(rest, wt))
    else:
        firsts = (after(first_z, *waited),)
    output_own, gains = call(
        output_and_gains, (shaped(model, part), shaped(8, model, dtype=f32)),
        whose, *firsts, smem=1, name="output_and_gains",
    )
    entry_full, attend_full, middle_full, closing_full = [gains[at:at + 1] for at in range(4)]
    low_shape = shaped(window, heads * width)
    pair_cost = 2 * heads * window * window * width
    entry_low, query_low, key_low, value_low, attended, log_totals, qkv_weight = call(
        attend_forward,
        (shaped(window, model), low_shape, low_shape, low_shape, low_shape,
         shaped(heads, SEQ, 8, rows, dtype=f32), shaped(model, 3 * part)),
        whose, entry_full, cosine, sine, query_code, *token_blocks,
        after(firsts[0], output_own), *firsts[1:], smem=1,
        scratch=(
            pltpu.VMEM((window, model), bf16),
            pltpu.VMEM((window, 128), f32),
        ),
        name="attend_forward",
    )
    if lines:
        gate_up_z = after(gate_up_z, attended)
        rest = call(
            others, shaped(3, shard, 2 * hidden_part), around, gate_up_z, smem=1, name="others",
        )
        attended, rest = lax.optimization_barrier((attended, rest))
        gate_ups = (gate_up_z, gate_up_x[None], across(rest, wt))
    else:
        gate_ups = (gate_up_z,)
    output_far = after(swap(output_own, 2), attended)
    output_rows = call(
        arrange, shaped(model, model),
        here, output_own, swap(output_own, 1), output_far, swap(output_far, 1), smem=1,
        name="arrange",
    )

    gate_up = call(
        assemble, shaped(model, 2 * hidden_part), whose, *gate_ups, smem=1, name="assemble",
    )

    def exchange(blocks):
        return [blocks[0], swap(blocks[1], 1), swap(blocks[2], 2), swap(blocks[3], 3)]

    joined = exchange([attended[at * rows:(at + 1) * rows] for at in range(SEQ)])
    joined = [joined[0], joined[1]] + [after(got, output_rows) for got in joined[2:]]
    inputs = tokens.astype(f32)
    mixed = dot(jnp.concatenate(joined, 1), output_rows)
    attend_normed, attend_inverse = normed_of(mixed)
    hidden_state = inputs + attend_normed * attend_full
    middle_normed, middle_inverse = normed_of(hidden_state)
    middle_low = (middle_normed * middle_full).astype(bf16)

    full = shaped(rows, model, dtype=f32)
    both_shape = shaped(2 * rows, 2 * hidden_part)

    def forward(first_rows, second_rows):
        return call(
            feed_forward, (both_shape, shaped(2 * rows, hidden_part), full, shaped(rows, model)),
            first_rows, second_rows, gate_up, down_part, name="feed_forward",
        )

    def backward(first_rows, second_rows, both):
        return call(
            feed_backward, (both_shape, full, shaped(rows, model)),
            first_rows, second_rows, both, gate_up, down_part, name="feed_backward",
        )

    def chip_sum(values, weights, product):
        second = product(values[rows:], weights).astype(bf16)
        return product(values[:rows], weights) + swap(second, 1).astype(f32)

    middle_far = swap(middle_low, 2)
    middle_near = swap(middle_low, 1)
    fed_near = forward(middle_low, middle_near)
    middle_far = after(middle_far, fed_near[0])
    channel_near = fed_near[2] + swap(fed_near[3], 1).astype(f32)
    channel_send = channel_near.astype(bf16)
    far_other = swap(channel_send, 2)
    middle_both = after(swap(middle_far, 1), channel_send)
    fed_far = forward(middle_far, middle_both)
    far_other = after(far_other, fed_far[0])
    channel_far = fed_far[2] + swap(fed_far[3], 1).astype(f32)
    near_other = swap(channel_far.astype(bf16), 2)

    def close(channel_out, cotangents):
        normed, inverse = normed_of(channel_out)
        back = norm_back(cotangents.astype(f32), normed, inverse, closing_full)
        return normed, back.astype(bf16)

    _, low_far = close(channel_far + far_other.astype(f32), cotangent_far)
    low_both = swap(low_far, 1)
    back_far = backward(low_far, low_both, fed_far[0])
    near_other = after(near_other, back_far[0])
    middle_send = (back_far[1] + swap(back_far[2], 1).astype(f32)).astype(bf16)
    far_got = swap(middle_send, 2)
    closing_normed, channel_low = close(
        channel_near + after(near_other, middle_send).astype(f32), cotangent
    )
    layer_output = (hidden_state + closing_normed * closing_full).astype(bf16)
    incoming = cotangent.astype(f32)
    closing_sum = jnp.sum(incoming * closing_normed, 0)
    low_near = swap(channel_low, 1)
    down_shape = shaped(hidden_part // 2, model)
    side = jnp.reshape(lax.axis_index("wt") % 2, (1,)).astype(jnp.int32)
    down_keep, down_send = call(
        functools.partial(down_weights, padded=padded), (down_shape, down_shape),
        side, channel_low, low_near, low_far, low_both, fed_near[1], fed_far[1], smem=1,
        scratch=(pltpu.VMEM((hidden_part, model), bf16),), name="down_weights",
    )
    down_got = across(down_send, wt)
    back_near = backward(channel_low, after(low_near, down_keep), fed_near[0])
    near_got = swap(back_near[2], 1)
    gate_shape = shaped(model // 2, hidden_part)
    gate_keep, gate_send, up_keep, up_send = call(
        functools.partial(feed_weights, shard=shard),
        (gate_shape,) * 4, side, middle_low, middle_near, middle_far, middle_both,
        after(back_near[0], near_got), back_far[0], smem=1,
        scratch=(pltpu.VMEM((model, 2 * hidden_part), bf16),), name="feed_weights",
    )
    gate_got = across(gate_send, wt)
    up_got = across(up_send, wt)
    far_got = after(far_got, gate_keep)
    down_sum = add_low(down_keep, after(down_got, far_got))
    down_share = scatter_levels(down_sum, wt)
    hidden_grad, mixed_low, middle_sums, *attended_grads = call(
        middle_backward,
        (full, shaped(rows, model), shaped(16, model, dtype=f32)) + (shaped(rows, part),) * SEQ,
        back_near[1], near_got, after(far_got, down_sum), hidden_state, mixed, cotangent, gains,
        output_rows, name="middle_backward",
    )
    attend_sum = jnp.sum(middle_sums[:8], 0)
    middle_sum = jnp.sum(middle_sums[8:], 0)
    attended_back = exchange(attended_grads)
    output_grads = call(
        output_weights,
        (shaped(model, part, dtype=f32), shaped(model, part), shaped(model, part, dtype=f32),
         shaped(model, part)),
        here, after(mixed_low, attended_grads[1]), *joined, smem=1,
        name="output_weights",
    )
    attended_back[1:] = [after(got, output_grads[0]) for got in attended_back[1:]]
    output_far = (output_grads[2] + swap(output_grads[3], 1).astype(f32)).astype(bf16)
    output_near = swap(output_grads[1], 1)
    output_far = after(output_far, *attended_back)
    gate_sum = add_low(gate_keep, after(gate_got, *attended_back[1:]))
    gate_share = scatter_levels(gate_sum, wt)
    attended_back[0] = after(attended_back[0], output_far, gate_sum)
    output_got = swap(output_far, 2)
    qkv_grad = call(
        attend_backward, shaped(window, 3 * part),
        query_low, key_low, value_low, log_totals, cosine, sine, query_code,
        *attended_back,
        scratch=(
            pltpu.VMEM((window, width), f32), pltpu.VMEM((window, width), f32),
            pltpu.VMEM((window, heads * width), bf16), pltpu.VMEM((window, 128), f32),
        ), name="attend_backward",
    )
    gain_rows = jnp.stack([attend_sum, middle_sum, closing_sum]).astype(bf16)
    gain_rows = gain_rows.reshape(3, wt, shard).transpose(1, 0, 2).reshape(wt, 1, 3 * shard)
    gain_rows = jnp.pad(gain_rows, ((0, 0), (0, GAIN_ROWS - 1), (0, model - 3 * shard)))
    levels = range(0, wt, 2)
    whose = numbers(*[at + xside for at in levels], *[at + 1 - xside for at in levels])
    up_sum = add_low(up_keep, after(up_got, down_share, qkv_grad))
    up_share = scatter_levels(up_sum, wt)
    last_shape = shaped(wt // 2 * (shard + GAIN_ROWS), model)
    last_keep, last_send = call(
        last_weights, (last_shape, last_shape),
        whose, entry_low, after(qkv_grad, up_sum), output_grads[0], output_near, after(output_got, qkv_grad), gain_rows,
        smem=1, scratch=(pltpu.VMEM((model, model), bf16),), name="last_weights",
    )
    qkv_grad = after(qkv_grad, last_send)

    entry_far = chip_sum(qkv_grad[2 * rows:], qkv_weight, dot_nt).astype(bf16)
    entry_near = chip_sum(after(qkv_grad[:2 * rows], entry_far), qkv_weight, dot_nt)
    last_sum = add_low(last_keep, after(across(last_send, wt), gate_share, up_sum, entry_near))
    last_share = scatter_levels(last_sum, wt)
    entry_got = swap(entry_far, 2)
    share = call(
        join_shares, shaped((2 * hidden_part * shard + model * padded) // piece, piece),
        after(gate_share, last_sum), up_share, down_share, name="join_shares",
    )
    share_got = gather_blocks(share)
    grad_gate, grad_up, grad_down = call(
        functools.partial(unpack_feed, shard=shard, padded=padded),
        (shaped(shard, hidden, dtype=f32), shaped(shard, hidden, dtype=f32),
         shaped(SEQ * chunk, model, dtype=f32)),
        here, *share_got, smem=1, name="unpack_feed",
    )
    entry_grad = entry_near + after(entry_got, grad_down).astype(f32)
    entry_normed, entry_inverse = normed_of(inputs)
    input_grad = hidden_grad + norm_back(entry_grad, entry_normed, entry_inverse, entry_full)
    last_got = gather_blocks(after(last_share, grad_down))
    weight_shape = shaped(shard, model, dtype=f32)
    grad_query, grad_key, grad_value, grad_output, gain_sums, grad_entry = call(
        functools.partial(unpack_last, shard=shard),
        (weight_shape,) * 4
        + (shaped(GAIN_ROWS, model, dtype=f32), shaped(1, shard, dtype=f32)),
        here, last_share, last_got[1], last_got[2],
        last_got[3], entry_gain[None], query_weight, key_weight, value_weight, smem=1,
        name="unpack_last",
    )
    grad_attend, grad_middle, grad_closing = [
        gain_sums[0, at * shard:(at + 1) * shard] for at in range(3)
    ]
    return (
        layer_output, input_grad, grad_entry[0], grad_query, grad_key, grad_value, grad_output,
        grad_attend, grad_middle, grad_gate, grad_up, grad_down, grad_closing,
    )


def solution(mesh):
    rows = P(("wt", "seq"), None)
    weight = P("wt", None)
    gain = P("wt")
    return jax.shard_map(
        on_device,
        mesh=mesh,
        in_specs=(
            rows, P(("wt", "seq")), gain, gain, gain, weight, weight, weight, weight, gain, gain,
            weight, weight, weight, gain, rows,
        ),
        out_specs=(
            rows, rows, gain, weight, weight, weight, weight, gain, gain, weight, weight, weight,
            gain,
        ),
        check_vma=False,
    )
```

```python
import functools

import jax
import jax.numpy as jnp
from jax import lax
from jax.experimental import pallas as pl
from jax.experimental.pallas import tpu as pltpu
from jax.sharding import PartitionSpec as P

HEADS = 8
EPSILON = 1e-06
ROTARY_BASE = 50000.0
DOC_LEN = 8192
DOC_STRIDE = 64
HIDDEN_LOW = -1e30
LOG2_E = 1.4426950408889634
SEQ = 4
GAIN_ROWS = 8
GRANTS = dict(
    feed_forward=16,
    feed_backward=16,
    down_weights=16,
    feed_weights=24,
    add_rows=8,
    middle_backward=16,
    assemble=16,
    output_weights=16,
    others=16,
)
COSTS = dict(
    pack_first=0.004,
    pack_feed=0.008,
    assemble=0.008,
    attend_forward=0.03,
    arrange=0.006,
    feed_weights=0.016,
    down_weights=0.008,
    feed_forward=0.012,
    feed_backward=0.014,
    output_weights=0.006,
    attend_backward=0.028,
    last_weights=0.012,
    join_shares=0.004,
    middle_backward=0.008,
    add_rows=0.002,
    others=0.002,
    output_and_gains=0.002,
    assemble_part=0.002,
    unpack_feed=0.018000000000000002,
    unpack_last=0.006,
)

f32 = jnp.float32
bf16 = jnp.bfloat16


def dot(left, right):
    return jnp.dot(left, right, preferred_element_type=f32)


def dot_nt(left, right):
    return lax.dot_general(left, right, (((1,), (1,)), ((), ())), preferred_element_type=f32)


def dot_tn(left, right):
    return lax.dot_general(left, right, (((0,), (0,)), ((), ())), preferred_element_type=f32)


def normed_of(values):
    inverse = lax.rsqrt(jnp.mean(values * values, -1, keepdims=True) + EPSILON)
    return values * inverse, inverse


def norm_back(incoming, normed, inverse, scales):
    scaled = incoming * scales
    return inverse * (scaled - normed * jnp.mean(scaled * normed, -1, keepdims=True))


def call(kernel, outs, *args, smem=0, scratch=(), name=None):
    many = isinstance(outs, (list, tuple))
    whole = pl.BlockSpec(memory_space=pltpu.VMEM)
    return pl.pallas_call(
        kernel,
        out_shape=tuple(outs) if many else outs,
        in_specs=[
            pl.BlockSpec(memory_space=pltpu.SMEM) if at < smem else whole
            for at in range(len(args))
        ],
        out_specs=(whole,) * len(outs) if many else whole,
        scratch_shapes=list(scratch),
        compiler_params=pltpu.CompilerParams(vmem_limit_bytes=GRANTS.get(name, 56) * 1024 * 1024),
        cost_estimate=pl.CostEstimate(flops=int(COSTS[name] * 1.15e9), transcendentals=0, bytes_accessed=0),
        name=name,
    )(*args)


def shaped(*shape, dtype=bf16):
    return jax.ShapeDtypeStruct(shape, dtype)


def after(value, *others):
    return lax.optimization_barrier((value,) + others)[0]


def swap(value, bit):
    return lax.ppermute(value, "seq", [(i, i ^ bit) for i in range(SEQ)])


def chosen(rows, columns, chunk, padded, place):
    row = lax.broadcasted_iota(jnp.int32, (rows, columns), 0)
    column = lax.broadcasted_iota(jnp.int32, (rows, columns), 1)
    block = column // padded
    inside = column - block * padded
    wanted = block * (SEQ * chunk) + place * chunk + inside
    return jnp.where((row == wanted) & (inside < chunk), 1.0, 0.0).astype(bf16)


def pack_first(place_ref, query_ref, key_ref, value_ref, output_ref, *refs):
    gain_refs, out_ref = refs[:4], refs[4]
    shard, model = query_ref.shape
    part = model // SEQ
    columns = pl.ds(pl.multiple_of(place_ref[0] * part, part), part)
    for at, ref in enumerate((query_ref, key_ref, value_ref, output_ref)):
        out_ref[:shard, at * part:(at + 1) * part] = ref[:, columns]
    out_ref[shard:, :] = jnp.zeros((GAIN_ROWS, model), bf16)
    for at, ref in enumerate(gain_refs):
        out_ref[shard:shard + 1, at * shard:(at + 1) * shard] = ref[...]


def pack_feed(place_ref, gate_ref, up_ref, down_ref, out_ref, down_out_ref):
    place = place_ref[0]
    wide = gate_ref.shape[1] // 2
    narrow = out_ref.shape[1] // 4
    chunk = down_ref.shape[0] // SEQ
    padded = down_out_ref.shape[0]
    pick = chosen(wide, narrow, chunk, padded, place)
    for number, ref in enumerate((gate_ref, up_ref)):
        for half in range(2):
            at = (2 * number + half) * narrow
            out_ref[:, at:at + narrow] = dot(
                ref[:, half * wide:(half + 1) * wide], pick
            ).astype(bf16)
    pick_rows = chosen(SEQ * chunk, padded, chunk, padded, place)
    down_out_ref[...] = dot_tn(pick_rows, down_ref[...]).astype(bf16)


def blocks_of(at_ref, refs):
    step = 0
    for ref in refs:
        for at in range(ref.shape[0]):
            yield at_ref[step], ref.at[at]
            step += 1


def assemble(at_ref, *refs):
    out_ref = refs[-1]
    rows = refs[0].shape[1]
    for at, block in blocks_of(at_ref, refs[:-1]):
        out_ref[pl.ds(pl.multiple_of(at * rows, rows), rows), :] = block[...]


def others(at_ref, ref, out_ref):
    for step in range(out_ref.shape[0]):
        out_ref[step] = ref[at_ref[step]]


def output_and_gains(at_ref, *refs):
    refs, (output_ref, gain_ref) = refs[:-2], refs[-2:]
    shard = refs[0].shape[1] - GAIN_ROWS
    part = output_ref.shape[1]
    for step, (at, block) in enumerate(blocks_of(at_ref, refs)):
        rows = pl.ds(pl.multiple_of(at * shard, shard), shard)
        output_ref[rows, :] = block[:shard, 3 * part:]
        if shard % 128:
            columns = pl.ds(step * shard, shard)
        else:
            columns = pl.ds(pl.multiple_of(at * shard, shard), shard)
        for number in range(4):
            gain_ref[number:number + 1, columns] = block[
                shard:shard + 1, number * shard:(number + 1) * shard
            ].astype(f32)


def join_shares(gate_ref, up_ref, down_ref, out_ref):
    piece = out_ref.shape[1]
    row = 0
    for ref in (gate_ref, up_ref, down_ref):
        for at in range(0, ref.shape[1], piece):
            out_ref[row:row + ref.shape[0], :] = ref[:, at:at + piece]
            row += ref.shape[0]


def unpack_feed(place_ref, *refs, shard, padded):
    blocks, (gate_ref, up_ref, down_ref) = refs[:SEQ], refs[SEQ:]
    place = place_ref[0]
    chunk = down_ref.shape[0] // SEQ
    model = down_ref.shape[1]
    piece = blocks[0].shape[1]
    wide = gate_ref.shape[1] // 2
    below = blocks[0].shape[0] - model // piece * padded
    pieces = below // shard // 2
    narrow = pieces * piece // 2
    pick = jnp.concatenate(
        [chosen(wide, narrow, chunk, padded, place ^ at) for at in range(SEQ)], 1
    )
    for number, out_ref in enumerate((gate_ref, up_ref)):
        joined = [
            jnp.concatenate(
                [
                    ref[(number * pieces + at) * shard:(number * pieces + at + 1) * shard, :]
                    for at in range(pieces)
                ], 1,
            )
            for ref in blocks
        ]
        for half in range(2):
            parts = [part[:, half * narrow:(half + 1) * narrow] for part in joined]
            out_ref[:, half * wide:(half + 1) * wide] = dot_nt(jnp.concatenate(parts, 1), pick)
    rows = jnp.concatenate(
        [chosen(SEQ * chunk, padded, chunk, padded, place ^ at) for at in range(SEQ)], 1
    )
    for at in range(model // piece):
        parts = [ref[below + at * padded:below + (at + 1) * padded, :] for ref in blocks]
        down_ref[:, at * piece:(at + 1) * piece] = dot(rows, jnp.concatenate(parts, 0))


def unpack_last(place_ref, *refs, shard):
    blocks, (gain_ref, *weights), outs = refs[:SEQ], refs[SEQ:SEQ + 4], refs[SEQ + 4:]
    place = place_ref[0]
    part = blocks[0].shape[1] // SEQ
    for step, block in enumerate(blocks):
        columns = pl.ds(pl.multiple_of((place ^ step) * part, part), part)
        for at in range(4):
            outs[at][:, columns] = block[:shard, at * part:(at + 1) * part].astype(f32)
    outs[4][...] = sum(block[shard:, :].astype(f32) for block in blocks)
    total = sum(
        jnp.sum(ref[...].astype(f32) * out[...], 1, keepdims=True)
        for ref, out in zip(weights, outs[:3])
    )
    outs[5][...] = total.T / gain_ref[...].astype(f32)


def arrange(place_ref, *refs):
    blocks, out_ref = refs[:SEQ], refs[SEQ]
    place = place_ref[0]
    part = blocks[0].shape[1]
    for step in range(SEQ):
        rows = pl.ds(pl.multiple_of((place ^ step) * part, part), part)
        for other in range(SEQ):
            columns = pl.ds(pl.multiple_of((place ^ other) * part, part), part)
            out_ref[step * part:(step + 1) * part, columns] = blocks[other][rows, :]


def turn(rows, cosine, sine):
    return rows * cosine + pltpu.roll(rows, rows.shape[-1] // 2, axis=1) * sine


def visible(key_code, query_code, tile):
    key_wide = jnp.concatenate([key_code] * (tile // 128), axis=1)
    return (key_wide <= query_code[0:1, :]) & (key_wide >= query_code[1:2, :])


def key_codes(query_code_ref, key_code_ref):
    tiles, _, tile = query_code_ref.shape
    for step in range(tiles):
        wide = jnp.broadcast_to(query_code_ref[step, 0:1, :], (128, tile))
        key_code_ref[step * tile:(step + 1) * tile, :] = wide.T


def attend_forward(
    at_ref, gain_ref, cos_ref, sin_ref, query_code_ref, own_ref, near_ref, far_ref, both_ref,
    *refs,
):
    firsts, refs = refs[:-9], refs[-9:]
    low_ref, query_ref, key_ref, value_ref, out_ref, log_ref, weight_ref, token_ref, key_code_ref = refs
    window, model = low_ref.shape
    shard = firsts[0].shape[1] - GAIN_ROWS
    tiles, _, tile = query_code_ref.shape
    width = cos_ref.shape[1]
    heads = query_ref.shape[1] // width
    scale = LOG2_E * width ** (-0.5)
    for at, block in blocks_of(at_ref, firsts):
        rows = pl.ds(pl.multiple_of(at * shard, shard), shard)
        weight_ref[rows, :] = block[:shard, :3 * heads * width]
    for step, ref in enumerate((own_ref, near_ref, far_ref, both_ref)):
        token_ref[step * tile:(step + 1) * tile, :] = ref[...]
    key_codes(query_code_ref, key_code_ref)

    def project(step, carry):
        rows = pl.ds(pl.multiple_of(step * tile, tile), tile)
        normed, _ = normed_of(token_ref[rows, :].astype(f32))
        low = (normed * gain_ref[0:1, :]).astype(bf16)
        low_ref[rows, :] = low
        raw = dot(low, weight_ref[...])
        cosine = cos_ref[rows, :]
        sine = sin_ref[rows, :]
        for head in range(heads):
            at = head * width
            query_ref[rows, at:at + width] = turn(raw[:, at:at + width], cosine, sine).astype(bf16)
            at = (heads + head) * width
            key_ref[rows, head * width:(head + 1) * width] = turn(
                raw[:, at:at + width], cosine, sine
            ).astype(bf16)
        value_ref[rows, :] = raw[:, 2 * heads * width:].astype(bf16)
        return carry

    lax.fori_loop(0, window // tile, project, 0)
    for head in range(heads):
        cols = slice(head * width, (head + 1) * width)
        value_turned = value_ref[:, cols].astype(f32).T.astype(bf16)

        def one_tile(step, carry):
            rows = pl.ds(pl.multiple_of(step * tile, tile), tile)
            scores = dot_nt(key_ref[:, cols], query_ref[rows, cols])
            shown = visible(key_code_ref[...], query_code_ref[step], tile)
            scores = jnp.where(shown, scores * scale, HIDDEN_LOW)
            top = jnp.max(scores, 0, keepdims=True)
            weights = jnp.exp2(scores - top)
            total = jnp.sum(weights, 0, keepdims=True)
            result = dot(value_turned, weights.astype(bf16)) * (1.0 / total)
            out_ref[rows, cols] = result.T.astype(bf16)
            log_ref[head, step] = jnp.broadcast_to(top + jnp.log2(total), (8, tile))
            return carry

        lax.fori_loop(0, tiles, one_tile, 0)


def attend_backward(
    query_ref, key_ref, value_ref, log_ref, cos_ref, sin_ref, query_code_ref, *refs,
):
    incoming_refs = refs[:SEQ]
    grad_ref, key_sum, value_sum, incoming_ref, key_code_ref = refs[SEQ:]
    key_codes(query_code_ref, key_code_ref)
    tiles, _, tile = query_code_ref.shape
    width = cos_ref.shape[1]
    heads = query_ref.shape[1] // width
    factor = width ** (-0.5)
    scale = LOG2_E * factor
    for step, ref in enumerate(incoming_refs):
        incoming_ref[step * tile:(step + 1) * tile, :] = ref[...]
    for head in range(heads):
        cols = slice(head * width, (head + 1) * width)
        key_turned = key_ref[:, cols].astype(f32).T.astype(bf16)
        key_sum[...] = jnp.zeros_like(key_sum)
        value_sum[...] = jnp.zeros_like(value_sum)

        def one_tile(step, carry):
            rows = pl.ds(pl.multiple_of(step * tile, tile), tile)
            queries = query_ref[rows, cols]
            incoming = incoming_ref[rows, cols]
            scores = dot_nt(key_ref[:, cols], queries)
            shown = visible(key_code_ref[...], query_code_ref[step], tile)
            probs = jnp.where(shown, jnp.exp2(scores * scale - log_ref[head, step, 0:1, :]), 0.0)
            value_sum[...] += dot(probs.astype(bf16), incoming)
            prob_grad = dot_nt(value_ref[:, cols], incoming)
            inner = jnp.sum(probs * prob_grad, 0, keepdims=True)
            score_grad = (probs * (prob_grad - inner)).astype(bf16)
            key_sum[...] += dot(score_grad, queries)
            query_grad = (dot(key_turned, score_grad) * factor).T
            grad_ref[rows, cols] = turn(query_grad, cos_ref[rows, :], -sin_ref[rows, :]).astype(bf16)
            return carry

        lax.fori_loop(0, tiles, one_tile, 0)
        at = (heads + head) * width
        grad_ref[:, at:at + width] = turn(
            key_sum[...] * factor, cos_ref[...], -sin_ref[...]
        ).astype(bf16)
        at = (2 * heads + head) * width
        grad_ref[:, at:at + width] = value_sum[...].astype(bf16)


def feed_forward(
    first_ref, second_ref, weight_ref, down_ref, both_ref, active_ref, keep_ref, send_ref,
):
    rows, model = first_ref.shape
    half = down_ref.shape[0]
    low = jnp.concatenate([first_ref[...], second_ref[...]], 0)
    step = 256
    for at in range(0, half, step):
        gate_value = dot(low, weight_ref[:, at:at + step])
        up_value = dot(low, weight_ref[:, half + at:half + at + step])
        both_ref[:, at:at + step] = gate_value.astype(bf16)
        both_ref[:, half + at:half + at + step] = up_value.astype(bf16)
        active_ref[:, at:at + step] = (gate_value * jax.nn.sigmoid(gate_value) * up_value).astype(
            bf16
        )
    for at in range(0, model, step):
        total = dot(active_ref[...], down_ref[:, at:at + step])
        keep_ref[:, at:at + step] = total[:rows]
        send_ref[:, at:at + step] = total[rows:].astype(bf16)


def feed_backward(
    first_ref, second_ref, both_ref, weight_ref, down_ref, grad_ref, keep_ref, send_ref,
):
    rows, model = first_ref.shape
    half = down_ref.shape[0]
    low = jnp.concatenate([first_ref[...], second_ref[...]], 0)
    step = 256
    for at in range(0, half, step):
        active_grad = dot_nt(low, down_ref[at:at + step, :])
        gate_value = both_ref[:, at:at + step].astype(f32)
        up_value = both_ref[:, half + at:half + at + step].astype(f32)
        share = jax.nn.sigmoid(gate_value)
        scaled = active_grad * share
        grad_ref[:, at:at + step] = (
            scaled * up_value * (1.0 + gate_value * (1.0 - share))
        ).astype(bf16)
        grad_ref[:, half + at:half + at + step] = (scaled * gate_value).astype(bf16)
    for at in range(0, model, step):
        total = dot_nt(grad_ref[...], weight_ref[at:at + step, :])
        keep_ref[:, at:at + step] = total[:rows]
        send_ref[:, at:at + step] = total[rows:].astype(bf16)


def halves_out(side, full, shard, columns, keep_ref, send_ref):
    for level in range(full.shape[0] // shard // 2):
        to = slice(level * shard, (level + 1) * shard)
        for at, ref in ((2 * level + side, keep_ref), (2 * level + 1 - side, send_ref)):
            rows = pl.ds(pl.multiple_of(at * shard, shard), shard)
            ref[to, :] = full[rows, columns]


def feed_weights(
    side_ref, own_ref, near_ref, far_ref, both_ref, near_grad, far_grad,
    gate_keep, gate_send, up_keep, up_send, full, *, shard,
):
    low = jnp.concatenate([own_ref[...], near_ref[...], far_ref[...], both_ref[...]], 0)
    grad = jnp.concatenate([near_grad[...], far_grad[...]], 0)
    full[...] = dot_tn(low, grad).astype(bf16)
    half = gate_keep.shape[1]
    side = side_ref[0]
    halves_out(side, full, shard, slice(0, half), gate_keep, gate_send)
    halves_out(side, full, shard, slice(half, 2 * half), up_keep, up_send)


def down_weights(
    side_ref, own_ref, near_ref, far_ref, both_ref, near_active, far_active, keep_ref, send_ref,
    full, *, padded,
):
    grad = jnp.concatenate([own_ref[...], near_ref[...], far_ref[...], both_ref[...]], 0)
    active = jnp.concatenate([near_active[...], far_active[...]], 0)
    full[...] = dot_tn(active, grad).astype(bf16)
    halves_out(side_ref[0], full, padded, slice(None), keep_ref, send_ref)


def folded(values):
    return jnp.sum(values.reshape(-1, 8, values.shape[-1]), 0)


def middle_backward(
    keep_ref, near_ref, far_ref, hidden_ref, mixed_ref, incoming_ref, gain_ref, weight_ref,
    grad_ref, low_ref, sum_ref, *outs,
):
    rows = keep_ref.shape[0]
    step = 64
    middle_scale = gain_ref[2:3, :]
    attend_scale = gain_ref[1:2, :]

    def some(at, sums):
        part = pl.ds(pl.multiple_of(at * step, step), step)
        middle_grad = (
            keep_ref[part, :] + near_ref[part, :].astype(f32) + far_ref[part, :].astype(f32)
        )
        normed, inverse = normed_of(hidden_ref[part, :])
        grad = incoming_ref[part, :].astype(f32) + norm_back(
            middle_grad, normed, inverse, middle_scale
        )
        grad_ref[part, :] = grad
        middle_sum = sums[1] + folded(middle_grad * normed)
        normed, inverse = normed_of(mixed_ref[part, :])
        low_ref[part, :] = norm_back(grad, normed, inverse, attend_scale).astype(bf16)
        return sums[0] + folded(grad * normed), middle_sum

    empty = jnp.zeros((8, keep_ref.shape[1]), f32)
    sums = lax.fori_loop(0, rows // step, some, (empty, empty))
    sum_ref[0:8, :] = sums[0]
    sum_ref[8:16, :] = sums[1]
    size = outs[0].shape[1]
    for at, ref in enumerate(outs):
        ref[...] = dot_nt(low_ref[...], weight_ref[at * size:(at + 1) * size, :]).astype(bf16)


def output_weights(place_ref, low_ref, *refs):
    pieces, outs = refs[:SEQ], refs[SEQ:]
    place = place_ref[0]
    part = outs[0].shape[1]
    for step in range(SEQ):
        columns = pl.ds(pl.multiple_of((place ^ step) * part, part), part)
        for other in range(SEQ):
            rows = pl.ds(pl.multiple_of((place ^ other) * part, part), part)
            outs[step][rows, :] = dot_tn(pieces[other][...], low_ref[:, columns]).astype(
                outs[step].dtype
            )


def last_weights(at_ref, low_ref, grad_ref, keep_ref, near_ref, far_ref, sum_ref, *refs):
    outs, full = refs[:2], refs[2]
    wt = at_ref.shape[0]
    model = outs[0].shape[1]
    total = outs[0].shape[0] // (wt // 2)
    shard = total - GAIN_ROWS
    part = keep_ref.shape[1]
    full[:, :3 * part] = dot_tn(low_ref[...], grad_ref[...]).astype(bf16)
    full[:, 3 * part:] = (
        keep_ref[...] + near_ref[...].astype(f32) + far_ref[...].astype(f32)
    ).astype(bf16)
    for number, ref in enumerate(outs):
        for step in range(wt // 2):
            at = at_ref[number * (wt // 2) + step]
            row = step * total
            ref[row:row + shard, :] = full[pl.ds(pl.multiple_of(at * shard, shard), shard), :]
            ref[row + shard:row + total, :] = sum_ref[at]


def gather_levels(own, wt):
    return lax.all_gather(
        own, "wt", axis=0, tiled=False,
        axis_index_groups=[list(range(side, wt, 2)) for side in range(2)],
    )


def across(value, wt):
    return lax.ppermute(value, "wt", [(at, at ^ 1) for at in range(wt)])


def scatter_levels(value, wt):
    return lax.psum_scatter(
        value, "wt", scatter_dimension=0, tiled=True,
        axis_index_groups=[list(range(side, wt, 2)) for side in range(2)],
    )


def add_rows(left_ref, right_ref, out_ref):
    step = 32

    def some(at, carry):
        rows = pl.ds(pl.multiple_of(at * step, step), step)
        out_ref[rows, :] = (
            left_ref[rows, :].astype(f32) + right_ref[rows, :].astype(f32)
        ).astype(bf16)
        return carry

    lax.fori_loop(0, out_ref.shape[0] // step, some, 0, unroll=2)


def add_low(left, right):
    return call(add_rows, shaped(*left.shape), left, right, name="add_rows")


def on_device(
    tokens, positions, doc_ids, block_ids, entry_gain, query_weight, key_weight, value_weight,
    output_weight, attend_gain, middle_gain, gate_weight, up_weight, down_weight, closing_gain,
    cotangent,
):
    place = lax.axis_index("seq")
    order = [place ^ step for step in range(SEQ)]
    here = jnp.reshape(place, (1,)).astype(jnp.int32)
    rows, model = tokens.shape
    window = rows * SEQ
    shard = query_weight.shape[0]
    wt = model // shard
    part = model // SEQ
    width = model // HEADS
    heads = HEADS // SEQ
    hidden = gate_weight.shape[1]
    chunk = hidden // (wt * SEQ)
    padded = (chunk + 15) // 16 * 16
    hidden_part = padded * wt
    piece = 256

    def gather_blocks(own):
        far = swap(own, 2)
        near = swap(own, 1)
        return own, near, far, swap(far, 1)

    lines = wt == 8
    first_own = call(
        pack_first, shaped(shard + GAIN_ROWS, model),
        here, query_weight, key_weight, value_weight, output_weight,
        *(gain[None] for gain in (entry_gain, attend_gain, middle_gain, closing_gain)),
        smem=1, name="pack_first",
    )
    gate_up_own, down_own = call(
        pack_feed, (shaped(shard, 2 * hidden_part), shaped(padded, model)),
        here, gate_weight, up_weight, after(down_weight, first_own), smem=1, name="pack_feed",
    )
    mine = lax.axis_index("wt")
    level = mine // 2
    xside = mine % 2

    def numbers(*values):
        return jnp.stack([jnp.asarray(value, jnp.int32) for value in values])

    if lines:
        around = numbers(level ^ 1, level ^ 2, level ^ 3)
        whose = numbers(
            *[2 * at + xside for at in range(4)],
            *[2 * (level ^ at) + 1 - xside for at in range(4)],
        )
        first_z = gather_levels(first_own, wt)
        gate_up_z = gather_levels(gate_up_own, wt)
        first_x = across(first_own, wt)
        gate_up_x = across(gate_up_own, wt)
        down_x = across(down_own, wt)
        down_pair = jnp.where(
            xside == 0, jnp.stack([down_own, down_x]), jnp.stack([down_x, down_own])
        )
        down_part = gather_levels(down_pair, wt).reshape(hidden_part, model)
    else:
        whose = jnp.arange(wt, dtype=jnp.int32)
        first_z = lax.all_gather(first_own, "wt", axis=0, tiled=False)
        gate_up_z = lax.all_gather(gate_up_own, "wt", axis=0, tiled=False)
        down_part = lax.all_gather(down_own, "wt", axis=0, tiled=True)
    token_blocks = gather_blocks(tokens)
    cotangent_far = swap(after(cotangent, token_blocks[2]), 2)

    offsets = jnp.arange(window, dtype=jnp.int32)
    leading = doc_ids == doc_ids[0]
    boundary = jnp.sum(leading.astype(jnp.int32))
    places = jnp.where(leading, DOC_LEN - boundary + offsets, offsets - boundary)
    codes = doc_ids * DOC_STRIDE + block_ids
    lows = doc_ids * DOC_STRIDE
    packed = jnp.stack([places, codes, lows]).reshape(3, SEQ, rows)
    packed = jnp.concatenate(
        [lax.dynamic_index_in_dim(packed, at, 1, keepdims=False) for at in order], 1
    )
    half = width // 2
    frequency = ROTARY_BASE ** (-2.0 * jnp.arange(half, dtype=f32) / width)
    angles = packed[0].astype(f32)[:, None] * frequency[None, :]
    cosine = jnp.cos(angles)
    sine = jnp.sin(angles)
    cosine = jnp.concatenate([cosine, cosine], 1)
    sine = jnp.concatenate([-sine, sine], 1)
    query_code = jnp.broadcast_to(
        packed[1:3].astype(f32).reshape(2, SEQ, rows).transpose(1, 0, 2)[:, :, None, :], (SEQ, 2, 4, rows)
    ).transpose(0, 2, 1, 3).reshape(SEQ, 8, rows)

    waited = (cosine, sine, query_code, *token_blocks, cotangent_far)
    if lines:
        first_z = after(first_z, *waited, first_x, gate_up_x, down_pair)
        rest = call(
            others, shaped(3, shard + GAIN_ROWS, model), around, first_z, smem=1, name="others",
        )
        firsts = (first_z, first_x[None], across(rest, wt))
    else:
        firsts = (after(first_z, *waited),)
    output_own, gains = call(
        output_and_gains, (shaped(model, part), shaped(8, model, dtype=f32)),
        whose, *firsts, smem=1, name="output_and_gains",
    )
    entry_full, attend_full, middle_full, closing_full = [gains[at:at + 1] for at in range(4)]
    low_shape = shaped(window, heads * width)
    pair_cost = 2 * heads * window * window * width
    entry_low, query_low, key_low, value_low, attended, log_totals, qkv_weight = call(
        attend_forward,
        (shaped(window, model), low_shape, low_shape, low_shape, low_shape,
         shaped(heads, SEQ, 8, rows, dtype=f32), shaped(model, 3 * part)),
        whose, entry_full, cosine, sine, query_code, *token_blocks,
        after(firsts[0], output_own), *firsts[1:], smem=1,
        scratch=(
            pltpu.VMEM((window, model), bf16),
            pltpu.VMEM((window, 128), f32),
        ),
        name="attend_forward",
    )
    if lines:
        gate_up_z = after(gate_up_z, attended)
        rest = call(
            others, shaped(3, shard, 2 * hidden_part), around, gate_up_z, smem=1, name="others",
        )
        attended, rest = lax.optimization_barrier((attended, rest))
        gate_ups = (gate_up_z, gate_up_x[None], across(rest, wt))
    else:
        gate_ups = (gate_up_z,)
    output_far = after(swap(output_own, 2), attended)
    output_rows = call(
        arrange, shaped(model, model),
        here, output_own, swap(output_own, 1), output_far, swap(output_far, 1), smem=1,
        name="arrange",
    )

    gate_up = call(
        assemble, shaped(model, 2 * hidden_part), whose, *gate_ups, smem=1, name="assemble",
    )

    def exchange(blocks):
        return [blocks[0], swap(blocks[1], 1), swap(blocks[2], 2), swap(blocks[3], 3)]

    joined = exchange([attended[at * rows:(at + 1) * rows] for at in range(SEQ)])
    joined = [joined[0], joined[1]] + [after(got, output_rows) for got in joined[2:]]
    inputs = tokens.astype(f32)
    mixed = dot(jnp.concatenate(joined, 1), output_rows)
    attend_normed, attend_inverse = normed_of(mixed)
    hidden_state = inputs + attend_normed * attend_full
    middle_normed, middle_inverse = normed_of(hidden_state)
    middle_low = (middle_normed * middle_full).astype(bf16)

    full = shaped(rows, model, dtype=f32)
    both_shape = shaped(2 * rows, 2 * hidden_part)

    def forward(first_rows, second_rows):
        return call(
            feed_forward, (both_shape, shaped(2 * rows, hidden_part), full, shaped(rows, model)),
            first_rows, second_rows, gate_up, down_part, name="feed_forward",
        )

    def backward(first_rows, second_rows, both):
        return call(
            feed_backward, (both_shape, full, shaped(rows, model)),
            first_rows, second_rows, both, gate_up, down_part, name="feed_backward",
        )

    def chip_sum(values, weights, product):
        second = product(values[rows:], weights).astype(bf16)
        return product(values[:rows], weights) + swap(second, 1).astype(f32)

    middle_far = swap(middle_low, 2)
    middle_near = swap(middle_low, 1)
    fed_near = forward(middle_low, middle_near)
    middle_far = after(middle_far, fed_near[0])
    channel_near = fed_near[2] + swap(fed_near[3], 1).astype(f32)
    channel_send = channel_near.astype(bf16)
    far_other = swap(channel_send, 2)
    middle_both = after(swap(middle_far, 1), channel_send)
    fed_far = forward(middle_far, middle_both)
    far_other = after(far_other, fed_far[0])
    channel_far = fed_far[2] + swap(fed_far[3], 1).astype(f32)
    near_other = swap(channel_far.astype(bf16), 2)

    def close(channel_out, cotangents):
        normed, inverse = normed_of(channel_out)
        back = norm_back(cotangents.astype(f32), normed, inverse, closing_full)
        return normed, back.astype(bf16)

    _, low_far = close(channel_far + far_other.astype(f32), cotangent_far)
    low_both = swap(low_far, 1)
    back_far = backward(low_far, low_both, fed_far[0])
    near_other = after(near_other, back_far[0])
    middle_send = (back_far[1] + swap(back_far[2], 1).astype(f32)).astype(bf16)
    far_got = swap(middle_send, 2)
    closing_normed, channel_low = close(
        channel_near + after(near_other, middle_send).astype(f32), cotangent
    )
    layer_output = (hidden_state + closing_normed * closing_full).astype(bf16)
    incoming = cotangent.astype(f32)
    closing_sum = jnp.sum(incoming * closing_normed, 0)
    low_near = swap(channel_low, 1)
    down_shape = shaped(hidden_part // 2, model)
    side = jnp.reshape(lax.axis_index("wt") % 2, (1,)).astype(jnp.int32)
    down_keep, down_send = call(
        functools.partial(down_weights, padded=padded), (down_shape, down_shape),
        side, channel_low, low_near, low_far, low_both, fed_near[1], fed_far[1], smem=1,
        scratch=(pltpu.VMEM((hidden_part, model), bf16),), name="down_weights",
    )
    down_got = across(down_send, wt)
    back_near = backward(channel_low, after(low_near, down_keep), fed_near[0])
    near_got = swap(back_near[2], 1)
    gate_shape = shaped(model // 2, hidden_part)
    gate_keep, gate_send, up_keep, up_send = call(
        functools.partial(feed_weights, shard=shard),
        (gate_shape,) * 4, side, middle_low, middle_near, middle_far, middle_both,
        after(back_near[0], near_got), back_far[0], smem=1,
        scratch=(pltpu.VMEM((model, 2 * hidden_part), bf16),), name="feed_weights",
    )
    gate_got = across(gate_send, wt)
    up_got = across(up_send, wt)
    far_got = after(far_got, gate_keep)
    down_sum = add_low(down_keep, after(down_got, far_got))
    down_share = scatter_levels(down_sum, wt)
    hidden_grad, mixed_low, middle_sums, *attended_grads = call(
        middle_backward,
        (full, shaped(rows, model), shaped(16, model, dtype=f32)) + (shaped(rows, part),) * SEQ,
        back_near[1], near_got, after(far_got, down_sum), hidden_state, mixed, cotangent, gains,
        output_rows, name="middle_backward",
    )
    attend_sum = jnp.sum(middle_sums[:8], 0)
    middle_sum = jnp.sum(middle_sums[8:], 0)
    attended_back = exchange(attended_grads)
    output_grads = call(
        output_weights,
        (shaped(model, part, dtype=f32), shaped(model, part), shaped(model, part, dtype=f32),
         shaped(model, part)),
        here, after(mixed_low, attended_grads[1]), *joined, smem=1,
        name="output_weights",
    )
    attended_back[1:] = [after(got, output_grads[0]) for got in attended_back[1:]]
    output_far = (output_grads[2] + swap(output_grads[3], 1).astype(f32)).astype(bf16)
    output_near = swap(output_grads[1], 1)
    output_far = after(output_far, *attended_back)
    gate_sum = add_low(gate_keep, after(gate_got, *attended_back[1:]))
    gate_share = scatter_levels(gate_sum, wt)
    attended_back[0] = after(attended_back[0], output_far, gate_sum)
    output_got = swap(output_far, 2)
    qkv_grad = call(
        attend_backward, shaped(window, 3 * part),
        query_low, key_low, value_low, log_totals, cosine, sine, query_code,
        *attended_back,
        scratch=(
            pltpu.VMEM((window, width), f32), pltpu.VMEM((window, width), f32),
            pltpu.VMEM((window, heads * width), bf16), pltpu.VMEM((window, 128), f32),
        ), name="attend_backward",
    )
    gain_rows = jnp.stack([attend_sum, middle_sum, closing_sum]).astype(bf16)
    gain_rows = gain_rows.reshape(3, wt, shard).transpose(1, 0, 2).reshape(wt, 1, 3 * shard)
    gain_rows = jnp.pad(gain_rows, ((0, 0), (0, GAIN_ROWS - 1), (0, model - 3 * shard)))
    levels = range(0, wt, 2)
    whose = numbers(*[at + xside for at in levels], *[at + 1 - xside for at in levels])
    up_sum = add_low(up_keep, after(up_got, down_share, qkv_grad))
    up_share = scatter_levels(up_sum, wt)
    last_shape = shaped(wt // 2 * (shard + GAIN_ROWS), model)
    last_keep, last_send = call(
        last_weights, (last_shape, last_shape),
        whose, entry_low, after(qkv_grad, up_sum), output_grads[0], output_near, after(output_got, qkv_grad), gain_rows,
        smem=1, scratch=(pltpu.VMEM((model, model), bf16),), name="last_weights",
    )
    qkv_grad = after(qkv_grad, last_send)

    entry_far = chip_sum(qkv_grad[2 * rows:], qkv_weight, dot_nt).astype(bf16)
    entry_near = chip_sum(after(qkv_grad[:2 * rows], entry_far), qkv_weight, dot_nt)
    last_sum = add_low(last_keep, after(across(last_send, wt), gate_share, up_sum, entry_near))
    last_share = scatter_levels(last_sum, wt)
    entry_got = swap(entry_far, 2)
    share = call(
        join_shares, shaped((2 * hidden_part * shard + model * padded) // piece, piece),
        after(gate_share, last_sum), up_share, down_share, name="join_shares",
    )
    share_got = gather_blocks(share)
    grad_gate, grad_up, grad_down = call(
        functools.partial(unpack_feed, shard=shard, padded=padded),
        (shaped(shard, hidden, dtype=f32), shaped(shard, hidden, dtype=f32),
         shaped(SEQ * chunk, model, dtype=f32)),
        here, *share_got, smem=1, name="unpack_feed",
    )
    entry_grad = entry_near + after(entry_got, grad_down).astype(f32)
    entry_normed, entry_inverse = normed_of(inputs)
    input_grad = hidden_grad + norm_back(entry_grad, entry_normed, entry_inverse, entry_full)
    last_got = gather_blocks(after(last_share, grad_down))
    weight_shape = shaped(shard, model, dtype=f32)
    grad_query, grad_key, grad_value, grad_output, gain_sums, grad_entry = call(
        functools.partial(unpack_last, shard=shard),
        (weight_shape,) * 4
        + (shaped(GAIN_ROWS, model, dtype=f32), shaped(1, shard, dtype=f32)),
        here, last_share, last_got[1], last_got[2],
        last_got[3], entry_gain[None], query_weight, key_weight, value_weight, smem=1,
        name="unpack_last",
    )
    grad_attend, grad_middle, grad_closing = [
        gain_sums[0, at * shard:(at + 1) * shard] for at in range(3)
    ]
    return (
        layer_output, input_grad, grad_entry[0], grad_query, grad_key, grad_value, grad_output,
        grad_attend, grad_middle, grad_gate, grad_up, grad_down, grad_closing,
    )


def solution(mesh):
    rows = P(("wt", "seq"), None)
    weight = P("wt", None)
    gain = P("wt")
    return jax.shard_map(
        on_device,
        mesh=mesh,
        in_specs=(
            rows, P(("wt", "seq")), gain, gain, gain, weight, weight, weight, weight, gain, gain,
            weight, weight, weight, gain, rows,
        ),
        out_specs=(
            rows, rows, gain, weight, weight, weight, weight, gain, gain, weight, weight, weight,
            gain,
        ),
        check_vma=False,
    )
```

```python
import functools

import jax
import jax.numpy as jnp
from jax import lax
from jax.experimental import pallas as pl
from jax.experimental.pallas import tpu as pltpu
from jax.sharding import PartitionSpec as P

HEADS = 8
EPSILON = 1e-06
ROTARY_BASE = 50000.0
DOC_LEN = 8192
DOC_STRIDE = 64
HIDDEN_LOW = -1e30
LOG2_E = 1.4426950408889634
SEQ = 4
GAIN_ROWS = 8
GRANTS = dict(
    unpack_last=16,
    last_weights=24,
    feed_forward=16,
    feed_backward=16,
    down_weights=16,
    feed_weights=24,
    add_rows=8,
    middle_backward=56,
    assemble=16,
    output_weights=16,
    others=16,
)
COSTS = dict(
    pack_first=0.004,
    pack_feed=0.008,
    assemble=0.008,
    attend_forward=0.03,
    arrange=0.006,
    feed_weights=0.016,
    down_weights=0.008,
    feed_forward=0.012,
    feed_backward=0.014,
    output_weights=0.006,
    attend_backward=0.028,
    last_weights=0.012,
    join_shares=0.004,
    middle_backward=0.008,
    add_rows=0.002,
    others=0.002,
    output_and_gains=0.002,
    assemble_part=0.002,
    unpack_feed=0.018000000000000002,
    unpack_last=0.006,
)

f32 = jnp.float32
bf16 = jnp.bfloat16


def dot(left, right):
    return jnp.dot(left, right, preferred_element_type=f32)


def dot_nt(left, right):
    return lax.dot_general(left, right, (((1,), (1,)), ((), ())), preferred_element_type=f32)


def dot_tn(left, right):
    return lax.dot_general(left, right, (((0,), (0,)), ((), ())), preferred_element_type=f32)


def normed_of(values):
    inverse = lax.rsqrt(jnp.mean(values * values, -1, keepdims=True) + EPSILON)
    return values * inverse, inverse


def norm_back(incoming, normed, inverse, scales):
    scaled = incoming * scales
    return inverse * (scaled - normed * jnp.mean(scaled * normed, -1, keepdims=True))


def call(kernel, outs, *args, smem=0, scratch=(), name=None):
    many = isinstance(outs, (list, tuple))
    whole = pl.BlockSpec(memory_space=pltpu.VMEM)
    return pl.pallas_call(
        kernel,
        out_shape=tuple(outs) if many else outs,
        in_specs=[
            pl.BlockSpec(memory_space=pltpu.SMEM) if at < smem else whole
            for at in range(len(args))
        ],
        out_specs=(whole,) * len(outs) if many else whole,
        scratch_shapes=list(scratch),
        compiler_params=pltpu.CompilerParams(vmem_limit_bytes=GRANTS.get(name, 56) * 1024 * 1024),
        cost_estimate=pl.CostEstimate(flops=int(COSTS[name] * 1.15e9), transcendentals=0, bytes_accessed=0),
        name=name,
    )(*args)


def shaped(*shape, dtype=bf16):
    return jax.ShapeDtypeStruct(shape, dtype)


def after(value, *others):
    return lax.optimization_barrier((value,) + others)[0]


def swap(value, bit):
    return lax.ppermute(value, "seq", [(i, i ^ bit) for i in range(SEQ)])


def chosen(rows, columns, chunk, padded, place):
    row = lax.broadcasted_iota(jnp.int32, (rows, columns), 0)
    column = lax.broadcasted_iota(jnp.int32, (rows, columns), 1)
    block = column // padded
    inside = column - block * padded
    wanted = block * (SEQ * chunk) + place * chunk + inside
    return jnp.where((row == wanted) & (inside < chunk), 1.0, 0.0).astype(bf16)


def pack_first(place_ref, query_ref, key_ref, value_ref, output_ref, *refs):
    gain_refs, out_ref = refs[:4], refs[4]
    shard, model = query_ref.shape
    part = model // SEQ
    columns = pl.ds(pl.multiple_of(place_ref[0] * part, part), part)
    for at, ref in enumerate((query_ref, key_ref, value_ref, output_ref)):
        out_ref[:shard, at * part:(at + 1) * part] = ref[:, columns]
    out_ref[shard:, :] = jnp.zeros((GAIN_ROWS, model), bf16)
    for at, ref in enumerate(gain_refs):
        out_ref[shard:shard + 1, at * shard:(at + 1) * shard] = ref[...]


def pack_feed(place_ref, gate_ref, up_ref, down_ref, out_ref, down_out_ref):
    place = place_ref[0]
    wide = gate_ref.shape[1] // 2
    narrow = out_ref.shape[1] // 4
    chunk = down_ref.shape[0] // SEQ
    padded = down_out_ref.shape[0]
    pick = chosen(wide, narrow, chunk, padded, place)
    for number, ref in enumerate((gate_ref, up_ref)):
        for half in range(2):
            at = (2 * number + half) * narrow
            out_ref[:, at:at + narrow] = dot(
                ref[:, half * wide:(half + 1) * wide], pick
            ).astype(bf16)
    pick_rows = chosen(SEQ * chunk, padded, chunk, padded, place)
    down_out_ref[...] = dot_tn(pick_rows, down_ref[...]).astype(bf16)


def blocks_of(at_ref, refs):
    step = 0
    for ref in refs:
        for at in range(ref.shape[0]):
            yield at_ref[step], ref.at[at]
            step += 1


def assemble(at_ref, *refs):
    out_ref = refs[-1]
    rows = refs[0].shape[1]
    for at, block in blocks_of(at_ref, refs[:-1]):
        out_ref[pl.ds(pl.multiple_of(at * rows, rows), rows), :] = block[...]


def others(at_ref, ref, out_ref):
    for step in range(out_ref.shape[0]):
        out_ref[step] = ref[at_ref[step]]


def output_and_gains(at_ref, *refs):
    refs, (output_ref, gain_ref) = refs[:-2], refs[-2:]
    shard = refs[0].shape[1] - GAIN_ROWS
    part = output_ref.shape[1]
    for step, (at, block) in enumerate(blocks_of(at_ref, refs)):
        rows = pl.ds(pl.multiple_of(at * shard, shard), shard)
        output_ref[rows, :] = block[:shard, 3 * part:]
        if shard % 128:
            columns = pl.ds(step * shard, shard)
        else:
            columns = pl.ds(pl.multiple_of(at * shard, shard), shard)
        for number in range(4):
            gain_ref[number:number + 1, columns] = block[
                shard:shard + 1, number * shard:(number + 1) * shard
            ].astype(f32)


def join_shares(gate_ref, up_ref, down_ref, out_ref):
    piece = out_ref.shape[1]
    row = 0
    for ref in (gate_ref, up_ref, down_ref):
        for at in range(0, ref.shape[1], piece):
            out_ref[row:row + ref.shape[0], :] = ref[:, at:at + piece]
            row += ref.shape[0]


def unpack_feed(place_ref, *refs, shard, padded):
    blocks, (gate_ref, up_ref, down_ref) = refs[:SEQ], refs[SEQ:]
    place = place_ref[0]
    chunk = down_ref.shape[0] // SEQ
    model = down_ref.shape[1]
    piece = blocks[0].shape[1]
    wide = gate_ref.shape[1] // 2
    below = blocks[0].shape[0] - model // piece * padded
    pieces = below // shard // 2
    narrow = pieces * piece // 2
    pick = jnp.concatenate(
        [chosen(wide, narrow, chunk, padded, place ^ at) for at in range(SEQ)], 1
    )
    for number, out_ref in enumerate((gate_ref, up_ref)):
        joined = [
            jnp.concatenate(
                [
                    ref[(number * pieces + at) * shard:(number * pieces + at + 1) * shard, :]
                    for at in range(pieces)
                ], 1,
            )
            for ref in blocks
        ]
        for half in range(2):
            parts = [part[:, half * narrow:(half + 1) * narrow] for part in joined]
            out_ref[:, half * wide:(half + 1) * wide] = dot_nt(jnp.concatenate(parts, 1), pick)
    rows = jnp.concatenate(
        [chosen(SEQ * chunk, padded, chunk, padded, place ^ at) for at in range(SEQ)], 1
    )
    for at in range(model // piece):
        parts = [ref[below + at * padded:below + (at + 1) * padded, :] for ref in blocks]
        down_ref[:, at * piece:(at + 1) * piece] = dot(rows, jnp.concatenate(parts, 0))


def unpack_last(place_ref, *refs, shard):
    blocks, (gain_ref, *weights), outs = refs[:SEQ], refs[SEQ:SEQ + 4], refs[SEQ + 4:]
    place = place_ref[0]
    part = blocks[0].shape[1] // SEQ
    for step, block in enumerate(blocks):
        columns = pl.ds(pl.multiple_of((place ^ step) * part, part), part)
        for at in range(4):
            outs[at][:, columns] = block[:shard, at * part:(at + 1) * part].astype(f32)
    sums = sum(block[shard:, :].astype(f32) for block in blocks)
    for at, ref in enumerate(outs[5:]):
        ref[...] = sums[0:1, at * shard:(at + 1) * shard]
    total = sum(
        jnp.sum(ref[...].astype(f32) * out[...], 1, keepdims=True)
        for ref, out in zip(weights, outs[:3])
    )
    outs[4][...] = total.T / gain_ref[...].astype(f32)


def arrange(place_ref, *refs):
    blocks, out_ref = refs[:SEQ], refs[SEQ]
    place = place_ref[0]
    part = blocks[0].shape[1]
    for step in range(SEQ):
        rows = pl.ds(pl.multiple_of((place ^ step) * part, part), part)
        for other in range(SEQ):
            columns = pl.ds(pl.multiple_of((place ^ other) * part, part), part)
            out_ref[step * part:(step + 1) * part, columns] = blocks[other][rows, :]


def turn(rows, cosine, sine):
    return rows * cosine + pltpu.roll(rows, rows.shape[-1] // 2, axis=1) * sine


def visible(key_code, query_code, tile):
    key_wide = jnp.concatenate([key_code] * (tile // 128), axis=1)
    return (key_wide <= query_code[0:1, :]) & (key_wide >= query_code[1:2, :])


def key_codes(query_code_ref, key_code_ref):
    tiles, _, tile = query_code_ref.shape
    for step in range(tiles):
        wide = jnp.broadcast_to(query_code_ref[step, 0:1, :], (128, tile))
        key_code_ref[step * tile:(step + 1) * tile, :] = wide.T


def attend_forward(
    at_ref, gain_ref, cos_ref, sin_ref, query_code_ref, own_ref, near_ref, far_ref, both_ref,
    *refs,
):
    firsts, refs = refs[:-9], refs[-9:]
    low_ref, query_ref, key_ref, value_ref, out_ref, log_ref, weight_ref, token_ref, key_code_ref = refs
    window, model = low_ref.shape
    shard = firsts[0].shape[1] - GAIN_ROWS
    tiles, _, tile = query_code_ref.shape
    width = cos_ref.shape[1]
    heads = query_ref.shape[1] // width
    scale = LOG2_E * width ** (-0.5)
    for at, block in blocks_of(at_ref, firsts):
        rows = pl.ds(pl.multiple_of(at * shard, shard), shard)
        weight_ref[rows, :] = block[:shard, :3 * heads * width]
    for step, ref in enumerate((own_ref, near_ref, far_ref, both_ref)):
        token_ref[step * tile:(step + 1) * tile, :] = ref[...]
    key_codes(query_code_ref, key_code_ref)

    def project(step, carry):
        rows = pl.ds(pl.multiple_of(step * tile, tile), tile)
        normed, _ = normed_of(token_ref[rows, :].astype(f32))
        low = (normed * gain_ref[0:1, :]).astype(bf16)
        low_ref[rows, :] = low
        raw = dot(low, weight_ref[...])
        cosine = cos_ref[rows, :]
        sine = sin_ref[rows, :]
        for head in range(heads):
            at = head * width
            query_ref[rows, at:at + width] = turn(raw[:, at:at + width], cosine, sine).astype(bf16)
            at = (heads + head) * width
            key_ref[rows, head * width:(head + 1) * width] = turn(
                raw[:, at:at + width], cosine, sine
            ).astype(bf16)
        value_ref[rows, :] = raw[:, 2 * heads * width:].astype(bf16)
        return carry

    lax.fori_loop(0, window // tile, project, 0)
    turned = [
        value_ref[:, head * width:(head + 1) * width].astype(f32).T.astype(bf16)
        for head in range(heads)
    ]

    def one_tile(step, carry):
        rows = pl.ds(pl.multiple_of(step * tile, tile), tile)
        shown = visible(key_code_ref[...], query_code_ref[step], tile)
        for head in range(heads):
            cols = slice(head * width, (head + 1) * width)
            scores = dot_nt(key_ref[:, cols], query_ref[rows, cols])
            scores = jnp.where(shown, scores * scale, HIDDEN_LOW)
            top = jnp.max(scores, 0, keepdims=True)
            weights = jnp.exp2(scores - top)
            total = jnp.sum(weights, 0, keepdims=True)
            result = dot(turned[head], weights.astype(bf16)) * (1.0 / total)
            out_ref[rows, cols] = result.T.astype(bf16)
            log_ref[head, step] = jnp.broadcast_to(top + jnp.log2(total), (8, tile))
        return carry

    lax.fori_loop(0, tiles, one_tile, 0)


def attend_backward(
    query_ref, key_ref, value_ref, out_ref, log_ref, cos_ref, sin_ref, query_code_ref, *refs,
):
    incoming_refs, (grad_ref, *scratch) = refs[:SEQ], refs[SEQ:]
    key_sum, value_sum, incoming_ref, key_code_ref = scratch
    key_codes(query_code_ref, key_code_ref)
    tiles, _, tile = query_code_ref.shape
    width = cos_ref.shape[1]
    heads = query_ref.shape[1] // width
    factor = width ** (-0.5)
    scale = LOG2_E * factor
    for step, ref in enumerate(incoming_refs):
        incoming_ref[step * tile:(step + 1) * tile, :] = ref[...]
    turned = [
        key_ref[:, head * width:(head + 1) * width].astype(f32).T.astype(bf16)
        for head in range(heads)
    ]
    key_sum[...] = jnp.zeros_like(key_sum)
    value_sum[...] = jnp.zeros_like(value_sum)

    def one_tile(step, carry):
        rows = pl.ds(pl.multiple_of(step * tile, tile), tile)
        shown = visible(key_code_ref[...], query_code_ref[step], tile)
        for head in range(heads):
            cols = slice(head * width, (head + 1) * width)
            queries = query_ref[rows, cols]
            incoming = incoming_ref[rows, cols]
            products = incoming.astype(f32) * out_ref[rows, cols].astype(f32)
            inner = jnp.sum(products.T, 0, keepdims=True)
            scores = dot_nt(key_ref[:, cols], queries)
            probs = jnp.where(shown, jnp.exp2(scores * scale - log_ref[head, step, 0:1, :]), 0.0)
            value_sum[head] += dot(probs.astype(bf16), incoming)
            prob_grad = dot_nt(value_ref[:, cols], incoming)
            score_grad = (probs * (prob_grad - inner)).astype(bf16)
            key_sum[head] += dot(score_grad, queries)
            query_grad = (dot(turned[head], score_grad) * factor).T
            grad_ref[rows, cols] = turn(query_grad, cos_ref[rows, :], -sin_ref[rows, :]).astype(bf16)
        return carry

    lax.fori_loop(0, tiles, one_tile, 0)
    for head in range(heads):
        at = (heads + head) * width
        grad_ref[:, at:at + width] = turn(
            key_sum[head] * factor, cos_ref[...], -sin_ref[...]
        ).astype(bf16)
        at = (2 * heads + head) * width
        grad_ref[:, at:at + width] = value_sum[head].astype(bf16)


def feed_forward(
    first_ref, second_ref, weight_ref, down_ref, both_ref, active_ref, keep_ref, send_ref,
):
    rows, model = first_ref.shape
    half = down_ref.shape[0]
    low = jnp.concatenate([first_ref[...], second_ref[...]], 0)
    step = 256
    for at in range(0, half, step):
        gate_value = dot(low, weight_ref[:, at:at + step])
        up_value = dot(low, weight_ref[:, half + at:half + at + step])
        both_ref[:, at:at + step] = gate_value.astype(bf16)
        both_ref[:, half + at:half + at + step] = up_value.astype(bf16)
        active_ref[:, at:at + step] = (gate_value * jax.nn.sigmoid(gate_value) * up_value).astype(
            bf16
        )
    for at in range(0, model, step):
        total = dot(active_ref[...], down_ref[:, at:at + step])
        keep_ref[:, at:at + step] = total[:rows]
        send_ref[:, at:at + step] = total[rows:].astype(bf16)


def feed_backward(
    first_ref, second_ref, both_ref, weight_ref, down_ref, grad_ref, keep_ref, send_ref,
):
    rows, model = first_ref.shape
    half = down_ref.shape[0]
    low = jnp.concatenate([first_ref[...], second_ref[...]], 0)
    step = 256
    for at in range(0, half, step):
        active_grad = dot_nt(low, down_ref[at:at + step, :])
        gate_value = both_ref[:, at:at + step].astype(f32)
        up_value = both_ref[:, half + at:half + at + step].astype(f32)
        share = jax.nn.sigmoid(gate_value)
        scaled = active_grad * share
        grad_ref[:, at:at + step] = (
            scaled * up_value * (1.0 + gate_value * (1.0 - share))
        ).astype(bf16)
        grad_ref[:, half + at:half + at + step] = (scaled * gate_value).astype(bf16)
    for at in range(0, model, step):
        total = dot_nt(grad_ref[...], weight_ref[at:at + step, :])
        keep_ref[:, at:at + step] = total[:rows]
        send_ref[:, at:at + step] = total[rows:].astype(bf16)


def halves_out(side, full, shard, columns, keep_ref, send_ref):
    for level in range(full.shape[0] // shard // 2):
        to = slice(level * shard, (level + 1) * shard)
        for at, ref in ((2 * level + side, keep_ref), (2 * level + 1 - side, send_ref)):
            rows = pl.ds(pl.multiple_of(at * shard, shard), shard)
            ref[to, :] = full[rows, columns]


def feed_weights(
    side_ref, own_ref, near_ref, far_ref, both_ref, near_grad, far_grad,
    gate_keep, gate_send, up_keep, up_send, full, *, shard,
):
    low = jnp.concatenate([own_ref[...], near_ref[...], far_ref[...], both_ref[...]], 0)
    grad = jnp.concatenate([near_grad[...], far_grad[...]], 0)
    full[...] = dot_tn(low, grad).astype(bf16)
    half = gate_keep.shape[1]
    side = side_ref[0]
    halves_out(side, full, shard, slice(0, half), gate_keep, gate_send)
    halves_out(side, full, shard, slice(half, 2 * half), up_keep, up_send)


def down_weights(
    side_ref, own_ref, near_ref, far_ref, both_ref, near_active, far_active, keep_ref, send_ref,
    full, *, padded,
):
    grad = jnp.concatenate([own_ref[...], near_ref[...], far_ref[...], both_ref[...]], 0)
    active = jnp.concatenate([near_active[...], far_active[...]], 0)
    full[...] = dot_tn(active, grad).astype(bf16)
    halves_out(side_ref[0], full, padded, slice(None), keep_ref, send_ref)


def folded(values):
    return jnp.sum(values.reshape(-1, 8, values.shape[-1]), 0)


def middle_backward(
    keep_ref, near_ref, far_ref, hidden_ref, mixed_ref, incoming_ref, gain_ref, weight_ref,
    grad_ref, low_ref, sum_ref, *outs,
):
    step = pl.program_id(0)
    rows = keep_ref.shape[0]
    *outs, all_low = outs
    middle_grad = keep_ref[...] + near_ref[...].astype(f32) + far_ref[...].astype(f32)
    normed, inverse = normed_of(hidden_ref[...])
    grad = incoming_ref[...].astype(f32) + norm_back(
        middle_grad, normed, inverse, gain_ref[2:3, :]
    )
    grad_ref[...] = grad
    middle_sum = folded(middle_grad * normed)
    normed, inverse = normed_of(mixed_ref[...])
    low = norm_back(grad, normed, inverse, gain_ref[1:2, :]).astype(bf16)
    low_ref[...] = low
    all_low[pl.ds(pl.multiple_of(step * rows, rows), rows), :] = low

    @pl.when(step == 0)
    def _():
        sum_ref[...] = jnp.zeros_like(sum_ref)

    sum_ref[0:8, :] += folded(grad * normed)
    sum_ref[8:16, :] += middle_sum

    @pl.when(step == pl.num_programs(0) - 1)
    def _():
        size = outs[0].shape[1]
        for at, ref in enumerate(outs):
            ref[...] = dot_nt(all_low[...], weight_ref[at * size:(at + 1) * size, :]).astype(bf16)


def output_weights(place_ref, low_ref, *refs):
    pieces, outs = refs[:SEQ], refs[SEQ:]
    place = place_ref[0]
    part = outs[0].shape[1]
    for step in range(SEQ):
        columns = pl.ds(pl.multiple_of((place ^ step) * part, part), part)
        for other in range(SEQ):
            rows = pl.ds(pl.multiple_of((place ^ other) * part, part), part)
            outs[step][rows, :] = dot_tn(pieces[other][...], low_ref[:, columns]).astype(
                outs[step].dtype
            )


def last_weights(
    at_ref, low_ref, grad_ref, keep_ref, near_ref, far_ref, middle_ref, closing_ref, *refs
):
    outs, full, sum_ref = refs[:2], refs[2], refs[3]
    wt = at_ref.shape[0]
    model = outs[0].shape[1]
    total = outs[0].shape[0] // (wt // 2)
    shard = total - GAIN_ROWS
    part = keep_ref.shape[1]
    full[:, :3 * part] = dot_tn(low_ref[...], grad_ref[...]).astype(bf16)
    full[:, 3 * part:] = (
        keep_ref[...] + near_ref[...].astype(f32) + far_ref[...].astype(f32)
    ).astype(bf16)
    sums = (
        jnp.sum(middle_ref[:8, :], 0, keepdims=True), jnp.sum(middle_ref[8:, :], 0, keepdims=True),
        closing_ref[...],
    )
    sum_ref[...] = jnp.zeros_like(sum_ref)
    for at in range(wt):
        for number, total_row in enumerate(sums):
            sum_ref[at, 0:1, number * shard:(number + 1) * shard] = total_row[
                :, at * shard:(at + 1) * shard
            ].astype(bf16)
    for number, ref in enumerate(outs):
        for step in range(wt // 2):
            at = at_ref[number * (wt // 2) + step]
            row = step * total
            ref[row:row + shard, :] = full[pl.ds(pl.multiple_of(at * shard, shard), shard), :]
            ref[row + shard:row + total, :] = sum_ref[at]


def gather_levels(own, wt):
    return lax.all_gather(
        own, "wt", axis=0, tiled=False,
        axis_index_groups=[list(range(side, wt, 2)) for side in range(2)],
    )


def across(value, wt):
    return lax.ppermute(value, "wt", [(at, at ^ 1) for at in range(wt)])


def scatter_levels(value, wt):
    return lax.psum_scatter(
        value, "wt", scatter_dimension=0, tiled=True,
        axis_index_groups=[list(range(side, wt, 2)) for side in range(2)],
    )


def add_rows(left_ref, right_ref, out_ref):
    step = 32

    def some(at, carry):
        rows = pl.ds(pl.multiple_of(at * step, step), step)
        out_ref[rows, :] = (
            left_ref[rows, :].astype(f32) + right_ref[rows, :].astype(f32)
        ).astype(bf16)
        return carry

    lax.fori_loop(0, out_ref.shape[0] // step, some, 0, unroll=2)


def add_low(left, right):
    return call(add_rows, shaped(*left.shape), left, right, name="add_rows")


def on_device(
    tokens, positions, doc_ids, block_ids, entry_gain, query_weight, key_weight, value_weight,
    output_weight, attend_gain, middle_gain, gate_weight, up_weight, down_weight, closing_gain,
    cotangent,
):
    place = lax.axis_index("seq")
    order = [place ^ step for step in range(SEQ)]
    here = jnp.reshape(place, (1,)).astype(jnp.int32)
    rows, model = tokens.shape
    window = rows * SEQ
    shard = query_weight.shape[0]
    wt = model // shard
    part = model // SEQ
    width = model // HEADS
    heads = HEADS // SEQ
    hidden = gate_weight.shape[1]
    chunk = hidden // (wt * SEQ)
    padded = (chunk + 15) // 16 * 16
    hidden_part = padded * wt
    piece = 256

    def gather_blocks(own):
        far = swap(own, 2)
        near = swap(own, 1)
        return own, near, far, swap(far, 1)

    lines = wt == 8
    first_own = call(
        pack_first, shaped(shard + GAIN_ROWS, model),
        here, query_weight, key_weight, value_weight, output_weight,
        *(gain[None] for gain in (entry_gain, attend_gain, middle_gain, closing_gain)),
        smem=1, name="pack_first",
    )
    gate_up_own, down_own = call(
        pack_feed, (shaped(shard, 2 * hidden_part), shaped(padded, model)),
        here, gate_weight, up_weight, after(down_weight, first_own), smem=1, name="pack_feed",
    )
    mine = lax.axis_index("wt")
    level = mine // 2
    xside = mine % 2

    def numbers(*values):
        return jnp.stack([jnp.asarray(value, jnp.int32) for value in values])

    if lines:
        around = numbers(level ^ 1, level ^ 2, level ^ 3)
        whose = numbers(
            *[2 * at + xside for at in range(4)],
            *[2 * (level ^ at) + 1 - xside for at in range(4)],
        )
        first_z = gather_levels(first_own, wt)
        gate_up_z = gather_levels(gate_up_own, wt)
        first_x = across(first_own, wt)
        gate_up_x = across(gate_up_own, wt)
        down_x = across(down_own, wt)
        down_pair = jnp.where(
            xside == 0, jnp.stack([down_own, down_x]), jnp.stack([down_x, down_own])
        )
        down_part = gather_levels(down_pair, wt).reshape(hidden_part, model)
    else:
        whose = jnp.arange(wt, dtype=jnp.int32)
        first_z = lax.all_gather(first_own, "wt", axis=0, tiled=False)
        gate_up_z = lax.all_gather(gate_up_own, "wt", axis=0, tiled=False)
        down_part = lax.all_gather(down_own, "wt", axis=0, tiled=True)
    token_blocks = gather_blocks(tokens)
    cotangent_far = swap(after(cotangent, token_blocks[2]), 2)

    offsets = jnp.arange(window, dtype=jnp.int32)
    leading = doc_ids == doc_ids[0]
    boundary = jnp.sum(leading.astype(jnp.int32))
    places = jnp.where(leading, DOC_LEN - boundary + offsets, offsets - boundary)
    codes = doc_ids * DOC_STRIDE + block_ids
    lows = doc_ids * DOC_STRIDE
    packed = jnp.stack([places, codes, lows]).reshape(3, SEQ, rows)
    packed = jnp.concatenate(
        [lax.dynamic_index_in_dim(packed, at, 1, keepdims=False) for at in order], 1
    )
    half = width // 2
    frequency = ROTARY_BASE ** (-2.0 * jnp.arange(half, dtype=f32) / width)
    angles = packed[0].astype(f32)[:, None] * frequency[None, :]
    cosine = jnp.cos(angles)
    sine = jnp.sin(angles)
    cosine = jnp.concatenate([cosine, cosine], 1)
    sine = jnp.concatenate([-sine, sine], 1)
    query_code = jnp.broadcast_to(
        packed[1:3].astype(f32).reshape(2, SEQ, rows).transpose(1, 0, 2)[:, :, None, :], (SEQ, 2, 4, rows)
    ).transpose(0, 2, 1, 3).reshape(SEQ, 8, rows)

    waited = (cosine, sine, query_code, *token_blocks, cotangent_far)
    if lines:
        first_z = after(first_z, *waited, first_x, gate_up_x, down_pair)
        rest = call(
            others, shaped(3, shard + GAIN_ROWS, model), around, first_z, smem=1, name="others",
        )
        firsts = (first_z, first_x[None], across(rest, wt))
    else:
        firsts = (after(first_z, *waited),)
    output_own, gains = call(
        output_and_gains, (shaped(model, part), shaped(8, model, dtype=f32)),
        whose, *firsts, smem=1, name="output_and_gains",
    )
    entry_full, attend_full, middle_full, closing_full = [gains[at:at + 1] for at in range(4)]
    low_shape = shaped(window, heads * width)
    pair_cost = 2 * heads * window * window * width
    entry_low, query_low, key_low, value_low, attended, log_totals, qkv_weight = call(
        attend_forward,
        (shaped(window, model), low_shape, low_shape, low_shape, low_shape,
         shaped(heads, SEQ, 8, rows, dtype=f32), shaped(model, 3 * part)),
        whose, entry_full, cosine, sine, query_code, *token_blocks,
        after(firsts[0], output_own), *firsts[1:], smem=1,
        scratch=(
            pltpu.VMEM((window, model), bf16),
            pltpu.VMEM((window, 128), f32),
        ),
        name="attend_forward",
    )
    attended_own = attended
    if lines:
        gate_up_z = after(gate_up_z, attended)
        rest = call(
            others, shaped(3, shard, 2 * hidden_part), around, gate_up_z, smem=1, name="others",
        )
        attended, rest = lax.optimization_barrier((attended, rest))
        gate_ups = (gate_up_z, gate_up_x[None], across(rest, wt))
    else:
        gate_ups = (gate_up_z,)
    output_far = after(swap(output_own, 2), attended)
    output_rows = call(
        arrange, shaped(model, model),
        here, output_own, swap(output_own, 1), output_far, swap(output_far, 1), smem=1,
        name="arrange",
    )

    gate_up = call(
        assemble, shaped(model, 2 * hidden_part), whose, *gate_ups, smem=1, name="assemble",
    )

    def exchange(blocks):
        return [blocks[0], swap(blocks[1], 1), swap(blocks[2], 2), swap(blocks[3], 3)]

    joined = exchange([attended[at * rows:(at + 1) * rows] for at in range(SEQ)])
    joined = [joined[0], joined[1]] + [after(got, output_rows) for got in joined[2:]]
    inputs = tokens.astype(f32)
    mixed = dot(jnp.concatenate(joined, 1), output_rows)
    attend_normed, attend_inverse = normed_of(mixed)
    hidden_state = inputs + attend_normed * attend_full
    middle_normed, middle_inverse = normed_of(hidden_state)
    middle_low = (middle_normed * middle_full).astype(bf16)

    full = shaped(rows, model, dtype=f32)
    both_shape = shaped(2 * rows, 2 * hidden_part)

    def forward(first_rows, second_rows):
        return call(
            feed_forward, (both_shape, shaped(2 * rows, hidden_part), full, shaped(rows, model)),
            first_rows, second_rows, gate_up, down_part, name="feed_forward",
        )

    def backward(first_rows, second_rows, both):
        return call(
            feed_backward, (both_shape, full, shaped(rows, model)),
            first_rows, second_rows, both, gate_up, down_part, name="feed_backward",
        )

    def chip_sum(values, weights, product):
        second = product(values[rows:], weights).astype(bf16)
        return product(values[:rows], weights) + swap(second, 1).astype(f32)

    middle_far = swap(middle_low, 2)
    middle_near = swap(middle_low, 1)
    fed_near = forward(middle_low, middle_near)
    middle_far = after(middle_far, fed_near[0])
    channel_near = fed_near[2] + swap(fed_near[3], 1).astype(f32)
    channel_send = channel_near.astype(bf16)
    far_other = swap(channel_send, 2)
    middle_both = after(swap(middle_far, 1), channel_send)
    fed_far = forward(middle_far, middle_both)
    far_other = after(far_other, fed_far[0])
    channel_far = fed_far[2] + swap(fed_far[3], 1).astype(f32)
    near_other = swap(channel_far.astype(bf16), 2)

    def close(channel_out, cotangents):
        normed, inverse = normed_of(channel_out)
        back = norm_back(cotangents.astype(f32), normed, inverse, closing_full)
        return normed, back.astype(bf16)

    _, low_far = close(channel_far + far_other.astype(f32), cotangent_far)
    low_both = swap(low_far, 1)
    back_far = backward(low_far, low_both, fed_far[0])
    near_other = after(near_other, back_far[0])
    middle_send = (back_far[1] + swap(back_far[2], 1).astype(f32)).astype(bf16)
    far_got = swap(middle_send, 2)
    closing_normed, channel_low = close(
        channel_near + after(near_other, middle_send).astype(f32), cotangent
    )
    layer_output = (hidden_state + closing_normed * closing_full).astype(bf16)
    incoming = cotangent.astype(f32)
    closing_sum = jnp.sum(incoming * closing_normed, 0)
    low_near = swap(channel_low, 1)
    down_shape = shaped(hidden_part // 2, model)
    side = jnp.reshape(lax.axis_index("wt") % 2, (1,)).astype(jnp.int32)
    down_keep, down_send = call(
        functools.partial(down_weights, padded=padded), (down_shape, down_shape),
        side, channel_low, low_near, low_far, low_both, fed_near[1], fed_far[1], smem=1,
        scratch=(pltpu.VMEM((hidden_part, model), bf16),), name="down_weights",
    )
    down_got = across(down_send, wt)
    back_near = backward(channel_low, after(low_near, down_keep), fed_near[0])
    near_got = swap(back_near[2], 1)
    gate_shape = shaped(model // 2, hidden_part)
    gate_keep, gate_send, up_keep, up_send = call(
        functools.partial(feed_weights, shard=shard),
        (gate_shape,) * 4, side, middle_low, middle_near, middle_far, middle_both,
        after(back_near[0], near_got), back_far[0], smem=1,
        scratch=(pltpu.VMEM((model, 2 * hidden_part), bf16),), name="feed_weights",
    )
    gate_got = across(gate_send, wt)
    up_got = across(up_send, wt)
    far_got = after(far_got, gate_keep)
    down_sum = add_low(down_keep, after(down_got, far_got))
    down_share = scatter_levels(down_sum, wt)
    row_block = pl.BlockSpec((rows // 4, model), lambda step: (step, 0))

    def fixed(*shape):
        return pl.BlockSpec(shape, lambda step: (0, 0))

    hidden_grad, mixed_low, middle_sums, *attended_grads = pl.pallas_call(
        middle_backward,
        grid=(4,),
        out_shape=(full, shaped(rows, model), shaped(16, model, dtype=f32))
        + (shaped(rows, part),) * SEQ,
        in_specs=[row_block] * 6 + [fixed(8, model), fixed(model, model)],
        out_specs=(row_block, row_block, fixed(16, model)) + (fixed(rows, part),) * SEQ,
        scratch_shapes=[pltpu.VMEM((rows, model), bf16)],
        compiler_params=pltpu.CompilerParams(
            vmem_limit_bytes=GRANTS.get("middle_backward", 56) * 1024 * 1024
        ),
        cost_estimate=pl.CostEstimate(
            flops=int(COSTS["middle_backward"] * 1.15e9), transcendentals=0, bytes_accessed=0
        ),
        name="middle_backward",
    )(
        back_near[1], near_got, after(far_got, down_sum), hidden_state, mixed, cotangent, gains,
        output_rows,
    )
    attended_back = exchange(attended_grads)
    output_grads = call(
        output_weights,
        (shaped(model, part, dtype=f32), shaped(model, part), shaped(model, part, dtype=f32),
         shaped(model, part)),
        here, after(mixed_low, *attended_back[1:]), *joined, smem=1,
        name="output_weights",
    )
    output_far = (output_grads[2] + swap(output_grads[3], 1).astype(f32)).astype(bf16)
    output_near = swap(output_grads[1], 1)
    output_far = after(output_far, *attended_back)
    gate_sum = add_low(gate_keep, after(gate_got, *attended_back[1:]))
    gate_share = scatter_levels(gate_sum, wt)
    attended_back[0] = after(attended_back[0], output_far, gate_sum)
    output_got = swap(output_far, 2)
    qkv_grad = call(
        attend_backward, shaped(window, 3 * part),
        query_low, key_low, value_low, attended_own, log_totals, cosine, sine, query_code,
        *attended_back,
        scratch=(
            pltpu.VMEM((heads, window, width), f32), pltpu.VMEM((heads, window, width), f32),
            pltpu.VMEM((window, heads * width), bf16), pltpu.VMEM((window, 128), f32),
        ),
        name="attend_backward",
    )
    levels = range(0, wt, 2)
    whose = numbers(*[at + xside for at in levels], *[at + 1 - xside for at in levels])
    last_shape = shaped(wt // 2 * (shard + GAIN_ROWS), model)
    last_keep, last_send = call(
        last_weights, (last_shape, last_shape),
        whose, entry_low, qkv_grad, output_grads[0], output_near, after(output_got, qkv_grad), middle_sums,
        closing_sum[None],
        smem=1, scratch=(pltpu.VMEM((model, model), bf16), pltpu.VMEM((wt, GAIN_ROWS, model), bf16)),
        name="last_weights",
    )
    up_sum = add_low(up_keep, after(up_got, down_share, last_send))
    up_share = scatter_levels(up_sum, wt)
    qkv_grad = after(qkv_grad, last_send, up_sum)

    entry_far = chip_sum(qkv_grad[2 * rows:], qkv_weight, dot_nt).astype(bf16)
    entry_near = chip_sum(after(qkv_grad[:2 * rows], entry_far), qkv_weight, dot_nt)
    share = call(
        join_shares, shaped((2 * hidden_part * shard + model * padded) // piece, piece),
        after(gate_share, entry_near), up_share, down_share, name="join_shares",
    )
    entry_got = swap(entry_far, 2)
    last_got = after(across(last_send, wt), gate_share, up_sum, entry_near, share, entry_got)
    last_sum = add_low(last_keep, last_got)
    last_share = scatter_levels(last_sum, wt)
    entry_grad = entry_near + after(entry_got, last_sum).astype(f32)
    entry_normed, entry_inverse = normed_of(inputs)
    input_grad = hidden_grad + norm_back(entry_grad, entry_normed, entry_inverse, entry_full)
    share_far = after(swap(share, 2), input_grad)
    share_got = (share, swap(share, 1), share_far, swap(share_far, 1))
    grad_gate, grad_up, grad_down = call(
        functools.partial(unpack_feed, shard=shard, padded=padded),
        (shaped(shard, hidden, dtype=f32), shaped(shard, hidden, dtype=f32),
         shaped(SEQ * chunk, model, dtype=f32)),
        here, *share_got, smem=1, name="unpack_feed",
    )
    last_got = gather_blocks(after(last_share, grad_down))
    weight_shape = shaped(shard, model, dtype=f32)
    grad_query, grad_key, grad_value, grad_output, *grad_gains = call(
        functools.partial(unpack_last, shard=shard),
        (weight_shape,) * 4
        + (shaped(1, shard, dtype=f32),) * 4,
        here, last_share, last_got[1], last_got[2],
        last_got[3], entry_gain[None], query_weight, key_weight, value_weight, smem=1,
        name="unpack_last",
    )
    grad_entry, grad_attend, grad_middle, grad_closing = [gain[0] for gain in grad_gains]
    return (
        layer_output, input_grad, grad_entry, grad_query, grad_key, grad_value, grad_output,
        grad_attend, grad_middle, grad_gate, grad_up, grad_down, grad_closing,
    )


def solution(mesh):
    rows = P(("wt", "seq"), None)
    weight = P("wt", None)
    gain = P("wt")
    return jax.shard_map(
        on_device,
        mesh=mesh,
        in_specs=(
            rows, P(("wt", "seq")), gain, gain, gain, weight, weight, weight, weight, gain, gain,
            weight, weight, weight, gain, rows,
        ),
        out_specs=(
            rows, rows, gain, weight, weight, weight, weight, gain, gain, weight, weight, weight,
            gain,
        ),
        check_vma=False,
    )
```

```python
import functools

import jax
import jax.numpy as jnp
from jax import lax
from jax.experimental import pallas as pl
from jax.experimental.pallas import tpu as pltpu
from jax.sharding import PartitionSpec as P

HEADS = 8
EPSILON = 1e-06
ROTARY_BASE = 50000.0
DOC_LEN = 8192
DOC_STRIDE = 64
HIDDEN_LOW = -1e30
LOG2_E = 1.4426950408889634
SEQ = 4
GAIN_ROWS = 8
GRANTS = dict(
    entry_backward=24,
    join_shares=8,
    unpack_feed=32,
    arrange=16,
    output_and_gains=16,
    unpack_last=16,
    last_weights=24,
    feed_forward=16,
    feed_backward=16,
    down_weights=16,
    feed_weights=24,
    add_rows=8,
    middle_backward=56,
    assemble=16,
    output_weights=16,
    others=16,
)
COSTS = dict(
    add_late=0.002,
    entry_backward=0.004,
    pack_first=0.004,
    pack_feed=0.008,
    assemble=0.008,
    attend_forward=0.03,
    arrange=0.006,
    feed_weights=0.016,
    down_weights=0.008,
    feed_forward=0.012,
    feed_backward=0.014,
    output_weights=0.006,
    attend_backward=0.028,
    last_weights=0.012,
    join_shares=0.004,
    middle_backward=0.008,
    add_rows=0.002,
    others=0.002,
    output_and_gains=0.002,
    assemble_part=0.002,
    unpack_feed=0.018000000000000002,
    unpack_last=0.006,
)

f32 = jnp.float32
bf16 = jnp.bfloat16


def dot(left, right):
    return jnp.dot(left, right, preferred_element_type=f32)


def dot_nt(left, right):
    return lax.dot_general(left, right, (((1,), (1,)), ((), ())), preferred_element_type=f32)


def dot_tn(left, right):
    return lax.dot_general(left, right, (((0,), (0,)), ((), ())), preferred_element_type=f32)


def normed_of(values):
    inverse = lax.rsqrt(jnp.mean(values * values, -1, keepdims=True) + EPSILON)
    return values * inverse, inverse


def norm_back(incoming, normed, inverse, scales):
    scaled = incoming * scales
    return inverse * (scaled - normed * jnp.mean(scaled * normed, -1, keepdims=True))


def call(kernel, outs, *args, smem=0, scratch=(), name=None):
    many = isinstance(outs, (list, tuple))
    whole = pl.BlockSpec(memory_space=pltpu.VMEM)
    return pl.pallas_call(
        kernel,
        out_shape=tuple(outs) if many else outs,
        in_specs=[
            pl.BlockSpec(memory_space=pltpu.SMEM) if at < smem else whole
            for at in range(len(args))
        ],
        out_specs=(whole,) * len(outs) if many else whole,
        scratch_shapes=list(scratch),
        compiler_params=pltpu.CompilerParams(vmem_limit_bytes=GRANTS.get(name, 56) * 1024 * 1024),
        cost_estimate=pl.CostEstimate(flops=int(COSTS[name] * 1.15e9), transcendentals=0, bytes_accessed=0),
        name=name,
    )(*args)


def shaped(*shape, dtype=bf16):
    return jax.ShapeDtypeStruct(shape, dtype)


def after(value, *others):
    return lax.optimization_barrier((value,) + others)[0]


def swap(value, bit):
    return lax.ppermute(value, "seq", [(i, i ^ bit) for i in range(SEQ)])


def chosen(rows, columns, chunk, padded, place):
    row = lax.broadcasted_iota(jnp.int32, (rows, columns), 0)
    column = lax.broadcasted_iota(jnp.int32, (rows, columns), 1)
    block = column // padded
    inside = column - block * padded
    wanted = block * (SEQ * chunk) + place * chunk + inside
    return jnp.where((row == wanted) & (inside < chunk), 1.0, 0.0).astype(bf16)


def pack_first(place_ref, query_ref, key_ref, value_ref, output_ref, *refs):
    gain_refs, out_ref = refs[:4], refs[4]
    shard, model = query_ref.shape
    part = model // SEQ
    columns = pl.ds(pl.multiple_of(place_ref[0] * part, part), part)
    for at, ref in enumerate((query_ref, key_ref, value_ref, output_ref)):
        out_ref[:shard, at * part:(at + 1) * part] = ref[:, columns]
    out_ref[shard:, :] = jnp.zeros((GAIN_ROWS, model), bf16)
    for at, ref in enumerate(gain_refs):
        out_ref[shard:shard + 1, at * shard:(at + 1) * shard] = ref[...]


def pack_feed(place_ref, gate_ref, up_ref, down_ref, out_ref, down_out_ref):
    place = place_ref[0]
    wide = gate_ref.shape[1] // 2
    narrow = out_ref.shape[1] // 4
    chunk = down_ref.shape[0] // SEQ
    padded = down_out_ref.shape[0]
    pick = chosen(wide, narrow, chunk, padded, place)
    for number, ref in enumerate((gate_ref, up_ref)):
        for half in range(2):
            at = (2 * number + half) * narrow
            out_ref[:, at:at + narrow] = dot(
                ref[:, half * wide:(half + 1) * wide], pick
            ).astype(bf16)
    pick_rows = chosen(SEQ * chunk, padded, chunk, padded, place)
    down_out_ref[...] = dot_tn(pick_rows, down_ref[...]).astype(bf16)


def blocks_of(at_ref, refs):
    step = 0
    for ref in refs:
        for at in range(ref.shape[0]):
            yield at_ref[step], ref.at[at]
            step += 1


def assemble(at_ref, *refs):
    out_ref = refs[-1]
    rows = refs[0].shape[1]
    for at, block in blocks_of(at_ref, refs[:-1]):
        out_ref[pl.ds(pl.multiple_of(at * rows, rows), rows), :] = block[...]


def others(at_ref, ref, out_ref):
    for step in range(out_ref.shape[0]):
        out_ref[step] = ref[at_ref[step]]


def output_and_gains(at_ref, *refs):
    refs, (output_ref, gain_ref) = refs[:-2], refs[-2:]
    shard = refs[0].shape[1] - GAIN_ROWS
    part = output_ref.shape[1]
    for step, (at, block) in enumerate(blocks_of(at_ref, refs)):
        rows = pl.ds(pl.multiple_of(at * shard, shard), shard)
        output_ref[rows, :] = block[:shard, 3 * part:]
        if shard % 128:
            columns = pl.ds(step * shard, shard)
        else:
            columns = pl.ds(pl.multiple_of(at * shard, shard), shard)
        for number in range(4):
            gain_ref[number:number + 1, columns] = block[
                shard:shard + 1, number * shard:(number + 1) * shard
            ].astype(f32)


def join_shares(gate_ref, up_ref, down_ref, out_ref):
    piece = out_ref.shape[1]
    row = 0
    for ref in (gate_ref, up_ref, down_ref):
        for at in range(0, ref.shape[1], piece):
            out_ref[row:row + ref.shape[0], :] = ref[:, at:at + piece]
            row += ref.shape[0]


def unpack_feed(place_ref, *refs, shard, padded):
    blocks, (gate_ref, up_ref, down_ref) = refs[:SEQ], refs[SEQ:]
    place = place_ref[0]
    chunk = down_ref.shape[0] // SEQ
    model = down_ref.shape[1]
    piece = blocks[0].shape[1]
    wide = gate_ref.shape[1] // 2
    below = blocks[0].shape[0] - model // piece * padded
    pieces = below // shard // 2
    narrow = pieces * piece // 2
    pick = jnp.concatenate(
        [chosen(wide, narrow, chunk, padded, place ^ at) for at in range(SEQ)], 1
    )
    for number, out_ref in enumerate((gate_ref, up_ref)):
        joined = [
            jnp.concatenate(
                [
                    ref[(number * pieces + at) * shard:(number * pieces + at + 1) * shard, :]
                    for at in range(pieces)
                ], 1,
            )
            for ref in blocks
        ]
        for half in range(2):
            parts = [part[:, half * narrow:(half + 1) * narrow] for part in joined]
            out_ref[:, half * wide:(half + 1) * wide] = dot_nt(jnp.concatenate(parts, 1), pick)
    rows = jnp.concatenate(
        [chosen(SEQ * chunk, padded, chunk, padded, place ^ at) for at in range(SEQ)], 1
    )
    for at in range(model // piece):
        parts = [ref[below + at * padded:below + (at + 1) * padded, :] for ref in blocks]
        down_ref[:, at * piece:(at + 1) * piece] = dot(rows, jnp.concatenate(parts, 0))


def unpack_last(place_ref, *refs, shard):
    blocks, (gain_ref, *weights), outs = refs[:SEQ], refs[SEQ:SEQ + 4], refs[SEQ + 4:]
    place = place_ref[0]
    part = blocks[0].shape[1] // SEQ
    for step, block in enumerate(blocks):
        columns = pl.ds(pl.multiple_of((place ^ step) * part, part), part)
        for at in range(4):
            outs[at][:, columns] = block[:shard, at * part:(at + 1) * part].astype(f32)
    sums = sum(block[shard:, :].astype(f32) for block in blocks)
    for at, ref in enumerate(outs[5:]):
        ref[...] = sums[0:1, at * shard:(at + 1) * shard]
    total = sum(
        jnp.sum(ref[...].astype(f32) * out[...], 1, keepdims=True)
        for ref, out in zip(weights, outs[:3])
    )
    outs[4][...] = total.T / gain_ref[...].astype(f32)


def arrange(place_ref, *refs):
    blocks, out_ref = refs[:SEQ], refs[SEQ]
    place = place_ref[0]
    part = blocks[0].shape[1]
    for step in range(SEQ):
        rows = pl.ds(pl.multiple_of((place ^ step) * part, part), part)
        for other in range(SEQ):
            columns = pl.ds(pl.multiple_of((place ^ other) * part, part), part)
            out_ref[step * part:(step + 1) * part, columns] = blocks[other][rows, :]


def turn(rows, cosine, sine):
    return rows * cosine + pltpu.roll(rows, rows.shape[-1] // 2, axis=1) * sine


def visible(key_code, query_code, tile):
    key_wide = jnp.concatenate([key_code] * (tile // 128), axis=1)
    return (key_wide <= query_code[0:1, :]) & (key_wide >= query_code[1:2, :])


def key_codes(query_code_ref, key_code_ref):
    tiles, _, tile = query_code_ref.shape
    for step in range(tiles):
        wide = jnp.broadcast_to(query_code_ref[step, 0:1, :], (128, tile))
        key_code_ref[step * tile:(step + 1) * tile, :] = wide.T


def attend_forward(
    at_ref, gain_ref, cos_ref, sin_ref, query_code_ref, own_ref, near_ref, far_ref, both_ref,
    *refs,
):
    firsts, refs = refs[:-9], refs[-9:]
    low_ref, query_ref, key_ref, value_ref, out_ref, log_ref, weight_ref, token_ref, key_code_ref = refs
    window, model = low_ref.shape
    shard = firsts[0].shape[1] - GAIN_ROWS
    tiles, _, tile = query_code_ref.shape
    width = cos_ref.shape[1]
    heads = query_ref.shape[1] // width
    scale = LOG2_E * width ** (-0.5)
    for at, block in blocks_of(at_ref, firsts):
        rows = pl.ds(pl.multiple_of(at * shard, shard), shard)
        weight_ref[rows, :] = block[:shard, :3 * heads * width]
    for step, ref in enumerate((own_ref, near_ref, far_ref, both_ref)):
        token_ref[step * tile:(step + 1) * tile, :] = ref[...]
    key_codes(query_code_ref, key_code_ref)

    def project(step, carry):
        rows = pl.ds(pl.multiple_of(step * tile, tile), tile)
        normed, _ = normed_of(token_ref[rows, :].astype(f32))
        low = (normed * gain_ref[0:1, :]).astype(bf16)
        low_ref[rows, :] = low
        raw = dot(low, weight_ref[...])
        cosine = cos_ref[rows, :]
        sine = sin_ref[rows, :]
        for head in range(heads):
            at = head * width
            query_ref[rows, at:at + width] = turn(raw[:, at:at + width], cosine, sine).astype(bf16)
            at = (heads + head) * width
            key_ref[rows, head * width:(head + 1) * width] = turn(
                raw[:, at:at + width], cosine, sine
            ).astype(bf16)
        value_ref[rows, :] = raw[:, 2 * heads * width:].astype(bf16)
        return carry

    lax.fori_loop(0, window // tile, project, 0)
    turned = [
        value_ref[:, head * width:(head + 1) * width].astype(f32).T.astype(bf16)
        for head in range(heads)
    ]

    def one_tile(step, carry):
        rows = pl.ds(pl.multiple_of(step * tile, tile), tile)
        shown = visible(key_code_ref[...], query_code_ref[step], tile)
        for head in range(heads):
            cols = slice(head * width, (head + 1) * width)
            scores = dot_nt(key_ref[:, cols], query_ref[rows, cols])
            scores = jnp.where(shown, scores * scale, HIDDEN_LOW)
            top = jnp.max(scores, 0, keepdims=True)
            weights = jnp.exp2(scores - top)
            total = jnp.sum(weights, 0, keepdims=True)
            result = dot(turned[head], weights.astype(bf16)) * (1.0 / total)
            out_ref[rows, cols] = result.T.astype(bf16)
            log_ref[head, step] = jnp.broadcast_to(top + jnp.log2(total), (8, tile))
        return carry

    lax.fori_loop(0, tiles, one_tile, 0)


def attend_backward(
    query_ref, key_ref, value_ref, out_ref, log_ref, cos_ref, sin_ref, query_code_ref, *refs,
):
    incoming_refs, (grad_ref, *scratch) = refs[:SEQ], refs[SEQ:]
    key_sum, value_sum, incoming_ref, key_code_ref = scratch
    key_codes(query_code_ref, key_code_ref)
    tiles, _, tile = query_code_ref.shape
    width = cos_ref.shape[1]
    heads = query_ref.shape[1] // width
    factor = width ** (-0.5)
    scale = LOG2_E * factor
    for step, ref in enumerate(incoming_refs):
        incoming_ref[step * tile:(step + 1) * tile, :] = ref[...]
    turned = [
        key_ref[:, head * width:(head + 1) * width].astype(f32).T.astype(bf16)
        for head in range(heads)
    ]
    key_sum[...] = jnp.zeros_like(key_sum)
    value_sum[...] = jnp.zeros_like(value_sum)

    def one_tile(step, carry):
        rows = pl.ds(pl.multiple_of(step * tile, tile), tile)
        shown = visible(key_code_ref[...], query_code_ref[step], tile)
        for head in range(heads):
            cols = slice(head * width, (head + 1) * width)
            queries = query_ref[rows, cols]
            incoming = incoming_ref[rows, cols]
            products = incoming.astype(f32) * out_ref[rows, cols].astype(f32)
            inner = jnp.sum(products.T, 0, keepdims=True)
            scores = dot_nt(key_ref[:, cols], queries)
            probs = jnp.where(shown, jnp.exp2(scores * scale - log_ref[head, step, 0:1, :]), 0.0)
            value_sum[head] += dot(probs.astype(bf16), incoming)
            prob_grad = dot_nt(value_ref[:, cols], incoming)
            score_grad = (probs * (prob_grad - inner)).astype(bf16)
            key_sum[head] += dot(score_grad, queries)
            query_grad = (dot(turned[head], score_grad) * factor).T
            grad_ref[rows, cols] = turn(query_grad, cos_ref[rows, :], -sin_ref[rows, :]).astype(bf16)
        return carry

    lax.fori_loop(0, tiles, one_tile, 0)
    for head in range(heads):
        at = (heads + head) * width
        grad_ref[:, at:at + width] = turn(
            key_sum[head] * factor, cos_ref[...], -sin_ref[...]
        ).astype(bf16)
        at = (2 * heads + head) * width
        grad_ref[:, at:at + width] = value_sum[head].astype(bf16)


def feed_forward(
    first_ref, second_ref, weight_ref, down_ref, both_ref, active_ref, keep_ref, send_ref,
):
    rows, model = first_ref.shape
    half = down_ref.shape[0]
    low = jnp.concatenate([first_ref[...], second_ref[...]], 0)
    step = 256
    for at in range(0, half, step):
        gate_value = dot(low, weight_ref[:, at:at + step])
        up_value = dot(low, weight_ref[:, half + at:half + at + step])
        both_ref[:, at:at + step] = gate_value.astype(bf16)
        both_ref[:, half + at:half + at + step] = up_value.astype(bf16)
        active_ref[:, at:at + step] = (gate_value * jax.nn.sigmoid(gate_value) * up_value).astype(
            bf16
        )
    for at in range(0, model, step):
        total = dot(active_ref[...], down_ref[:, at:at + step])
        keep_ref[:, at:at + step] = total[:rows]
        send_ref[:, at:at + step] = total[rows:].astype(bf16)


def feed_backward(
    first_ref, second_ref, both_ref, weight_ref, down_ref, grad_ref, keep_ref, send_ref,
):
    rows, model = first_ref.shape
    half = down_ref.shape[0]
    low = jnp.concatenate([first_ref[...], second_ref[...]], 0)
    step = 256
    for at in range(0, half, step):
        active_grad = dot_nt(low, down_ref[at:at + step, :])
        gate_value = both_ref[:, at:at + step].astype(f32)
        up_value = both_ref[:, half + at:half + at + step].astype(f32)
        share = jax.nn.sigmoid(gate_value)
        scaled = active_grad * share
        grad_ref[:, at:at + step] = (
            scaled * up_value * (1.0 + gate_value * (1.0 - share))
        ).astype(bf16)
        grad_ref[:, half + at:half + at + step] = (scaled * gate_value).astype(bf16)
    for at in range(0, model, step):
        total = dot_nt(grad_ref[...], weight_ref[at:at + step, :])
        keep_ref[:, at:at + step] = total[:rows]
        send_ref[:, at:at + step] = total[rows:].astype(bf16)


def halves_out(side, full, shard, columns, keep_ref, send_ref):
    for level in range(full.shape[0] // shard // 2):
        to = slice(level * shard, (level + 1) * shard)
        for at, ref in ((2 * level + side, keep_ref), (2 * level + 1 - side, send_ref)):
            rows = pl.ds(pl.multiple_of(at * shard, shard), shard)
            ref[to, :] = full[rows, columns]


def feed_weights(
    side_ref, own_ref, near_ref, far_ref, both_ref, near_grad, far_grad,
    gate_keep, gate_send, up_keep, up_send, full, *, shard,
):
    low = jnp.concatenate([own_ref[...], near_ref[...], far_ref[...], both_ref[...]], 0)
    grad = jnp.concatenate([near_grad[...], far_grad[...]], 0)
    full[...] = dot_tn(low, grad).astype(bf16)
    half = gate_keep.shape[1]
    side = side_ref[0]
    halves_out(side, full, shard, slice(0, half), gate_keep, gate_send)
    halves_out(side, full, shard, slice(half, 2 * half), up_keep, up_send)


def down_weights(
    side_ref, own_ref, near_ref, far_ref, both_ref, near_active, far_active, keep_ref, send_ref,
    full, *, padded,
):
    grad = jnp.concatenate([own_ref[...], near_ref[...], far_ref[...], both_ref[...]], 0)
    active = jnp.concatenate([near_active[...], far_active[...]], 0)
    full[...] = dot_tn(active, grad).astype(bf16)
    halves_out(side_ref[0], full, padded, slice(None), keep_ref, send_ref)


def folded(values):
    return jnp.sum(values.reshape(-1, 8, values.shape[-1]), 0)


def middle_backward(
    keep_ref, near_ref, far_ref, hidden_ref, mixed_ref, incoming_ref, gain_ref, weight_ref,
    grad_ref, low_ref, sum_ref, *outs,
):
    step = pl.program_id(0)
    rows = keep_ref.shape[0]
    *outs, all_low = outs
    middle_grad = keep_ref[...] + near_ref[...].astype(f32) + far_ref[...].astype(f32)
    normed, inverse = normed_of(hidden_ref[...])
    grad = incoming_ref[...].astype(f32) + norm_back(
        middle_grad, normed, inverse, gain_ref[2:3, :]
    )
    grad_ref[...] = grad
    middle_sum = folded(middle_grad * normed)
    normed, inverse = normed_of(mixed_ref[...])
    low = norm_back(grad, normed, inverse, gain_ref[1:2, :]).astype(bf16)
    low_ref[...] = low
    all_low[pl.ds(pl.multiple_of(step * rows, rows), rows), :] = low

    @pl.when(step == 0)
    def _():
        sum_ref[...] = jnp.zeros_like(sum_ref)

    sum_ref[0:8, :] += folded(grad * normed)
    sum_ref[8:16, :] += middle_sum

    @pl.when(step == pl.num_programs(0) - 1)
    def _():
        size = outs[0].shape[1]
        for at, ref in enumerate(outs):
            ref[...] = dot_nt(all_low[...], weight_ref[at * size:(at + 1) * size, :]).astype(bf16)


def output_weights(place_ref, low_ref, *refs):
    pieces, outs = refs[:SEQ], refs[SEQ:]
    place = place_ref[0]
    part = outs[0].shape[1]
    for step in range(SEQ):
        columns = pl.ds(pl.multiple_of((place ^ step) * part, part), part)
        for other in range(SEQ):
            rows = pl.ds(pl.multiple_of((place ^ other) * part, part), part)
            outs[step][rows, :] = dot_tn(pieces[other][...], low_ref[:, columns]).astype(
                outs[step].dtype
            )


def last_weights(
    at_ref, low_ref, grad_ref, keep_ref, near_ref, far_ref, middle_ref, closing_ref, *refs
):
    outs, full, sum_ref = refs[:2], refs[2], refs[3]
    wt = at_ref.shape[0]
    model = outs[0].shape[1]
    total = outs[0].shape[0] // (wt // 2)
    shard = total - GAIN_ROWS
    part = keep_ref.shape[1]
    full[:, :3 * part] = dot_tn(low_ref[...], grad_ref[...]).astype(bf16)
    full[:, 3 * part:] = (
        keep_ref[...] + near_ref[...].astype(f32) + far_ref[...].astype(f32)
    ).astype(bf16)
    sums = (
        jnp.sum(middle_ref[:8, :], 0, keepdims=True), jnp.sum(middle_ref[8:, :], 0, keepdims=True),
        closing_ref[...],
    )
    sum_ref[...] = jnp.zeros_like(sum_ref)
    for at in range(wt):
        for number, total_row in enumerate(sums):
            sum_ref[at, 0:1, number * shard:(number + 1) * shard] = total_row[
                :, at * shard:(at + 1) * shard
            ].astype(bf16)
    for number, ref in enumerate(outs):
        for step in range(wt // 2):
            at = at_ref[number * (wt // 2) + step]
            row = step * total
            ref[row:row + shard, :] = full[pl.ds(pl.multiple_of(at * shard, shard), shard), :]
            ref[row + shard:row + total, :] = sum_ref[at]


def entry_backward(grad_ref, weight_ref, *outs):
    rows = outs[0].shape[0]
    for at, ref in zip((3, 2, 1, 0), outs):
        ref[...] = dot_nt(grad_ref[at * rows:(at + 1) * rows, :], weight_ref[...]).astype(ref.dtype)


def gather_levels(own, wt):
    return lax.all_gather(
        own, "wt", axis=0, tiled=False,
        axis_index_groups=[list(range(side, wt, 2)) for side in range(2)],
    )


def across(value, wt):
    return lax.ppermute(value, "wt", [(at, at ^ 1) for at in range(wt)])


def scatter_levels(value, wt):
    return lax.psum_scatter(
        value, "wt", scatter_dimension=0, tiled=True,
        axis_index_groups=[list(range(side, wt, 2)) for side in range(2)],
    )


def add_rows(left_ref, right_ref, out_ref):
    step = 32

    def some(at, carry):
        rows = pl.ds(pl.multiple_of(at * step, step), step)
        out_ref[rows, :] = (
            left_ref[rows, :].astype(f32) + right_ref[rows, :].astype(f32)
        ).astype(bf16)
        return carry

    lax.fori_loop(0, out_ref.shape[0] // step, some, 0, unroll=2)


def add_low(left, right, name="add_rows"):
    return call(add_rows, shaped(*left.shape), left, right, name=name)


def on_device(
    tokens, positions, doc_ids, block_ids, entry_gain, query_weight, key_weight, value_weight,
    output_weight, attend_gain, middle_gain, gate_weight, up_weight, down_weight, closing_gain,
    cotangent,
):
    place = lax.axis_index("seq")
    order = [place ^ step for step in range(SEQ)]
    here = jnp.reshape(place, (1,)).astype(jnp.int32)
    rows, model = tokens.shape
    window = rows * SEQ
    shard = query_weight.shape[0]
    wt = model // shard
    part = model // SEQ
    width = model // HEADS
    heads = HEADS // SEQ
    hidden = gate_weight.shape[1]
    chunk = hidden // (wt * SEQ)
    padded = (chunk + 15) // 16 * 16
    hidden_part = padded * wt
    piece = 256

    def gather_blocks(own):
        far = swap(own, 2)
        near = swap(own, 1)
        return own, near, far, swap(far, 1)

    lines = wt == 8
    first_own = call(
        pack_first, shaped(shard + GAIN_ROWS, model),
        here, query_weight, key_weight, value_weight, output_weight,
        *(gain[None] for gain in (entry_gain, attend_gain, middle_gain, closing_gain)),
        smem=1, name="pack_first",
    )
    gate_up_own, down_own = call(
        pack_feed, (shaped(shard, 2 * hidden_part), shaped(padded, model)),
        here, gate_weight, up_weight, after(down_weight, first_own), smem=1, name="pack_feed",
    )
    mine = lax.axis_index("wt")
    level = mine // 2
    xside = mine % 2

    def numbers(*values):
        return jnp.stack([jnp.asarray(value, jnp.int32) for value in values])

    if lines:
        around = numbers(level ^ 1, level ^ 2, level ^ 3)
        whose = numbers(
            *[2 * at + xside for at in range(4)],
            *[2 * (level ^ at) + 1 - xside for at in range(4)],
        )
        first_z = gather_levels(first_own, wt)
        gate_up_z = gather_levels(gate_up_own, wt)
        first_x = across(first_own, wt)
        gate_up_x = across(gate_up_own, wt)
        down_x = across(down_own, wt)
        down_pair = jnp.where(
            xside == 0, jnp.stack([down_own, down_x]), jnp.stack([down_x, down_own])
        )
        down_part = gather_levels(down_pair, wt).reshape(hidden_part, model)
    else:
        whose = jnp.arange(wt, dtype=jnp.int32)
        first_z = lax.all_gather(first_own, "wt", axis=0, tiled=False)
        gate_up_z = lax.all_gather(gate_up_own, "wt", axis=0, tiled=False)
        down_part = lax.all_gather(down_own, "wt", axis=0, tiled=True)
    token_blocks = gather_blocks(tokens)
    cotangent_far = swap(after(cotangent, token_blocks[2]), 2)

    offsets = jnp.arange(window, dtype=jnp.int32)
    leading = doc_ids == doc_ids[0]
    boundary = jnp.sum(leading.astype(jnp.int32))
    places = jnp.where(leading, DOC_LEN - boundary + offsets, offsets - boundary)
    codes = doc_ids * DOC_STRIDE + block_ids
    lows = doc_ids * DOC_STRIDE
    packed = jnp.stack([places, codes, lows]).reshape(3, SEQ, rows)
    packed = jnp.concatenate(
        [lax.dynamic_index_in_dim(packed, at, 1, keepdims=False) for at in order], 1
    )
    half = width // 2
    frequency = ROTARY_BASE ** (-2.0 * jnp.arange(half, dtype=f32) / width)
    angles = packed[0].astype(f32)[:, None] * frequency[None, :]
    cosine = jnp.cos(angles)
    sine = jnp.sin(angles)
    cosine = jnp.concatenate([cosine, cosine], 1)
    sine = jnp.concatenate([-sine, sine], 1)
    query_code = jnp.broadcast_to(
        packed[1:3].astype(f32).reshape(2, SEQ, rows).transpose(1, 0, 2)[:, :, None, :], (SEQ, 2, 4, rows)
    ).transpose(0, 2, 1, 3).reshape(SEQ, 8, rows)

    waited = (cosine, sine, query_code, *token_blocks, cotangent_far)
    if lines:
        first_z = after(first_z, *waited, first_x, gate_up_x, down_pair)
        rest = call(
            others, shaped(3, shard + GAIN_ROWS, model), around, first_z, smem=1, name="others",
        )
        firsts = (first_z, first_x[None], across(rest, wt))
    else:
        firsts = (after(first_z, *waited),)
    output_own, gains = call(
        output_and_gains, (shaped(model, part), shaped(8, model, dtype=f32)),
        whose, *firsts, smem=1, name="output_and_gains",
    )
    entry_full, attend_full, middle_full, closing_full = [gains[at:at + 1] for at in range(4)]
    low_shape = shaped(window, heads * width)
    pair_cost = 2 * heads * window * window * width
    entry_low, query_low, key_low, value_low, attended, log_totals, qkv_weight = call(
        attend_forward,
        (shaped(window, model), low_shape, low_shape, low_shape, low_shape,
         shaped(heads, SEQ, 8, rows, dtype=f32), shaped(model, 3 * part)),
        whose, entry_full, cosine, sine, query_code, *token_blocks,
        after(firsts[0], output_own), *firsts[1:], smem=1,
        scratch=(
            pltpu.VMEM((window, model), bf16),
            pltpu.VMEM((window, 128), f32),
        ),
        name="attend_forward",
    )
    attended_own = attended
    if lines:
        gate_up_z = after(gate_up_z, attended)
        rest = call(
            others, shaped(3, shard, 2 * hidden_part), around, gate_up_z, smem=1, name="others",
        )
        attended, rest = lax.optimization_barrier((attended, rest))
        gate_ups = (gate_up_z, gate_up_x[None], across(rest, wt))
    else:
        gate_ups = (gate_up_z,)
    output_far = after(swap(output_own, 2), attended)
    output_rows = call(
        arrange, shaped(model, model),
        here, output_own, swap(output_own, 1), output_far, swap(output_far, 1), smem=1,
        name="arrange",
    )

    gate_up = call(
        assemble, shaped(model, 2 * hidden_part), whose, *gate_ups, smem=1, name="assemble",
    )

    def exchange(blocks):
        return [blocks[0], swap(blocks[1], 1), swap(blocks[2], 2), swap(blocks[3], 3)]

    joined = exchange([attended[at * rows:(at + 1) * rows] for at in range(SEQ)])
    joined = [joined[0], joined[1]] + [after(got, output_rows) for got in joined[2:]]
    inputs = tokens.astype(f32)
    mixed = dot(jnp.concatenate(joined, 1), output_rows)
    attend_normed, attend_inverse = normed_of(mixed)
    hidden_state = inputs + attend_normed * attend_full
    middle_normed, middle_inverse = normed_of(hidden_state)
    middle_low = (middle_normed * middle_full).astype(bf16)

    full = shaped(rows, model, dtype=f32)
    both_shape = shaped(2 * rows, 2 * hidden_part)

    def forward(first_rows, second_rows):
        return call(
            feed_forward, (both_shape, shaped(2 * rows, hidden_part), full, shaped(rows, model)),
            first_rows, second_rows, gate_up, down_part, name="feed_forward",
        )

    def backward(first_rows, second_rows, both):
        return call(
            feed_backward, (both_shape, full, shaped(rows, model)),
            first_rows, second_rows, both, gate_up, down_part, name="feed_backward",
        )

    def chip_sum(values, weights, product):
        second = product(values[rows:], weights).astype(bf16)
        return product(values[:rows], weights) + swap(second, 1).astype(f32)

    middle_far = swap(middle_low, 2)
    middle_near = swap(middle_low, 1)
    fed_near = forward(middle_low, middle_near)
    middle_far = after(middle_far, fed_near[0])
    channel_near = fed_near[2] + swap(fed_near[3], 1).astype(f32)
    channel_send = channel_near.astype(bf16)
    far_other = swap(channel_send, 2)
    middle_both = after(swap(middle_far, 1), channel_send)
    fed_far = forward(middle_far, middle_both)
    far_other = after(far_other, fed_far[0])
    channel_far = fed_far[2] + swap(fed_far[3], 1).astype(f32)
    near_other = swap(channel_far.astype(bf16), 2)

    def close(channel_out, cotangents):
        normed, inverse = normed_of(channel_out)
        back = norm_back(cotangents.astype(f32), normed, inverse, closing_full)
        return normed, back.astype(bf16)

    _, low_far = close(channel_far + far_other.astype(f32), cotangent_far)
    low_both = swap(low_far, 1)
    back_far = backward(low_far, low_both, fed_far[0])
    near_other = after(near_other, back_far[0])
    middle_send = (back_far[1] + swap(back_far[2], 1).astype(f32)).astype(bf16)
    far_got = swap(middle_send, 2)
    closing_normed, channel_low = close(
        channel_near + after(near_other, middle_send).astype(f32), cotangent
    )
    layer_output = (hidden_state + closing_normed * closing_full).astype(bf16)
    incoming = cotangent.astype(f32)
    closing_sum = jnp.sum(incoming * closing_normed, 0)
    low_near = swap(channel_low, 1)
    down_shape = shaped(hidden_part // 2, model)
    side = jnp.reshape(lax.axis_index("wt") % 2, (1,)).astype(jnp.int32)
    down_keep, down_send = call(
        functools.partial(down_weights, padded=padded), (down_shape, down_shape),
        side, channel_low, low_near, low_far, low_both, fed_near[1], fed_far[1], smem=1,
        scratch=(pltpu.VMEM((hidden_part, model), bf16),), name="down_weights",
    )
    down_got = across(down_send, wt)
    back_near = backward(channel_low, after(low_near, down_keep), fed_near[0])
    near_got = swap(back_near[2], 1)
    gate_shape = shaped(model // 2, hidden_part)
    gate_keep, gate_send, up_keep, up_send = call(
        functools.partial(feed_weights, shard=shard),
        (gate_shape,) * 4, side, middle_low, middle_near, middle_far, middle_both,
        after(back_near[0], near_got), back_far[0], smem=1,
        scratch=(pltpu.VMEM((model, 2 * hidden_part), bf16),), name="feed_weights",
    )
    gate_got = across(gate_send, wt)
    up_got = across(up_send, wt)
    far_got = after(far_got, gate_keep)
    down_sum = add_low(down_keep, after(down_got, far_got))
    down_share = scatter_levels(down_sum, wt)
    row_block = pl.BlockSpec((rows // 4, model), lambda step: (step, 0))

    def fixed(*shape):
        return pl.BlockSpec(shape, lambda step: (0, 0))

    hidden_grad, mixed_low, middle_sums, *attended_grads = pl.pallas_call(
        middle_backward,
        grid=(4,),
        out_shape=(full, shaped(rows, model), shaped(16, model, dtype=f32))
        + (shaped(rows, part),) * SEQ,
        in_specs=[row_block] * 6 + [fixed(8, model), fixed(model, model)],
        out_specs=(row_block, row_block, fixed(16, model)) + (fixed(rows, part),) * SEQ,
        scratch_shapes=[pltpu.VMEM((rows, model), bf16)],
        compiler_params=pltpu.CompilerParams(
            vmem_limit_bytes=GRANTS.get("middle_backward", 56) * 1024 * 1024
        ),
        cost_estimate=pl.CostEstimate(
            flops=int(COSTS["middle_backward"] * 1.15e9), transcendentals=0, bytes_accessed=0
        ),
        name="middle_backward",
    )(
        back_near[1], near_got, after(far_got, down_sum), hidden_state, mixed, cotangent, gains,
        output_rows,
    )
    attended_back = exchange(attended_grads)
    output_grads = call(
        output_weights,
        (shaped(model, part, dtype=f32), shaped(model, part), shaped(model, part, dtype=f32),
         shaped(model, part)),
        here, after(mixed_low, *attended_back[1:]), *joined, smem=1,
        name="output_weights",
    )
    output_far = (output_grads[2] + swap(output_grads[3], 1).astype(f32)).astype(bf16)
    output_near = swap(output_grads[1], 1)
    output_far = after(output_far, *attended_back)
    gate_sum = add_low(gate_keep, after(gate_got, *attended_back[1:]))
    gate_share = scatter_levels(gate_sum, wt)
    attended_back[0] = after(attended_back[0], output_far, gate_sum)
    output_got = swap(output_far, 2)
    qkv_grad = call(
        attend_backward, shaped(window, 3 * part),
        query_low, key_low, value_low, attended_own, log_totals, cosine, sine, query_code,
        *attended_back,
        scratch=(
            pltpu.VMEM((heads, window, width), f32), pltpu.VMEM((heads, window, width), f32),
            pltpu.VMEM((window, heads * width), bf16), pltpu.VMEM((window, 128), f32),
        ),
        name="attend_backward",
    )
    levels = range(0, wt, 2)
    whose = numbers(*[at + xside for at in levels], *[at + 1 - xside for at in levels])
    last_shape = shaped(wt // 2 * (shard + GAIN_ROWS), model)
    last_keep, last_send = call(
        last_weights, (last_shape, last_shape),
        whose, entry_low, qkv_grad, output_grads[0], output_near, after(output_got, qkv_grad), middle_sums,
        closing_sum[None],
        smem=1, scratch=(pltpu.VMEM((model, model), bf16), pltpu.VMEM((wt, GAIN_ROWS, model), bf16)),
        name="last_weights",
    )
    up_sum = add_low(up_keep, after(up_got, down_share, last_send), "add_late")
    up_share = scatter_levels(up_sum, wt)
    qkv_grad = after(qkv_grad, last_send, up_sum)

    low_full = shaped(rows, model)
    far_send, far_keep, near_send, near_keep = call(
        entry_backward, (low_full, full, low_full, full), qkv_grad, qkv_weight,
        name="entry_backward",
    )
    entry_far = (far_keep + swap(far_send, 1).astype(f32)).astype(bf16)
    entry_near = near_keep + swap(near_send, 1).astype(f32)
    share = call(
        join_shares, shaped((2 * hidden_part * shard + model * padded) // piece, piece),
        after(gate_share, entry_near), up_share, down_share, name="join_shares",
    )
    entry_got = swap(entry_far, 2)
    last_got = after(across(last_send, wt), gate_share, up_sum, entry_near, share, entry_got)
    last_sum = add_low(last_keep, last_got)
    last_share = scatter_levels(last_sum, wt)
    entry_grad = entry_near + after(entry_got, last_sum).astype(f32)
    entry_normed, entry_inverse = normed_of(inputs)
    input_grad = hidden_grad + norm_back(entry_grad, entry_normed, entry_inverse, entry_full)
    share_far = after(swap(share, 2), input_grad)
    share_got = (share, swap(share, 1), share_far, swap(share_far, 1))
    grad_gate, grad_up, grad_down = call(
        functools.partial(unpack_feed, shard=shard, padded=padded),
        (shaped(shard, hidden, dtype=f32), shaped(shard, hidden, dtype=f32),
         shaped(SEQ * chunk, model, dtype=f32)),
        here, *share_got, smem=1, name="unpack_feed",
    )
    last_got = gather_blocks(after(last_share, grad_down))
    weight_shape = shaped(shard, model, dtype=f32)
    grad_query, grad_key, grad_value, grad_output, *grad_gains = call(
        functools.partial(unpack_last, shard=shard),
        (weight_shape,) * 4
        + (shaped(1, shard, dtype=f32),) * 4,
        here, last_share, last_got[1], last_got[2],
        last_got[3], entry_gain[None], query_weight, key_weight, value_weight, smem=1,
        name="unpack_last",
    )
    grad_entry, grad_attend, grad_middle, grad_closing = [gain[0] for gain in grad_gains]
    return (
        layer_output, input_grad, grad_entry, grad_query, grad_key, grad_value, grad_output,
        grad_attend, grad_middle, grad_gate, grad_up, grad_down, grad_closing,
    )


def solution(mesh):
    rows = P(("wt", "seq"), None)
    weight = P("wt", None)
    gain = P("wt")
    return jax.shard_map(
        on_device,
        mesh=mesh,
        in_specs=(
            rows, P(("wt", "seq")), gain, gain, gain, weight, weight, weight, weight, gain, gain,
            weight, weight, weight, gain, rows,
        ),
        out_specs=(
            rows, rows, gain, weight, weight, weight, weight, gain, gain, weight, weight, weight,
            gain,
        ),
        check_vma=False,
    )
```
